32 devices in a mesh: groups: 1, ctx: 2 (over x), fsdp: 16 (over z, y, core).
Axes of the slice: x: 2, y: 2, z: 4, core: 2. Of those that a mesh axis runs over, the one named last changes fastest.
Arguments:
- tokens: bfloat16 [16, 256, 3072], P(('groups', 'fsdp'), 'ctx'), may hold values from -600 to 600
- trace_index: int32 [16, 256], P(('groups', 'fsdp'), 'ctx'), may hold values from 0 to 1, never falling along the last dimension, each value on 1 to 192 neighbouring positions
- input_norm_scale: bfloat16 [3072], replicated, may hold values from 0.099609375 to 1.8984375
- query_weight: bfloat16 [3072, 2048], P('fsdp'), may hold values from -0.109375 to 0.109375
- key_weight: bfloat16 [3072, 1024], P('fsdp'), may hold values from -0.109375 to 0.109375
- value_weight: bfloat16 [3072, 1024], P('fsdp'), may hold values from -0.109375 to 0.109375
- query_down_weight: bfloat16 [3072, 16], replicated, may hold values from -0.109375 to 0.109375
- query_up_weight: bfloat16 [16, 2048], replicated, may hold values from -1.5 to 1.5
- value_down_weight: bfloat16 [3072, 16], replicated, may hold values from -0.109375 to 0.109375
- value_up_weight: bfloat16 [16, 1024], replicated, may hold values from -1.5 to 1.5
- output_gradient: bfloat16 [16, 256, 2048], P(('groups', 'fsdp'), 'ctx'), may hold values from -24 to 24
Outputs:
- grad_a_query: float32 [3072, 16], P('groups')
- grad_b_query: float32 [16, 2048], P('groups')
- grad_a_value: float32 [3072, 16], P('groups')
- grad_b_value: float32 [16, 1024], P('groups')
The draws below stay inside these ranges and needn't reach their ends.
Inputs may be any that keep to these rules, and one draw needn't show every extreme that they name: `trace_index`: ids never fall along a sequence; one trace holds at most 192 positions.
All inputs are finite; a program needn't handle non-finite values.
Results may differ from the reference program's by a relative error of at most 0.013.
Values may be sent and summed in bfloat16 or wider, within the bound.
A program may use at most 128 MiB of HBM per device.

```python
import math
import jax
import jax.numpy as jnp
import numpy as np
from jax import lax

MODEL_FEATURES = 3072
QUERY_HEADS = 16
KEY_VALUE_HEADS = 8
HEAD_SIZE = 128
ADAPTER_RANK = 16
TOK_DEV = 128
WINDOW = 256
SEQ = 256
TRACES = 2
TRACE = 192
NSEQ = 16
TOKEN_COUNT = 4096


def draw_tokens(key, part):
    first, second, third = jax.random.split(key, 3)
    base = jnp.clip(jax.random.normal(first, (NSEQ, SEQ, MODEL_FEATURES), jnp.float32), -6.0, 6.0)
    row_scale = jnp.exp(jax.random.uniform(second, (NSEQ, SEQ, 1), jnp.float32, 0.0, math.log(10.0)))
    col_scale = jnp.exp(jax.random.uniform(third, (MODEL_FEATURES,), jnp.float32, 0.0, math.log(10.0)))
    return (base * row_scale * col_scale).astype(jnp.bfloat16)


def shard_levels(stream_key, shape, shards, least, high):
    level, own = 1.0, jax.random.fold_in(stream_key, 6)
    for position, parts in shards:
        steps = jnp.exp(jax.random.uniform(jax.random.fold_in(own, position), (parts,), jnp.float32, least / len(shards), high / len(shards)))
        level = level * jnp.repeat(steps, shape[position] // parts).reshape([-1 if axis == position else 1 for axis in range(len(shape))])
    return level


def length_profile(amount, total, limit, lean):
    weights = [(1 << 20) // math.isqrt(rank ** lean) + 1 for rank in range(2, amount + 1)]
    rest, counts = total - limit - (amount - 1), [1] * (amount - 1)
    while rest > 0:
        free = [i for i in range(amount - 1) if counts[i] < limit]
        whole, remaining = sum([weights[i] for i in free]), rest
        for i in free:
            extra = min(limit - counts[i], max(1, remaining * weights[i] // whole), rest)
            counts[i] = counts[i] + extra
            rest = rest - extra
    return np.array([limit] + counts)


def ragged_sizes(own_key, count, total, most, slope):
    if count == 2:
        one = jax.random.randint(own_key, (), max(1, total - most), min(most, total - 1) + 1)
        return jnp.stack([one, total - one])
    lengths = jnp.asarray(length_profile(count, total, most, slope), jnp.int32)
    pairs = (count - 1) // 2
    donor, sink = lengths[1:1 + 2 * pairs:2], lengths[2:2 + 2 * pairs:2]
    margin = jnp.minimum(donor - 1, most - sink)
    moved = jax.random.randint(jax.random.fold_in(own_key, 1), (pairs,), 0, 1 << 20) % (margin + 1)
    lengths = lengths.at[1:1 + 2 * pairs:2].set(donor - moved).at[2:2 + 2 * pairs:2].set(sink + moved)
    return lengths[jax.random.permutation(jax.random.fold_in(own_key, 2), count)]


def bell_draw(key, extent, deviation, reach, shards=(), kind=jnp.bfloat16):
    drawn = jax.random.normal(key, extent, jnp.float32) * deviation
    if len(shards) > 0:
        drawn = shard_levels(key, extent, shards, -0.22, 0.18) * drawn
    return jnp.clip(drawn, min=-reach, max=reach).astype(kind)


def setup_inputs(seed: int = 0, part: int = 0) -> dict:
    key_of = jax.random.split(jax.random.key(seed), 12)
    own_keys = jax.random.split(jax.random.fold_in(key_of[11], part), 12)
    return {
        "tokens": draw_tokens(jax.random.fold_in(jax.random.fold_in(key_of[11], part), 71), part),
        "trace_index": jax.vmap(lambda own: jnp.searchsorted(jnp.cumsum(ragged_sizes(own, TRACES, SEQ, TRACE, 0)), jnp.arange(SEQ), side="right"))(jax.random.split(own_keys[1], NSEQ)).reshape((NSEQ, SEQ)).astype(jnp.int32),
        "input_norm_scale": jnp.clip(1.0 + 0.18 * jax.random.normal(key_of[2], (MODEL_FEATURES,), jnp.float32), 0.099609375, 1.8984375).astype(jnp.bfloat16),
        "query_weight": bell_draw(key_of[3], (MODEL_FEATURES, QUERY_HEADS * HEAD_SIZE), MODEL_FEATURES ** -0.5, 0.109375, ((0, 16),)),
        "key_weight": bell_draw(key_of[4], (MODEL_FEATURES, KEY_VALUE_HEADS * HEAD_SIZE), MODEL_FEATURES ** -0.5, 0.109375, ((0, 16),)),
        "value_weight": bell_draw(key_of[5], (MODEL_FEATURES, KEY_VALUE_HEADS * HEAD_SIZE), MODEL_FEATURES ** -0.5, 0.109375, ((0, 16),)),
        "query_down_weight": bell_draw(key_of[6], (MODEL_FEATURES, ADAPTER_RANK), MODEL_FEATURES ** -0.5, 0.109375),
        "query_up_weight": bell_draw(key_of[7], (ADAPTER_RANK, QUERY_HEADS * HEAD_SIZE), ADAPTER_RANK ** -0.5, 1.5),
        "value_down_weight": bell_draw(key_of[8], (MODEL_FEATURES, ADAPTER_RANK), MODEL_FEATURES ** -0.5, 0.109375),
        "value_up_weight": bell_draw(key_of[9], (ADAPTER_RANK, KEY_VALUE_HEADS * HEAD_SIZE), ADAPTER_RANK ** -0.5, 1.5),
        "output_gradient": bell_draw(own_keys[10], (NSEQ, SEQ, QUERY_HEADS * HEAD_SIZE), 4.0, 24.0, ((0, 16), (1, 2))),
    }


CAP = 50.0
QSCALE = 1.0 / 12.0
ADAPTER_NAME = 0.5
EPS = 1e-06

def normed_rows(values, gain):
    flt = values.astype(jnp.float32)
    meansq = lax.optimization_barrier(jnp.mean(flt * flt, axis=-1, keepdims=True))
    return (flt * lax.rsqrt(meansq + EPS) * gain.astype(jnp.float32)).astype(jnp.bfloat16)

def earlier_blocks(stack, distance):
    filler = jnp.zeros((distance,) + stack.shape[1:], stack.dtype)
    return jnp.concatenate([filler, stack[:stack.shape[0] - distance]], 0)

def later_blocks(stack, distance):
    filler = jnp.zeros((distance,) + stack.shape[1:], stack.dtype)
    return jnp.concatenate([stack[distance:], filler], 0)

def attend_block(operands):
    q_blk, k_blk, v_blk, g_blk, mask = operands
    qf = q_blk.astype(jnp.float32)
    kf = k_blk.astype(jnp.float32)
    vf = v_blk.astype(jnp.float32)
    gf = g_blk.astype(jnp.float32)
    s = jnp.einsum('ikgd,jkd->kgij', qf, kf) * QSCALE
    t = jnp.tanh(s / CAP)
    capped = CAP * t
    expo = jnp.where(mask[None, None], jnp.exp(capped), jnp.float32(0.0))
    weights = expo / lax.optimization_barrier(jnp.sum(expo, axis=-1, keepdims=True))
    weights16 = weights.astype(jnp.bfloat16).astype(jnp.float32)
    attended = jnp.einsum('kgij,jkd->ikgd', weights16, vf)
    dweight = jnp.einsum('ikgd,jkd->kgij', gf, vf)
    delta = jnp.einsum('ikgd,ikgd->kgi', gf, attended)
    dscore = (weights * (dweight - delta[..., None]) * (1.0 - t * t) * QSCALE).astype(jnp.bfloat16)
    query_gradient = jnp.einsum('kgij,jkd->ikgd', dscore.astype(jnp.float32), kf).astype(jnp.bfloat16)
    value_gradient = jnp.einsum('kgij,ikgd->jkd', weights16, gf)
    return (query_gradient, value_gradient)

def reference(tokens, trace_index, input_norm_scale, query_weight, key_weight, value_weight, query_down_weight, query_up_weight, value_down_weight, value_up_weight, output_gradient):
    row_slice = NSEQ * SEQ
    head_group = QUERY_HEADS // KEY_VALUE_HEADS
    window_width = TOK_DEV
    block_list = row_slice // window_width
    per_seq = SEQ // window_width
    normalized_input = normed_rows(tokens.reshape(row_slice, MODEL_FEATURES), input_norm_scale)
    query_reduced = jnp.dot(normalized_input, query_down_weight, preferred_element_type=jnp.float32).astype(jnp.bfloat16)
    value_reduced = jnp.dot(normalized_input, value_down_weight, preferred_element_type=jnp.float32).astype(jnp.bfloat16)
    query_matrix = (jnp.dot(normalized_input, query_weight, preferred_element_type=jnp.float32) + ADAPTER_NAME * jnp.dot(query_reduced, query_up_weight, preferred_element_type=jnp.float32)).astype(jnp.bfloat16)
    key = jnp.dot(normalized_input, key_weight, preferred_element_type=jnp.float32).astype(jnp.bfloat16)
    value_matrix = (jnp.dot(normalized_input, value_weight, preferred_element_type=jnp.float32) + ADAPTER_NAME * jnp.dot(value_reduced, value_up_weight, preferred_element_type=jnp.float32)).astype(jnp.bfloat16)
    query_blocks = query_matrix.reshape(block_list, window_width, KEY_VALUE_HEADS, head_group, HEAD_SIZE)
    gradient_blocks = output_gradient.reshape(block_list, window_width, KEY_VALUE_HEADS, head_group, HEAD_SIZE)
    key_blocks = key.reshape(block_list, window_width, KEY_VALUE_HEADS, HEAD_SIZE)
    value_blocks = value_matrix.reshape(block_list, window_width, KEY_VALUE_HEADS, HEAD_SIZE)
    k_triples = jnp.concatenate([earlier_blocks(key_blocks, 2), earlier_blocks(key_blocks, 1), key_blocks], 1)
    v_triples = jnp.concatenate([earlier_blocks(value_blocks, 2), earlier_blocks(value_blocks, 1), value_blocks], 1)
    seg_blocks = trace_index.reshape(block_list, window_width)
    seg_keys = jnp.concatenate([earlier_blocks(seg_blocks, 2), earlier_blocks(seg_blocks, 1), seg_blocks], 1)
    pos_q = jnp.arange(window_width, dtype=jnp.int32)[:, None]
    pos_k = jnp.arange(3 * window_width, dtype=jnp.int32)[None, :]
    band = (pos_k > pos_q) & (pos_k <= pos_q + WINDOW)
    offset = jnp.arange(block_list, dtype=jnp.int32) % per_seq
    valid = (pos_k >= 2 * window_width)[None] | (pos_k >= window_width)[None] & (offset >= 1)[:, None, None] | (offset >= 2)[:, None, None]
    mask = band[None] & (seg_keys[:, None, :] == seg_blocks[:, :, None]) & valid
    query_gradient, dvalue_triples = lax.map(attend_block, (query_blocks, k_triples, v_triples, gradient_blocks, mask))
    query_gradient = query_gradient.reshape(row_slice, QUERY_HEADS * HEAD_SIZE)
    self_portion = dvalue_triples[:, 2 * window_width:]
    nearby_portion = later_blocks(dvalue_triples[:, window_width:2 * window_width], 1)
    distant_portion = later_blocks(dvalue_triples[:, :window_width], 2)
    value_gradient = (self_portion + nearby_portion + distant_portion).reshape(row_slice, KEY_VALUE_HEADS * HEAD_SIZE)
    query_backward = jnp.dot(query_gradient, query_up_weight.T, preferred_element_type=jnp.float32).astype(jnp.bfloat16)
    value_backward = jnp.dot(value_gradient, value_up_weight.astype(jnp.float32).T, precision=lax.Precision.HIGHEST)
    coefficient = ADAPTER_NAME / math.sqrt(TOKEN_COUNT)
    grad_a_query = jnp.dot(normalized_input.T, query_backward, preferred_element_type=jnp.float32) * coefficient
    grad_b_query = jnp.dot(query_reduced.T, query_gradient, preferred_element_type=jnp.float32) * coefficient
    grad_a_value = jnp.dot(normalized_input.astype(jnp.float32).T, value_backward, precision=lax.Precision.HIGHEST) * coefficient
    grad_b_value = jnp.dot(value_reduced.astype(jnp.float32).T, value_gradient, precision=lax.Precision.HIGHEST) * coefficient
    return (grad_a_query, grad_b_query, grad_a_value, grad_b_value)
```

```python
import functools
import math

import jax
import jax.numpy as jnp
from jax import lax
from jax.experimental import pallas as pl
from jax.experimental.pallas import tpu as pltpu
from jax.sharding import PartitionSpec as P

HEAD_SIZE = 128


CAP = 50.0
QSCALE = 1.0 / 12.0
ADAPTER_NAME = 0.5
EPS = 1e-06


def shifted(value, axis, by):
    devices = lax.axis_size(axis)
    pairs = [(i, i + by) for i in range(devices) if 0 <= i + by < devices]
    return lax.ppermute(value, axis, pairs)


def normed_rows(values, gain):
    flt = values.astype(jnp.float32)
    meansq = jnp.mean(flt * flt, axis=-1, keepdims=True)
    return (flt * lax.rsqrt(meansq + EPS) * gain.astype(jnp.float32)).astype(jnp.bfloat16)


def add_rows(left, piece):
    return jnp.dot(left, piece, preferred_element_type=jnp.float32)


def attend_head(operands, mask):
    q_head, k_head, v_head, g_head = operands
    s = jnp.einsum("igd,jd->gij", q_head, k_head, preferred_element_type=jnp.float32) * QSCALE
    t = jnp.tanh(s / CAP)
    capped = CAP * t
    expo = jnp.where(mask[None], jnp.exp(capped), jnp.float32(0.0))
    weights = expo / jnp.sum(expo, axis=-1, keepdims=True)
    weights16 = weights.astype(jnp.bfloat16)
    attended = jnp.einsum("gij,jd->igd", weights16, v_head, preferred_element_type=jnp.float32)
    dweight = jnp.einsum("igd,jd->gij", g_head, v_head, preferred_element_type=jnp.float32)
    delta = jnp.sum(g_head.astype(jnp.float32) * attended, axis=-1).T
    dscore = (weights * (dweight - delta[..., None]) * (1.0 - t * t) * QSCALE).astype(jnp.bfloat16)
    query_gradient = jnp.einsum(
        "gij,jd->igd", dscore, k_head, preferred_element_type=jnp.float32
    ).astype(jnp.bfloat16)
    value_gradient = jnp.einsum(
        "gij,igd->jd", weights16, g_head, preferred_element_type=jnp.float32
    )
    return (query_gradient, value_gradient)


def partial_attend(mask):

    def run_head(operands):
        return attend_head(operands, mask)

    return run_head


def on_device(
    tokens,
    trace_index,
    input_norm_scale,
    query_weight,
    key_weight,
    value_weight,
    query_down_weight,
    query_up_weight,
    value_down_weight,
    value_up_weight,
    output_gradient,
):
    window_width = tokens.shape[1]
    feats = tokens.shape[2]
    heads_kv = key_weight.shape[1] // HEAD_SIZE
    heads_q = query_weight.shape[1] // HEAD_SIZE
    head_group = heads_q // heads_kv
    normalized_input = normed_rows(tokens.reshape(window_width, feats), input_norm_scale)
    seg_own = trace_index.reshape(window_width).astype(jnp.bfloat16)
    seg_parts = []

    def add_keyval(piece):
        return add_rows(normalized_input, piece)

    query_frozen = add_rows(
        normalized_input, lax.all_gather(query_weight, "fsdp", axis=0, tiled=True)
    )
    k_base = add_keyval(lax.all_gather(key_weight, "fsdp", axis=0, tiled=True))
    value_frozen = add_keyval(lax.all_gather(value_weight, "fsdp", axis=0, tiled=True))
    query_reduced = jnp.dot(
        normalized_input, query_down_weight, preferred_element_type=jnp.float32
    ).astype(jnp.bfloat16)
    reduced_rows = jnp.dot(
        normalized_input, value_down_weight, preferred_element_type=jnp.float32
    ).astype(jnp.bfloat16)
    query_matrix = (
        query_frozen
        + ADAPTER_NAME * jnp.dot(query_reduced, query_up_weight, preferred_element_type=jnp.float32)
    ).astype(jnp.bfloat16)
    key_rows = k_base.astype(jnp.bfloat16)
    value_rows = (
        value_frozen
        + ADAPTER_NAME * jnp.dot(reduced_rows, value_up_weight, preferred_element_type=jnp.float32)
    ).astype(jnp.bfloat16)
    key_parts = []
    value_parts = []
    for distance in (2, 1):
        key_prev, value_prev, seg_prev = shifted((key_rows, value_rows, seg_own), "ctx", distance)
        key_parts.append(key_prev)
        value_parts.append(value_prev)
        seg_parts.append(seg_prev)
    keys_all = jnp.concatenate(key_parts + [key_rows], 0)
    values_all = jnp.concatenate(value_parts + [value_rows], 0)
    seg_keys = jnp.concatenate(seg_parts + [seg_own], 0)
    pos_q = jnp.arange(window_width, dtype=jnp.int32)[:, None]
    pos_k = jnp.arange(3 * window_width, dtype=jnp.int32)[None, :]
    position = lax.axis_index("ctx")
    mask = (
        (pos_k > pos_q)
        & (pos_k <= pos_q + 2 * window_width)
        & (seg_keys[None, :] == seg_own[:, None])
    )
    mask = mask & (
        (pos_k >= 2 * window_width) | (pos_k >= window_width) & (position >= 1) | (position >= 2)
    )
    q_heads = jnp.moveaxis(
        query_matrix.reshape(window_width, heads_kv, head_group, HEAD_SIZE), 1, 0
    )
    g_heads = jnp.moveaxis(
        output_gradient.reshape(window_width, heads_kv, head_group, HEAD_SIZE), 1, 0
    )
    k_heads = jnp.moveaxis(keys_all.reshape(3 * window_width, heads_kv, HEAD_SIZE), 1, 0)
    v_heads = jnp.moveaxis(values_all.reshape(3 * window_width, heads_kv, HEAD_SIZE), 1, 0)
    dquery_heads, dvalue_heads = lax.map(partial_attend(mask), (q_heads, k_heads, v_heads, g_heads))
    query_gradient = jnp.moveaxis(dquery_heads, 0, 1).reshape(window_width, heads_q * HEAD_SIZE)
    dvalue_triple = jnp.moveaxis(dvalue_heads, 0, 1).reshape(3 * window_width, heads_kv * HEAD_SIZE)
    value_gradient = dvalue_triple[2 * window_width :]
    for distance in (1, 2):
        begin = (2 - distance) * window_width
        value_gradient = value_gradient + shifted(
            dvalue_triple[begin : begin + window_width], "ctx", -distance
        )
    query_backward = jnp.dot(
        query_gradient, query_up_weight.T, preferred_element_type=jnp.float32
    ).astype(jnp.bfloat16)
    value_backward = jnp.dot(
        value_gradient, value_up_weight.astype(jnp.float32).T, precision=lax.Precision.HIGHEST
    )
    part_aq = jnp.dot(normalized_input.T, query_backward, preferred_element_type=jnp.float32)
    part_bq = jnp.dot(query_reduced.T, query_gradient, preferred_element_type=jnp.float32)
    part_av = jnp.dot(
        normalized_input.astype(jnp.float32).T, value_backward, precision=lax.Precision.HIGHEST
    )
    part_bv = jnp.dot(
        reduced_rows.astype(jnp.float32).T, value_gradient, precision=lax.Precision.HIGHEST
    )
    sum_aq, sum_bq, sum_av, sum_bv = lax.psum((part_aq, part_bq, part_av, part_bv), ("ctx", "fsdp"))
    token_total = lax.axis_size("ctx") * lax.axis_size("fsdp") * window_width
    coefficient = ADAPTER_NAME / math.sqrt(token_total)
    return (sum_aq * coefficient, sum_bq * coefficient, sum_av * coefficient, sum_bv * coefficient)


F32 = jnp.float32
BF16 = jnp.bfloat16
PLANE = 8


def dot(a, b, dims=((1,), (0,))):
    return lax.dot_general(a, b, (dims, ((), ())), preferred_element_type=F32)


def plane_kernel(
    chain, coefficient,
    raw, seg, gain, wq, wk, wv, qd, qu, vd, vu, grad,
    OUTQ, OUTV,
    N, M, WA, WV, G, SG, acc, accv, P, C, K, DQ, DV, LQ, LV,
    AQ, RAQ, RSQ, TQ, AV, RAV, RSV, TV,
    local_sem, w_send, w_recv, t_send, t_recv, g_send, g_recv, s_send, s_recv,
    up_send, up_recv, down_send, down_recv, vup_send, vup_recv, vdown_send, vdown_recv,
    q1_send, q1_recv, q2_send, q2_recv, q3_send, q3_recv,
    v1_send, v1_recv, v2_send, v2_recv, v3_send, v3_recv,
):
    x = lax.axis_index("ctx")
    f = lax.axis_index("fsdp")
    z = f // 4
    y = (f // 2) % 2
    c = f % 2
    tok, feats = raw.shape
    rows = wq.shape[0]
    qcols = wq.shape[1] // PLANE
    kcols = wk.shape[1] // PLANE
    acols = qcols + kcols
    piece = feats // PLANE
    seq = 2 * tok
    sub = tok // 4
    heads = qcols // kcols
    middle = (z > 0) & (z < chain - 1)
    outer = (z == 0) | (z == chain - 1)

    def coords(r):
        px = 1 - x if r & 4 else x
        py = 1 - y if r & 2 else y
        pc = 1 - c if r & 1 else c
        return px, py, pc

    def head_of(r):
        px, py, pc = coords(r)
        return (px * 2 + py) * 2 + pc

    def peer(r):
        px, py, pc = coords(r)
        return {"ctx": px, "fsdp": (z * 2 + py) * 2 + pc}

    def above(pz):
        return {"ctx": x, "fsdp": (pz * 2 + y) * 2 + c}

    def tok_slot(r):
        px, py, pc = coords(r)
        return (py * 2 + pc) * 2 + px

    def tok_piece(r, low, count):
        begin = tok_slot(r) * tok + low * sub
        return pl.ds(pl.multiple_of(begin, sub), count * sub)

    def tok_rows(r):
        return pl.ds(pl.multiple_of(tok_slot(r) * tok, tok), tok)

    def remote(src, dst, send, recv, device):
        return pltpu.make_async_remote_copy(
            src_ref=src, dst_ref=dst, send_sem=send, recv_sem=recv,
            device_id=device, device_id_type=pl.DeviceIdType.MESH,
        )

    barrier = pltpu.get_barrier_semaphore()
    for r in range(1, PLANE):
        pl.semaphore_signal(barrier, inc=1, device_id=peer(r), device_id_type=pl.DeviceIdType.MESH)
    for d in range(1, chain):
        pl.semaphore_signal(
            barrier, inc=1, device_id=above((z + d) % chain), device_id_type=pl.DeviceIdType.MESH
        )

    def w_rows(r):
        px, py, pc = coords(r)
        return pl.ds(pl.multiple_of(((z * 2 + py) * 2 + pc) * rows, rows), rows)

    def w_parts(r):
        h = head_of(r)
        own = w_rows(0)
        return (
            (wq.at[:, pl.ds(pl.multiple_of(h * qcols, qcols), qcols)], WA.at[own, pl.ds(0, qcols)]),
            (wk.at[:, pl.ds(pl.multiple_of(h * kcols, kcols), kcols)], WA.at[own, pl.ds(qcols, kcols)]),
            (wv.at[:, pl.ds(pl.multiple_of(h * kcols, kcols), kcols)], WV.at[own]),
        )

    def g_cols(r):
        h = head_of(r)
        return grad.at[:, pl.ds(pl.multiple_of(h * qcols, qcols), qcols)]

    local = [pltpu.make_async_copy(a, b, local_sem.at[i]) for i, (a, b) in enumerate(w_parts(0))]
    local.append(pltpu.make_async_copy(raw, N.at[tok_rows(0)], local_sem.at[3]))
    local.append(pltpu.make_async_copy(g_cols(0), G.at[tok_rows(0)], local_sem.at[4]))
    local.append(pltpu.make_async_copy(seg, SG.at[tok_slot(0)], local_sem.at[5]))
    for copy in local:
        copy.start()
    for i in range(2):
        local[i].wait()
    pl.semaphore_wait(barrier, PLANE - 1 + chain - 1)

    def half_rows(plane, half):
        py = y if half == 0 else 1 - y
        return pl.ds(pl.multiple_of((plane * 4 + py * 2) * rows, 2 * rows), 2 * rows)

    def quarter_rows(plane, quarter):
        px, py, pc = coords(quarter)
        return pl.ds(pl.multiple_of((plane * 4 + py * 2 + pc) * rows, rows), rows)

    def has_up(t):
        return (z < chain - 1) & (z - t >= 0)

    def has_down(t):
        return (z > 0) & (z + t <= chain - 1)

    def from_below(t):
        return z - 1 - t >= 0

    def from_above(t):
        return z + 1 + t <= chain - 1

    def pieces_of(t):
        return range(4) if t == 0 else range(2)

    def piece_rows(plane, t, i):
        return quarter_rows(plane, i) if t == 0 else half_rows(plane, i)

    def up_copy(t, i):
        at = WA.at[piece_rows(z - t, t, i)]
        return remote(at, at, up_send.at[t, i], up_recv.at[t, i], above(z + 1))

    def down_copy(t, i):
        at = WA.at[piece_rows(z + t, t, i)]
        return remote(at, at, down_send.at[t, i], down_recv.at[t, i], above(z - 1))

    def up_arrival(t, i):
        at = WA.at[piece_rows(z - 1 - t, t, i)]
        return remote(at, at, up_send.at[t, i], up_recv.at[t, i], above(z - 1))

    def down_arrival(t, i):
        at = WA.at[piece_rows(z + 1 + t, t, i)]
        return remote(at, at, down_send.at[t, i], down_recv.at[t, i], above(z + 1))

    def vup_copy(t, half):
        at = WV.at[half_rows(z - t, half)]
        return remote(at, at, vup_send.at[t, half], vup_recv.at[t, half], above(z + 1))

    def vdown_copy(t, half):
        at = WV.at[half_rows(z + t, half)]
        return remote(at, at, vdown_send.at[t, half], vdown_recv.at[t, half], above(z - 1))

    def vup_arrival(t, half):
        at = WV.at[half_rows(z - 1 - t, half)]
        return remote(at, at, vup_send.at[t, half], vup_recv.at[t, half], above(z - 1))

    def vdown_arrival(t, half):
        at = WV.at[half_rows(z + 1 + t, half)]
        return remote(at, at, vdown_send.at[t, half], vdown_recv.at[t, half], above(z + 1))

    def send_chain(t, i):
        @pl.when(has_up(t))
        def _():
            up_copy(t, i).start()

        @pl.when(has_down(t))
        def _():
            down_copy(t, i).start()

    def recv_chain(t, i):
        @pl.when(from_below(t))
        def _():
            up_arrival(t, i).wait_recv()

        @pl.when(from_above(t))
        def _():
            down_arrival(t, i).wait_recv()

    def recv_half(t, half):
        for i in (2 * half, 2 * half + 1) if t == 0 else (half,):
            recv_chain(t, i)

    def send_value_first(k):
        @pl.when(has_up(k - 1) & jnp.logical_not(has_up(k)))
        def _():
            for half in range(2):
                vup_copy(0, half).start()

        @pl.when(has_down(k - 1) & jnp.logical_not(has_down(k)))
        def _():
            for half in range(2):
                vdown_copy(0, half).start()

    def send_value(t, half):
        @pl.when(has_up(t))
        def _():
            vup_copy(t, half).start()

        @pl.when(has_down(t))
        def _():
            vdown_copy(t, half).start()

    def recv_value(t, half):
        @pl.when(from_below(t))
        def _():
            vup_arrival(t, half).wait_recv()

        @pl.when(from_above(t))
        def _():
            vdown_arrival(t, half).wait_recv()

    w_copies = {}
    for r in (1, 2, 3):
        w_copies[r] = [
            remote(a, b, w_send.at[r, i], w_recv.at[r, i], peer(r)) for i, (a, b) in enumerate(w_parts(r))
        ]
    for r in (1, 2, 3):
        for i in range(2):
            w_copies[r][i].start()
    send_chain(0, 0)
    w_copies[1][2].start()

    t_copies = []

    def send_token(r_mine, r_there, hop, low=0, count=4):
        at = N.at[tok_piece(r_mine, low, count)]
        source = raw.at[pl.ds(low * sub, count * sub)] if r_mine == 0 else at
        copy = remote(source, at, t_send.at[r_there, low], t_recv.at[r_there, low], peer(hop))
        copy.start()
        t_copies.append(copy)

    def wait_token(r, low=0, count=4):
        at = N.at[tok_piece(r, low, count)]
        remote(at, at, t_send.at[r, low], t_recv.at[r, low], peer(1)).wait_recv()

    send_token(0, 1, 1)
    send_token(0, 4, 4, 3, 1)
    send_token(0, 4, 4, 0, 3)
    for low in range(4):
        send_token(0, 2, 2, low, 1)
    g_copies = {}
    s_copies = {}
    for r in range(1, PLANE):
        g_copies[r] = remote(g_cols(r), G.at[tok_rows(0)], g_send.at[r], g_recv.at[r], peer(r))
        s_copies[r] = remote(seg, SG.at[tok_slot(0)], s_send.at[r], s_recv.at[r], peer(r))
    for r in (2, 3):
        w_copies[r][2].start()

    def wait_weight(r, value=False):
        at = w_rows(r)
        if value:
            ref = WV.at[at]
            remote(ref, ref, w_send.at[r, 2], w_recv.at[r, 2], peer(r)).wait_recv()
            return
        for i, (lo, width) in enumerate(((0, qcols), (qcols, kcols))):
            ref = WA.at[at, pl.ds(lo, width)]
            remote(ref, ref, w_send.at[r, i], w_recv.at[r, i], peer(r)).wait_recv()

    part_rows = 4 * tok

    def part_at(part, i, height):
        py = y if part == 0 else 1 - y
        return pl.ds(pl.multiple_of(py * part_rows + i * height, height), height)

    h = head_of(0)
    qu_own = qu[:, pl.ds(pl.multiple_of(h * qcols, qcols), qcols)]
    vu_own = vu[:, pl.ds(pl.multiple_of(h * kcols, kcols), kcols)]

    def prepare(r):
        height = tok // 2

        @pl.loop(0, 2)
        def _(i):
            begin = tok_slot(r) * tok + i * height
            at = pl.ds(pl.multiple_of(begin, height), height)
            flt = N[at, :].astype(F32)
            meansq = jnp.sum(flt * flt, axis=-1, keepdims=True) / feats
            M[at, :] = (flt * lax.rsqrt(meansq + EPS) * gain[...].astype(F32).reshape(1, feats)).astype(BF16)

        at = tok_rows(r)
        block = M[at, :]
        low_query = dot(block, qd[...], ((1,), (1,))).astype(BF16)
        low_value = dot(block, vd[...], ((1,), (1,))).astype(BF16)
        LQ[at, :] = low_query
        LV[at, :] = low_value
        acc[at, 0:qcols] = ADAPTER_NAME * dot(low_query, qu_own)
        acc[at, qcols:] = jnp.zeros((tok, kcols), F32)
        accv[at, :] = ADAPTER_NAME * dot(low_value, vu_own)

    def add_piece(plane, half, part):
        chosen = half_rows(plane, half)

        @pl.loop(0, part_rows // seq)
        def _(i):
            at = part_at(part, i, seq)
            acc[at, :] = acc[at, :] + dot(M[at, chosen], WA[chosen, :])

    def add_step(t, half, part):
        @pl.when(from_below(t))
        def _():
            add_piece(z - 1 - t, half, part)

        @pl.when(from_above(t))
        def _():
            add_piece(z + 1 + t, half, part)

    def add_value_piece(plane, half):
        chosen = half_rows(plane, half)

        @pl.loop(0, 2 * part_rows // seq)
        def _(i):
            at = pl.ds(pl.multiple_of(i * seq, seq), seq)
            accv[at, :] = accv[at, :] + dot(M[at, chosen], WV[chosen, :])

    def add_value(t, half):
        @pl.when(from_below(t))
        def _():
            add_value_piece(z - 1 - t, half)

        @pl.when(from_above(t))
        def _():
            add_value_piece(z + 1 + t, half)

    wait_weight(1)
    send_chain(0, 1)
    for r in range(1, PLANE):
        s_copies[r].start()
    local[3].wait()
    prepare(0)
    wait_token(1)
    prepare(1)
    wait_weight(2)
    send_chain(0, 2)
    wait_weight(3)
    send_chain(0, 3)
    recv_half(0, 0)
    send_chain(1, 0)
    wait_token(2, 0, 1)
    send_token(2, 6, 4, 0, 1)
    recv_half(0, 1)
    send_chain(1, 1)
    local[2].wait()
    wait_weight(1, True)
    wait_weight(2, True)
    wait_weight(3, True)
    send_value_first(1)
    wait_token(2, 1, 1)
    send_token(2, 6, 4, 1, 1)
    wait_token(4, 3, 1)
    send_token(4, 6, 2, 3, 1)
    wait_token(4, 0, 3)
    send_token(4, 5, 1)
    prepare(4)
    wait_token(2, 2, 1)
    send_token(2, 6, 4, 2, 1)
    for r in (6, 7, 4, 5, 2, 3, 1):
        g_copies[r].start()
    wait_token(5)
    prepare(5)
    recv_half(1, 0)
    send_chain(2, 0)
    for half in range(2):
        add_piece(z, half, 0)
    for half in range(2):
        add_step(0, half, 0)
    wait_token(2, 3, 1)
    send_token(2, 3, 1)
    prepare(2)
    wait_token(3)
    prepare(3)
    recv_half(1, 1)
    send_chain(2, 1)
    for k in range(2, chain):
        send_value_first(k)
    for half in range(2):
        add_step(1, half, 0)
    for low in range(4):
        wait_token(6, low, 1)
    send_token(6, 7, 1)
    prepare(6)
    wait_token(7)
    prepare(7)

    @pl.when(middle)
    def _():
        for half in range(2):
            recv_value(0, half)
            send_value(1, half)

    for half in range(2):
        add_piece(z, half, 1)
    for t in range(2):
        for half in range(2):
            add_step(t, half, 1)
    for t in range(2, chain - 1):
        for half in range(2):
            recv_half(t, half)
            if t + 1 < chain - 1:
                send_chain(t + 1, half)
            for part in range(2):
                add_step(t, half, part)

    tiles = PLANE * tok // seq
    local[4].wait()
    local[5].wait()
    for r in range(1, PLANE):
        at = G.at[tok_rows(r)]
        remote(at, at, g_send.at[r], g_recv.at[r], peer(r)).wait_recv()
        at = SG.at[tok_slot(r)]
        remote(at, at, s_send.at[r], s_recv.at[r], peer(r)).wait_recv()

    pos_i = lax.broadcasted_iota(jnp.int32, (seq, seq), 0)
    pos_j = lax.broadcasted_iota(jnp.int32, (seq, seq), 1)
    band = (pos_j <= pos_i) & (pos_j > pos_i - 2 * tok)

    @pl.loop(0, tiles, unroll=2)
    def _(i):
        at = pl.ds(pl.multiple_of(i * seq, seq), seq)
        q_all = acc[at, 0:qcols].astype(BF16)
        k = acc[at, qcols:].astype(BF16)
        K[at, :] = k
        g_all = G[at, :]
        traces = [SG[2 * i].astype(F32), SG[2 * i + 1].astype(F32)]
        along = jnp.concatenate(traces, axis=1)
        turned = [jnp.broadcast_to(own, (tok, tok)).T for own in traces]
        across = jnp.concatenate([jnp.concatenate([own, own], axis=1) for own in turned], axis=0)
        mask = band & (across == along)
        dv = jnp.zeros((seq, kcols), F32)
        for n in range(heads):
            q = q_all[:, n * kcols:(n + 1) * kcols]
            g = g_all[:, n * kcols:(n + 1) * kcols]
            t = jnp.tanh(dot(q, k, ((1,), (1,))) * (QSCALE / CAP))
            expo = jnp.where(mask, jnp.exp(CAP * t), 0.0)
            weights = expo * (1.0 / jnp.sum(expo, axis=-1, keepdims=True))
            weights16 = weights.astype(BF16)
            P[i * heads + n] = weights16
            C[i * heads + n] = weights * (1.0 - t * t)
            dv = dv + dot(weights16, g, ((0,), (0,)))
        DV[at, :] = dv.astype(BF16)

    @pl.when(middle)
    def _():
        for t in range(1, chain - 1):
            for half in range(2):
                recv_value(t, half)
                if t + 1 < chain - 1:
                    send_value(t + 1, half)

    def scatter(pull, part, arrived, send, recv):
        copies = []
        for r in (7, 6, 5, 4, 3, 2, 1, 0):
            columns = pl.ds(pl.multiple_of(head_of(r) * piece, piece), piece)
            part[r] = dot(pull, M[:, columns]).astype(BF16)
            if r > 0:
                copy = remote(part.at[r], arrived.at[r], send.at[r], recv.at[r], peer(r))
                copy.start()
                copies.append(copy)
        return copies

    def plane_sum(part, arrived):
        total = part[0].astype(F32)
        for r in range(1, PLANE):
            total = total + arrived[r].astype(F32)
        return total.astype(BF16)

    def share(sums, send, recv):
        own = sums.at[z]
        copies = []
        for d in range(1, chain):
            copy = remote(own, own, send.at[d], recv.at[d], above((z + d) % chain))
            copy.start()
            copies.append(copy)
        return copies

    def shared(sums, send, recv):
        for d in range(1, chain):
            at = sums.at[(z - d + chain) % chain]
            remote(at, at, send.at[d], recv.at[d], above((z + d) % chain)).wait_recv()
        total = sums[0].astype(F32)
        for d in range(1, chain):
            total = total + sums[d].astype(F32)
        return (total * coefficient).astype(BF16)

    def spread(total, mine, out, send, recv):
        mine[...] = total
        copies = []
        for r in (7, 6, 5, 4, 3, 2, 1):
            copy = remote(mine, out.at[h], send.at[r], recv.at[r], peer(r))
            copy.start()
            copies.append(copy)
        out[h] = total
        return copies

    def gathered(out, send, recv):
        for r in range(1, PLANE):
            at = out.at[head_of(r)]
            remote(at, at, send.at[r], recv.at[r], peer(r)).wait_recv()

    v1_copies = scatter(dot(vu_own, DV[...], ((1,), (1,))).astype(BF16), AV, RAV, v1_send, v1_recv)
    RSV.at[z][:, piece:] = dot(LV[...], DV[...], ((0,), (0,))).astype(BF16)
    for half in range(2):
        add_value_piece(z, half)
    for t in range(chain - 2):
        for half in range(2):
            @pl.when(outer)
            def _():
                recv_value(t, half)

            add_value(t, half)
    for copy in v1_copies:
        copy.wait_recv()
    RSV.at[z][:, 0:piece] = plane_sum(AV, RAV)
    v2_copies = share(RSV, v2_send, v2_recv)
    for half in range(2):
        @pl.when(outer)
        def _():
            recv_value(chain - 2, half)

        add_value(chain - 2, half)

    @pl.loop(0, tiles, unroll=2)
    def _(i):
        at = pl.ds(pl.multiple_of(i * seq, seq), seq)
        v = accv[at, :].astype(BF16)
        k = K[at, :]
        for n in range(heads):
            g = G[at, n * kcols:(n + 1) * kcols]
            dweight = dot(g, v, ((1,), (1,)))
            delta = jnp.sum(P[i * heads + n].astype(F32) * dweight, axis=-1, keepdims=True)
            dscore = (C[i * heads + n] * (dweight - delta)).astype(BF16)
            DQ[at, n * kcols:(n + 1) * kcols] = (dot(dscore, k) * QSCALE).astype(BF16)

    q1_copies = scatter(dot(qu_own, DQ[...], ((1,), (1,))).astype(BF16), AQ, RAQ, q1_send, q1_recv)
    RSQ.at[z][:, piece:] = dot(LQ[...], DQ[...], ((0,), (0,))).astype(BF16)
    v3_copies = spread(shared(RSV, v2_send, v2_recv), TV, OUTV, v3_send, v3_recv)
    for copy in q1_copies:
        copy.wait_recv()
    RSQ.at[z][:, 0:piece] = plane_sum(AQ, RAQ)
    q2_copies = share(RSQ, q2_send, q2_recv)
    q3_copies = spread(shared(RSQ, q2_send, q2_recv), TQ, OUTQ, q3_send, q3_recv)
    gathered(OUTV, v3_send, v3_recv)
    gathered(OUTQ, q3_send, q3_recv)

    for r in (1, 2, 3):
        for copy in w_copies[r]:
            copy.wait_send()
    for copy in t_copies:
        copy.wait_send()
    for r in range(1, PLANE):
        g_copies[r].wait_send()
        s_copies[r].wait_send()
    for t in range(chain - 1):
        @pl.when(has_up(t))
        def _():
            for i in pieces_of(t):
                up_copy(t, i).wait_send()
            for half in range(2):
                vup_copy(t, half).wait_send()

        @pl.when(has_down(t))
        def _():
            for i in pieces_of(t):
                down_copy(t, i).wait_send()
            for half in range(2):
                vdown_copy(t, half).wait_send()
    for copy in v1_copies + v2_copies + v3_copies + q1_copies + q2_copies + q3_copies:
        copy.wait_send()


def unpack_kernel(outq, outv, out_aq, out_bq, out_av, out_bv):
    feats = out_aq.shape[1]
    piece = feats // PLANE
    qcols = out_bq.shape[1] // PLANE
    kcols = out_bv.shape[1] // PLANE
    for h in range(PLANE):
        value = outq[h].astype(F32)
        out_aq[:, h * piece:(h + 1) * piece] = value[:, 0:piece]
        out_bq[:, h * qcols:(h + 1) * qcols] = value[:, piece:]
        value = outv[h].astype(F32)
        out_av[:, h * piece:(h + 1) * piece] = value[:, 0:piece]
        out_bv[:, h * kcols:(h + 1) * kcols] = value[:, piece:]


def on_plane(
    tokens,
    trace_index,
    input_norm_scale,
    query_weight,
    key_weight,
    value_weight,
    query_down_weight,
    query_up_weight,
    value_down_weight,
    value_up_weight,
    output_gradient,
):
    tok = tokens.shape[1]
    feats = tokens.shape[2]
    fsdp = lax.axis_size("fsdp")
    chain = fsdp // 4
    ranks = query_down_weight.shape[1]
    qcols = query_weight.shape[1] // PLANE
    kcols = key_weight.shape[1] // PLANE
    piece = feats // PLANE
    many = PLANE * tok
    token_total = lax.axis_size("ctx") * fsdp * tok
    coefficient = ADAPTER_NAME / math.sqrt(token_total)
    hbm = pl.BlockSpec(memory_space=pltpu.HBM)
    vmem = pl.BlockSpec(memory_space=pltpu.VMEM)
    dma = pltpu.SemaphoreType.DMA
    steps = chain - 1
    tiles = many // (2 * tok)
    heads = qcols // kcols
    outq, outv = pl.pallas_call(
        functools.partial(plane_kernel, chain, coefficient),
        out_shape=(
            jax.ShapeDtypeStruct((PLANE, ranks, piece + qcols), BF16),
            jax.ShapeDtypeStruct((PLANE, ranks, piece + kcols), BF16),
        ),
        in_specs=[hbm, hbm, vmem, hbm, hbm, hbm, vmem, vmem, vmem, vmem, hbm],
        out_specs=(vmem, vmem),
        scratch_shapes=[
            pltpu.VMEM((many, feats), BF16),
            pltpu.VMEM((many, feats), BF16),
            pltpu.VMEM((feats, qcols + kcols), BF16),
            pltpu.VMEM((feats, kcols), BF16),
            pltpu.VMEM((many, qcols), BF16),
            pltpu.VMEM((PLANE, 1, tok), jnp.int32),
            pltpu.VMEM((many, qcols + kcols), F32),
            pltpu.VMEM((many, kcols), F32),
            pltpu.VMEM((tiles * heads, 2 * tok, 2 * tok), BF16),
            pltpu.VMEM((tiles * heads, 2 * tok, 2 * tok), F32),
            pltpu.VMEM((many, kcols), BF16),
            pltpu.VMEM((many, qcols), BF16),
            pltpu.VMEM((many, kcols), BF16),
            pltpu.VMEM((many, ranks), BF16),
            pltpu.VMEM((many, ranks), BF16),
            pltpu.VMEM((PLANE, ranks, piece), BF16),
            pltpu.VMEM((PLANE, ranks, piece), BF16),
            pltpu.VMEM((chain, ranks, piece + qcols), BF16),
            pltpu.VMEM((ranks, piece + qcols), BF16),
            pltpu.VMEM((PLANE, ranks, piece), BF16),
            pltpu.VMEM((PLANE, ranks, piece), BF16),
            pltpu.VMEM((chain, ranks, piece + kcols), BF16),
            pltpu.VMEM((ranks, piece + kcols), BF16),
            dma((6,)),
            dma((4, 3)), dma((4, 3)),
            dma((8, 4)), dma((8, 4)), dma((8,)), dma((8,)), dma((8,)), dma((8,)),
            dma((steps, 4)), dma((steps, 4)), dma((steps, 4)), dma((steps, 4)),
            dma((steps, 2)), dma((steps, 2)), dma((steps, 2)), dma((steps, 2)),
            dma((8,)), dma((8,)), dma((chain,)), dma((chain,)), dma((8,)), dma((8,)),
            dma((8,)), dma((8,)), dma((chain,)), dma((chain,)), dma((8,)), dma((8,)),
        ],
        compiler_params=pltpu.CompilerParams(
            collective_id=0, has_side_effects=True, vmem_limit_bytes=56 * 1024 * 1024
        ),
    )(
        tokens.reshape(tok, feats), trace_index, input_norm_scale,
        query_weight, key_weight, value_weight,
        query_down_weight.T, query_up_weight, value_down_weight.T, value_up_weight,
        output_gradient.reshape(tok, output_gradient.shape[2]),
    )
    aq, bq, av, bv = pl.pallas_call(
        unpack_kernel,
        out_shape=(
            jax.ShapeDtypeStruct((ranks, feats), F32),
            jax.ShapeDtypeStruct((ranks, query_weight.shape[1]), F32),
            jax.ShapeDtypeStruct((ranks, feats), F32),
            jax.ShapeDtypeStruct((ranks, value_weight.shape[1]), F32),
        ),
        in_specs=[vmem, vmem],
        out_specs=(vmem, vmem, vmem, vmem),
        compiler_params=pltpu.CompilerParams(vmem_limit_bytes=16 * 1024 * 1024),
    )(outq, outv)
    return (aq.T, bq, av.T, bv)


def solution(mesh):
    shape = mesh.shape
    planes = shape["groups"] == 1 and shape["ctx"] == 2 and shape["fsdp"] % 4 == 0 and shape["fsdp"] > 8
    return jax.shard_map(
        on_plane if planes else on_device,
        mesh=mesh,
        in_specs=(
            P(("groups", "fsdp"), "ctx", None),
            P(("groups", "fsdp"), "ctx"),
            P(),
            P("fsdp", None),
            P("fsdp", None),
            P("fsdp", None),
            P(),
            P(),
            P(),
            P(),
            P(("groups", "fsdp"), "ctx", None),
        ),
        out_specs=(P("groups", None), P("groups", None), P("groups", None), P("groups", None)),
        check_vma=False,
    )
```

```python
import functools
import math

import jax
import jax.numpy as jnp
from jax import lax
from jax.experimental import pallas as pl
from jax.experimental.pallas import tpu as pltpu
from jax.sharding import PartitionSpec as P

HEAD_SIZE = 128


CAP = 50.0
QSCALE = 1.0 / 12.0
ADAPTER_NAME = 0.5
EPS = 1e-06


def shifted(value, axis, by):
    devices = lax.axis_size(axis)
    pairs = [(i, i + by) for i in range(devices) if 0 <= i + by < devices]
    return lax.ppermute(value, axis, pairs)


def normed_rows(values, gain):
    flt = values.astype(jnp.float32)
    meansq = jnp.mean(flt * flt, axis=-1, keepdims=True)
    return (flt * lax.rsqrt(meansq + EPS) * gain.astype(jnp.float32)).astype(jnp.bfloat16)


def add_rows(left, piece):
    return jnp.dot(left, piece, preferred_element_type=jnp.float32)


def attend_head(operands, mask):
    q_head, k_head, v_head, g_head = operands
    s = jnp.einsum("igd,jd->gij", q_head, k_head, preferred_element_type=jnp.float32) * QSCALE
    t = jnp.tanh(s / CAP)
    capped = CAP * t
    expo = jnp.where(mask[None], jnp.exp(capped), jnp.float32(0.0))
    weights = expo / jnp.sum(expo, axis=-1, keepdims=True)
    weights16 = weights.astype(jnp.bfloat16)
    attended = jnp.einsum("gij,jd->igd", weights16, v_head, preferred_element_type=jnp.float32)
    dweight = jnp.einsum("igd,jd->gij", g_head, v_head, preferred_element_type=jnp.float32)
    delta = jnp.sum(g_head.astype(jnp.float32) * attended, axis=-1).T
    dscore = (weights * (dweight - delta[..., None]) * (1.0 - t * t) * QSCALE).astype(jnp.bfloat16)
    query_gradient = jnp.einsum(
        "gij,jd->igd", dscore, k_head, preferred_element_type=jnp.float32
    ).astype(jnp.bfloat16)
    value_gradient = jnp.einsum(
        "gij,igd->jd", weights16, g_head, preferred_element_type=jnp.float32
    )
    return (query_gradient, value_gradient)


def partial_attend(mask):

    def run_head(operands):
        return attend_head(operands, mask)

    return run_head


def on_device(
    tokens,
    trace_index,
    input_norm_scale,
    query_weight,
    key_weight,
    value_weight,
    query_down_weight,
    query_up_weight,
    value_down_weight,
    value_up_weight,
    output_gradient,
):
    window_width = tokens.shape[1]
    feats = tokens.shape[2]
    heads_kv = key_weight.shape[1] // HEAD_SIZE
    heads_q = query_weight.shape[1] // HEAD_SIZE
    head_group = heads_q // heads_kv
    normalized_input = normed_rows(tokens.reshape(window_width, feats), input_norm_scale)
    seg_own = trace_index.reshape(window_width).astype(jnp.bfloat16)
    seg_parts = []

    def add_keyval(piece):
        return add_rows(normalized_input, piece)

    query_frozen = add_rows(
        normalized_input, lax.all_gather(query_weight, "fsdp", axis=0, tiled=True)
    )
    k_base = add_keyval(lax.all_gather(key_weight, "fsdp", axis=0, tiled=True))
    value_frozen = add_keyval(lax.all_gather(value_weight, "fsdp", axis=0, tiled=True))
    query_reduced = jnp.dot(
        normalized_input, query_down_weight, preferred_element_type=jnp.float32
    ).astype(jnp.bfloat16)
    reduced_rows = jnp.dot(
        normalized_input, value_down_weight, preferred_element_type=jnp.float32
    ).astype(jnp.bfloat16)
    query_matrix = (
        query_frozen
        + ADAPTER_NAME * jnp.dot(query_reduced, query_up_weight, preferred_element_type=jnp.float32)
    ).astype(jnp.bfloat16)
    key_rows = k_base.astype(jnp.bfloat16)
    value_rows = (
        value_frozen
        + ADAPTER_NAME * jnp.dot(reduced_rows, value_up_weight, preferred_element_type=jnp.float32)
    ).astype(jnp.bfloat16)
    key_parts = []
    value_parts = []
    for distance in (2, 1):
        key_prev, value_prev, seg_prev = shifted((key_rows, value_rows, seg_own), "ctx", distance)
        key_parts.append(key_prev)
        value_parts.append(value_prev)
        seg_parts.append(seg_prev)
    keys_all = jnp.concatenate(key_parts + [key_rows], 0)
    values_all = jnp.concatenate(value_parts + [value_rows], 0)
    seg_keys = jnp.concatenate(seg_parts + [seg_own], 0)
    pos_q = jnp.arange(window_width, dtype=jnp.int32)[:, None]
    pos_k = jnp.arange(3 * window_width, dtype=jnp.int32)[None, :]
    position = lax.axis_index("ctx")
    mask = (
        (pos_k > pos_q)
        & (pos_k <= pos_q + 2 * window_width)
        & (seg_keys[None, :] == seg_own[:, None])
    )
    mask = mask & (
        (pos_k >= 2 * window_width) | (pos_k >= window_width) & (position >= 1) | (position >= 2)
    )
    q_heads = jnp.moveaxis(
        query_matrix.reshape(window_width, heads_kv, head_group, HEAD_SIZE), 1, 0
    )
    g_heads = jnp.moveaxis(
        output_gradient.reshape(window_width, heads_kv, head_group, HEAD_SIZE), 1, 0
    )
    k_heads = jnp.moveaxis(keys_all.reshape(3 * window_width, heads_kv, HEAD_SIZE), 1, 0)
    v_heads = jnp.moveaxis(values_all.reshape(3 * window_width, heads_kv, HEAD_SIZE), 1, 0)
    dquery_heads, dvalue_heads = lax.map(partial_attend(mask), (q_heads, k_heads, v_heads, g_heads))
    query_gradient = jnp.moveaxis(dquery_heads, 0, 1).reshape(window_width, heads_q * HEAD_SIZE)
    dvalue_triple = jnp.moveaxis(dvalue_heads, 0, 1).reshape(3 * window_width, heads_kv * HEAD_SIZE)
    value_gradient = dvalue_triple[2 * window_width :]
    for distance in (1, 2):
        begin = (2 - distance) * window_width
        value_gradient = value_gradient + shifted(
            dvalue_triple[begin : begin + window_width], "ctx", -distance
        )
    query_backward = jnp.dot(
        query_gradient, query_up_weight.T, preferred_element_type=jnp.float32
    ).astype(jnp.bfloat16)
    value_backward = jnp.dot(
        value_gradient, value_up_weight.astype(jnp.float32).T, precision=lax.Precision.HIGHEST
    )
    part_aq = jnp.dot(normalized_input.T, query_backward, preferred_element_type=jnp.float32)
    part_bq = jnp.dot(query_reduced.T, query_gradient, preferred_element_type=jnp.float32)
    part_av = jnp.dot(
        normalized_input.astype(jnp.float32).T, value_backward, precision=lax.Precision.HIGHEST
    )
    part_bv = jnp.dot(
        reduced_rows.astype(jnp.float32).T, value_gradient, precision=lax.Precision.HIGHEST
    )
    sum_aq, sum_bq, sum_av, sum_bv = lax.psum((part_aq, part_bq, part_av, part_bv), ("ctx", "fsdp"))
    token_total = lax.axis_size("ctx") * lax.axis_size("fsdp") * window_width
    coefficient = ADAPTER_NAME / math.sqrt(token_total)
    return (sum_aq * coefficient, sum_bq * coefficient, sum_av * coefficient, sum_bv * coefficient)


F32 = jnp.float32
BF16 = jnp.bfloat16
PLANE = 8


def dot(a, b, dims=((1,), (0,))):
    return lax.dot_general(a, b, (dims, ((), ())), preferred_element_type=F32)


def plane_kernel(
    chain, coefficient,
    raw, seg, gain, wq, wk, wv, qd, qu, vd, vu, grad,
    OUTQ, OUTV,
    N, M, WA, WV, G, SG, acc, accv, P, C, K, DQ, DV, LQ, LV,
    AQ, RAQ, RSQ, TQ, AV, RAV, RSV, TV,
    local_sem, w_send, w_recv, t_send, t_recv, g_send, g_recv, s_send, s_recv,
    up_send, up_recv, down_send, down_recv, vup_send, vup_recv, vdown_send, vdown_recv,
    q1_send, q1_recv, q2_send, q2_recv, q3_send, q3_recv,
    v1_send, v1_recv, v2_send, v2_recv, v3_send, v3_recv,
):
    x = lax.axis_index("ctx")
    f = lax.axis_index("fsdp")
    z = f // 4
    y = (f // 2) % 2
    c = f % 2
    tok, feats = raw.shape
    rows = wq.shape[0]
    qcols = wq.shape[1] // PLANE
    kcols = wk.shape[1] // PLANE
    acols = qcols + kcols
    piece = feats // PLANE
    seq = 2 * tok
    sub = tok // 4
    heads = qcols // kcols
    middle = (z > 0) & (z < chain - 1)
    outer = (z == 0) | (z == chain - 1)

    def coords(r):
        px = 1 - x if r & 4 else x
        py = 1 - y if r & 2 else y
        pc = 1 - c if r & 1 else c
        return px, py, pc

    def head_of(r):
        px, py, pc = coords(r)
        return (px * 2 + py) * 2 + pc

    def peer(r):
        px, py, pc = coords(r)
        return {"ctx": px, "fsdp": (z * 2 + py) * 2 + pc}

    def above(pz):
        return {"ctx": x, "fsdp": (pz * 2 + y) * 2 + c}

    def tok_slot(r):
        px, py, pc = coords(r)
        return (py * 2 + pc) * 2 + px

    def tok_piece(r, low, count):
        begin = tok_slot(r) * tok + low * sub
        return pl.ds(pl.multiple_of(begin, sub), count * sub)

    def tok_rows(r):
        return pl.ds(pl.multiple_of(tok_slot(r) * tok, tok), tok)

    def remote(src, dst, send, recv, device):
        return pltpu.make_async_remote_copy(
            src_ref=src, dst_ref=dst, send_sem=send, recv_sem=recv,
            device_id=device, device_id_type=pl.DeviceIdType.MESH,
        )

    barrier = pltpu.get_barrier_semaphore()
    for r in range(1, PLANE):
        pl.semaphore_signal(barrier, inc=1, device_id=peer(r), device_id_type=pl.DeviceIdType.MESH)
    for d in range(1, chain):
        pl.semaphore_signal(
            barrier, inc=1, device_id=above((z + d) % chain), device_id_type=pl.DeviceIdType.MESH
        )

    def w_rows(r):
        px, py, pc = coords(r)
        return pl.ds(pl.multiple_of(((z * 2 + py) * 2 + pc) * rows, rows), rows)

    def w_parts(r):
        h = head_of(r)
        own = w_rows(0)
        return (
            (wq.at[:, pl.ds(pl.multiple_of(h * qcols, qcols), qcols)], WA.at[own, pl.ds(0, qcols)]),
            (wk.at[:, pl.ds(pl.multiple_of(h * kcols, kcols), kcols)], WA.at[own, pl.ds(qcols, kcols)]),
            (wv.at[:, pl.ds(pl.multiple_of(h * kcols, kcols), kcols)], WV.at[own]),
        )

    def g_cols(r):
        h = head_of(r)
        return grad.at[:, pl.ds(pl.multiple_of(h * qcols, qcols), qcols)]

    local = [pltpu.make_async_copy(a, b, local_sem.at[i]) for i, (a, b) in enumerate(w_parts(0))]
    local.append(pltpu.make_async_copy(raw, N.at[tok_rows(0)], local_sem.at[3]))
    local.append(pltpu.make_async_copy(g_cols(0), G.at[tok_rows(0)], local_sem.at[4]))
    local.append(pltpu.make_async_copy(seg, SG.at[tok_slot(0)], local_sem.at[5]))
    for copy in local:
        copy.start()
    for i in range(2):
        local[i].wait()
    pl.semaphore_wait(barrier, PLANE - 1 + chain - 1)

    def half_rows(plane, half):
        py = y if half == 0 else 1 - y
        return pl.ds(pl.multiple_of((plane * 4 + py * 2) * rows, 2 * rows), 2 * rows)

    def quarter_rows(plane, quarter):
        px, py, pc = coords(quarter)
        return pl.ds(pl.multiple_of((plane * 4 + py * 2 + pc) * rows, rows), rows)

    def has_up(t):
        return (z < chain - 1) & (z - t >= 0)

    def has_down(t):
        return (z > 0) & (z + t <= chain - 1)

    def from_below(t):
        return z - 1 - t >= 0

    def from_above(t):
        return z + 1 + t <= chain - 1

    def pieces_of(t):
        return range(4) if t == 0 else range(2)

    def piece_rows(plane, t, i):
        return quarter_rows(plane, i) if t == 0 else half_rows(plane, i)

    def up_copy(t, i):
        at = WA.at[piece_rows(z - t, t, i)]
        return remote(at, at, up_send.at[t, i], up_recv.at[t, i], above(z + 1))

    def down_copy(t, i):
        at = WA.at[piece_rows(z + t, t, i)]
        return remote(at, at, down_send.at[t, i], down_recv.at[t, i], above(z - 1))

    def up_arrival(t, i):
        at = WA.at[piece_rows(z - 1 - t, t, i)]
        return remote(at, at, up_send.at[t, i], up_recv.at[t, i], above(z - 1))

    def down_arrival(t, i):
        at = WA.at[piece_rows(z + 1 + t, t, i)]
        return remote(at, at, down_send.at[t, i], down_recv.at[t, i], above(z + 1))

    def vup_copy(t, half):
        at = WV.at[half_rows(z - t, half)]
        return remote(at, at, vup_send.at[t, half], vup_recv.at[t, half], above(z + 1))

    def vdown_copy(t, half):
        at = WV.at[half_rows(z + t, half)]
        return remote(at, at, vdown_send.at[t, half], vdown_recv.at[t, half], above(z - 1))

    def vup_arrival(t, half):
        at = WV.at[half_rows(z - 1 - t, half)]
        return remote(at, at, vup_send.at[t, half], vup_recv.at[t, half], above(z - 1))

    def vdown_arrival(t, half):
        at = WV.at[half_rows(z + 1 + t, half)]
        return remote(at, at, vdown_send.at[t, half], vdown_recv.at[t, half], above(z + 1))

    def send_chain(t, i):
        @pl.when(has_up(t))
        def _():
            up_copy(t, i).start()

        @pl.when(has_down(t))
        def _():
            down_copy(t, i).start()

    def recv_chain(t, i):
        @pl.when(from_below(t))
        def _():
            up_arrival(t, i).wait_recv()

        @pl.when(from_above(t))
        def _():
            down_arrival(t, i).wait_recv()

    def recv_half(t, half):
        for i in (2 * half, 2 * half + 1) if t == 0 else (half,):
            recv_chain(t, i)

    def send_value_first(k):
        @pl.when(has_up(k - 1) & jnp.logical_not(has_up(k)))
        def _():
            for half in range(2):
                vup_copy(0, half).start()

        @pl.when(has_down(k - 1) & jnp.logical_not(has_down(k)))
        def _():
            for half in range(2):
                vdown_copy(0, half).start()

    def send_value(t, half):
        @pl.when(has_up(t))
        def _():
            vup_copy(t, half).start()

        @pl.when(has_down(t))
        def _():
            vdown_copy(t, half).start()

    def recv_value(t, half):
        @pl.when(from_below(t))
        def _():
            vup_arrival(t, half).wait_recv()

        @pl.when(from_above(t))
        def _():
            vdown_arrival(t, half).wait_recv()

    w_copies = {}
    for r in (1, 2, 3):
        w_copies[r] = [
            remote(a, b, w_send.at[r, i], w_recv.at[r, i], peer(r)) for i, (a, b) in enumerate(w_parts(r))
        ]
    for r in (1, 2, 3):
        for i in range(2):
            w_copies[r][i].start()
    send_chain(0, 0)
    for r in (1, 2, 3):
        w_copies[r][2].start()

    t_copies = []

    def send_token(r_mine, r_there, hop, low=0, count=4):
        at = N.at[tok_piece(r_mine, low, count)]
        source = raw.at[pl.ds(low * sub, count * sub)] if r_mine == 0 else at
        copy = remote(source, at, t_send.at[r_there, low], t_recv.at[r_there, low], peer(hop))
        copy.start()
        t_copies.append(copy)

    def wait_token(r, low=0, count=4):
        at = N.at[tok_piece(r, low, count)]
        remote(at, at, t_send.at[r, low], t_recv.at[r, low], peer(1)).wait_recv()

    send_token(0, 1, 1)
    send_token(0, 4, 4, 3, 1)
    send_token(0, 4, 4, 0, 3)
    for low in range(4):
        send_token(0, 2, 2, low, 1)
    g_copies = {}
    s_copies = {}
    for r in range(1, PLANE):
        g_copies[r] = remote(g_cols(r), G.at[tok_rows(0)], g_send.at[r], g_recv.at[r], peer(r))
        s_copies[r] = remote(seg, SG.at[tok_slot(0)], s_send.at[r], s_recv.at[r], peer(r))

    def wait_weight(r, value=False):
        at = w_rows(r)
        if value:
            ref = WV.at[at]
            remote(ref, ref, w_send.at[r, 2], w_recv.at[r, 2], peer(r)).wait_recv()
            return
        for i, (lo, width) in enumerate(((0, qcols), (qcols, kcols))):
            ref = WA.at[at, pl.ds(lo, width)]
            remote(ref, ref, w_send.at[r, i], w_recv.at[r, i], peer(r)).wait_recv()

    part_rows = 4 * tok

    def part_at(part, i, height):
        py = y if part == 0 else 1 - y
        return pl.ds(pl.multiple_of(py * part_rows + i * height, height), height)

    h = head_of(0)
    qu_own = qu[:, pl.ds(pl.multiple_of(h * qcols, qcols), qcols)]
    vu_own = vu[:, pl.ds(pl.multiple_of(h * kcols, kcols), kcols)]

    def prepare(r):
        height = tok // 2

        @pl.loop(0, 2)
        def _(i):
            begin = tok_slot(r) * tok + i * height
            at = pl.ds(pl.multiple_of(begin, height), height)
            flt = N[at, :].astype(F32)
            meansq = jnp.sum(flt * flt, axis=-1, keepdims=True) / feats
            M[at, :] = (flt * lax.rsqrt(meansq + EPS) * gain[...].astype(F32).reshape(1, feats)).astype(BF16)

        at = tok_rows(r)
        block = M[at, :]
        low_query = dot(block, qd[...], ((1,), (1,))).astype(BF16)
        low_value = dot(block, vd[...], ((1,), (1,))).astype(BF16)
        LQ[at, :] = low_query
        LV[at, :] = low_value
        acc[at, 0:qcols] = ADAPTER_NAME * dot(low_query, qu_own)
        acc[at, qcols:] = jnp.zeros((tok, kcols), F32)
        accv[at, :] = ADAPTER_NAME * dot(low_value, vu_own)

    def add_piece(plane, half, part):
        chosen = half_rows(plane, half)

        @pl.loop(0, part_rows // seq)
        def _(i):
            at = part_at(part, i, seq)
            acc[at, :] = acc[at, :] + dot(M[at, chosen], WA[chosen, :])

    def add_step(t, half, part):
        @pl.when(from_below(t))
        def _():
            add_piece(z - 1 - t, half, part)

        @pl.when(from_above(t))
        def _():
            add_piece(z + 1 + t, half, part)

    def add_value_piece(plane, half):
        chosen = half_rows(plane, half)

        @pl.loop(0, 2 * part_rows // seq)
        def _(i):
            at = pl.ds(pl.multiple_of(i * seq, seq), seq)
            accv[at, :] = accv[at, :] + dot(M[at, chosen], WV[chosen, :])

    def add_value(t, half):
        @pl.when(from_below(t))
        def _():
            add_value_piece(z - 1 - t, half)

        @pl.when(from_above(t))
        def _():
            add_value_piece(z + 1 + t, half)

    wait_weight(1)
    send_chain(0, 1)
    for r in range(1, PLANE):
        s_copies[r].start()
    local[3].wait()
    prepare(0)
    wait_token(1)
    prepare(1)
    wait_weight(2)
    send_chain(0, 2)
    wait_weight(3)
    send_chain(0, 3)
    recv_half(0, 0)
    send_chain(1, 0)
    wait_token(2, 0, 1)
    send_token(2, 6, 4, 0, 1)
    recv_half(0, 1)
    send_chain(1, 1)
    local[2].wait()
    wait_weight(1, True)
    wait_weight(2, True)
    wait_weight(3, True)
    send_value_first(1)
    wait_token(2, 1, 1)
    send_token(2, 6, 4, 1, 1)
    wait_token(4, 3, 1)
    send_token(4, 6, 2, 3, 1)
    wait_token(4, 0, 3)
    send_token(4, 5, 1)
    prepare(4)
    wait_token(2, 2, 1)
    send_token(2, 6, 4, 2, 1)
    for r in (6, 7, 4, 5, 2, 3, 1):
        g_copies[r].start()
    wait_token(5)
    prepare(5)
    recv_half(1, 0)
    send_chain(2, 0)
    for half in range(2):
        add_piece(z, half, 0)
    for half in range(2):
        add_step(0, half, 0)
    wait_token(2, 3, 1)
    send_token(2, 3, 1)
    prepare(2)
    wait_token(3)
    prepare(3)
    recv_half(1, 1)
    send_chain(2, 1)
    for k in range(2, chain):
        send_value_first(k)
    for half in range(2):
        add_step(1, half, 0)
    for low in range(4):
        wait_token(6, low, 1)
    send_token(6, 7, 1)
    prepare(6)
    wait_token(7)
    prepare(7)

    @pl.when(middle)
    def _():
        for half in range(2):
            recv_value(0, half)
            send_value(1, half)

    for half in range(2):
        add_piece(z, half, 1)
    for t in range(2):
        for half in range(2):
            add_step(t, half, 1)
    for t in range(2, chain - 1):
        for half in range(2):
            recv_half(t, half)
            if t + 1 < chain - 1:
                send_chain(t + 1, half)
            for part in range(2):
                add_step(t, half, part)

    tiles = PLANE * tok // seq
    local[4].wait()
    local[5].wait()
    for r in range(1, PLANE):
        at = G.at[tok_rows(r)]
        remote(at, at, g_send.at[r], g_recv.at[r], peer(r)).wait_recv()
        at = SG.at[tok_slot(r)]
        remote(at, at, s_send.at[r], s_recv.at[r], peer(r)).wait_recv()

    pos_i = lax.broadcasted_iota(jnp.int32, (seq, seq), 0)
    pos_j = lax.broadcasted_iota(jnp.int32, (seq, seq), 1)
    band = (pos_j <= pos_i) & (pos_j > pos_i - 2 * tok)

    @pl.loop(0, tiles, unroll=2)
    def _(i):
        at = pl.ds(pl.multiple_of(i * seq, seq), seq)
        q_all = acc[at, 0:qcols].astype(BF16)
        k = acc[at, qcols:].astype(BF16)
        K[at, :] = k
        g_all = G[at, :]
        traces = [SG[2 * i].astype(F32), SG[2 * i + 1].astype(F32)]
        along = jnp.concatenate(traces, axis=1)
        turned = [jnp.broadcast_to(own, (tok, tok)).T for own in traces]
        across = jnp.concatenate([jnp.concatenate([own, own], axis=1) for own in turned], axis=0)
        mask = band & (across == along)
        dv = jnp.zeros((seq, kcols), F32)
        for n in range(heads):
            q = q_all[:, n * kcols:(n + 1) * kcols]
            g = g_all[:, n * kcols:(n + 1) * kcols]
            t = jnp.tanh(dot(q, k, ((1,), (1,))) * (QSCALE / CAP))
            expo = jnp.where(mask, jnp.exp(CAP * t), 0.0)
            weights = expo * (1.0 / jnp.sum(expo, axis=-1, keepdims=True))
            weights16 = weights.astype(BF16)
            P[i * heads + n] = weights16
            C[i * heads + n] = weights * (1.0 - t * t)
            dv = dv + dot(weights16, g, ((0,), (0,)))
        DV[at, :] = dv.astype(BF16)

    @pl.when(middle)
    def _():
        for t in range(1, chain - 1):
            for half in range(2):
                recv_value(t, half)
                if t + 1 < chain - 1:
                    send_value(t + 1, half)

    def scatter(pull, part, arrived, send, recv):
        copies = []
        for r in (7, 6, 5, 4, 3, 2, 1, 0):
            columns = pl.ds(pl.multiple_of(head_of(r) * piece, piece), piece)
            part[r] = dot(pull, M[:, columns]).astype(BF16)
            if r > 0:
                copy = remote(part.at[r], arrived.at[r], send.at[r], recv.at[r], peer(r))
                copy.start()
                copies.append(copy)
        return copies

    def plane_sum(part, arrived):
        total = part[0].astype(F32)
        for r in range(1, PLANE):
            total = total + arrived[r].astype(F32)
        return total.astype(BF16)

    def share(sums, send, recv):
        own = sums.at[z]
        copies = []
        for d in range(1, chain):
            copy = remote(own, own, send.at[d], recv.at[d], above((z + d) % chain))
            copy.start()
            copies.append(copy)
        return copies

    def shared(sums, send, recv):
        for d in range(1, chain):
            at = sums.at[(z - d + chain) % chain]
            remote(at, at, send.at[d], recv.at[d], above((z + d) % chain)).wait_recv()
        total = sums[0].astype(F32)
        for d in range(1, chain):
            total = total + sums[d].astype(F32)
        return (total * coefficient).astype(BF16)

    def spread(total, mine, out, send, recv):
        mine[...] = total
        copies = []
        for r in (7, 6, 5, 4, 3, 2, 1):
            copy = remote(mine, out.at[h], send.at[r], recv.at[r], peer(r))
            copy.start()
            copies.append(copy)
        out[h] = total
        return copies

    def gathered(out, send, recv):
        for r in range(1, PLANE):
            at = out.at[head_of(r)]
            remote(at, at, send.at[r], recv.at[r], peer(r)).wait_recv()

    v1_copies = scatter(dot(vu_own, DV[...], ((1,), (1,))).astype(BF16), AV, RAV, v1_send, v1_recv)
    RSV.at[z][:, piece:] = dot(LV[...], DV[...], ((0,), (0,))).astype(BF16)
    for half in range(2):
        add_value_piece(z, half)
    for t in range(chain - 2):
        for half in range(2):
            @pl.when(outer)
            def _():
                recv_value(t, half)

            add_value(t, half)
    for copy in v1_copies:
        copy.wait_recv()
    RSV.at[z][:, 0:piece] = plane_sum(AV, RAV)
    v2_copies = share(RSV, v2_send, v2_recv)
    for half in range(2):
        @pl.when(outer)
        def _():
            recv_value(chain - 2, half)

        add_value(chain - 2, half)

    @pl.loop(0, tiles, unroll=2)
    def _(i):
        at = pl.ds(pl.multiple_of(i * seq, seq), seq)
        v = accv[at, :].astype(BF16)
        k = K[at, :]
        for n in range(heads):
            g = G[at, n * kcols:(n + 1) * kcols]
            dweight = dot(g, v, ((1,), (1,)))
            delta = jnp.sum(P[i * heads + n].astype(F32) * dweight, axis=-1, keepdims=True)
            dscore = (C[i * heads + n] * (dweight - delta)).astype(BF16)
            DQ[at, n * kcols:(n + 1) * kcols] = (dot(dscore, k) * QSCALE).astype(BF16)

    q1_copies = scatter(dot(qu_own, DQ[...], ((1,), (1,))).astype(BF16), AQ, RAQ, q1_send, q1_recv)
    RSQ.at[z][:, piece:] = dot(LQ[...], DQ[...], ((0,), (0,))).astype(BF16)
    v3_copies = spread(shared(RSV, v2_send, v2_recv), TV, OUTV, v3_send, v3_recv)
    for copy in q1_copies:
        copy.wait_recv()
    RSQ.at[z][:, 0:piece] = plane_sum(AQ, RAQ)
    q2_copies = share(RSQ, q2_send, q2_recv)
    q3_copies = spread(shared(RSQ, q2_send, q2_recv), TQ, OUTQ, q3_send, q3_recv)
    gathered(OUTV, v3_send, v3_recv)
    gathered(OUTQ, q3_send, q3_recv)

    for r in (1, 2, 3):
        for copy in w_copies[r]:
            copy.wait_send()
    for copy in t_copies:
        copy.wait_send()
    for r in range(1, PLANE):
        g_copies[r].wait_send()
        s_copies[r].wait_send()
    for t in range(chain - 1):
        @pl.when(has_up(t))
        def _():
            for i in pieces_of(t):
                up_copy(t, i).wait_send()
            for half in range(2):
                vup_copy(t, half).wait_send()

        @pl.when(has_down(t))
        def _():
            for i in pieces_of(t):
                down_copy(t, i).wait_send()
            for half in range(2):
                vdown_copy(t, half).wait_send()
    for copy in v1_copies + v2_copies + v3_copies + q1_copies + q2_copies + q3_copies:
        copy.wait_send()


def unpack_kernel(outq, outv, out_aq, out_bq, out_av, out_bv):
    feats = out_aq.shape[1]
    piece = feats // PLANE
    qcols = out_bq.shape[1] // PLANE
    kcols = out_bv.shape[1] // PLANE
    for h in range(PLANE):
        value = outq[h].astype(F32)
        out_aq[:, h * piece:(h + 1) * piece] = value[:, 0:piece]
        out_bq[:, h * qcols:(h + 1) * qcols] = value[:, piece:]
        value = outv[h].astype(F32)
        out_av[:, h * piece:(h + 1) * piece] = value[:, 0:piece]
        out_bv[:, h * kcols:(h + 1) * kcols] = value[:, piece:]


def on_plane(
    tokens,
    trace_index,
    input_norm_scale,
    query_weight,
    key_weight,
    value_weight,
    query_down_weight,
    query_up_weight,
    value_down_weight,
    value_up_weight,
    output_gradient,
):
    tok = tokens.shape[1]
    feats = tokens.shape[2]
    fsdp = lax.axis_size("fsdp")
    chain = fsdp // 4
    ranks = query_down_weight.shape[1]
    qcols = query_weight.shape[1] // PLANE
    kcols = key_weight.shape[1] // PLANE
    piece = feats // PLANE
    many = PLANE * tok
    token_total = lax.axis_size("ctx") * fsdp * tok
    coefficient = ADAPTER_NAME / math.sqrt(token_total)
    hbm = pl.BlockSpec(memory_space=pltpu.HBM)
    vmem = pl.BlockSpec(memory_space=pltpu.VMEM)
    dma = pltpu.SemaphoreType.DMA
    steps = chain - 1
    tiles = many // (2 * tok)
    heads = qcols // kcols
    outq, outv = pl.pallas_call(
        functools.partial(plane_kernel, chain, coefficient),
        out_shape=(
            pltpu.VMEM((PLANE, ranks, piece + qcols), BF16),
            pltpu.VMEM((PLANE, ranks, piece + kcols), BF16),
        ),
        in_specs=[hbm, hbm, vmem, hbm, hbm, hbm, vmem, vmem, vmem, vmem, hbm],
        out_specs=(vmem, vmem),
        scratch_shapes=[
            pltpu.VMEM((many, feats), BF16),
            pltpu.VMEM((many, feats), BF16),
            pltpu.VMEM((feats, qcols + kcols), BF16),
            pltpu.VMEM((feats, kcols), BF16),
            pltpu.VMEM((many, qcols), BF16),
            pltpu.VMEM((PLANE, 1, tok), jnp.int32),
            pltpu.VMEM((many, qcols + kcols), F32),
            pltpu.VMEM((many, kcols), F32),
            pltpu.VMEM((tiles * heads, 2 * tok, 2 * tok), BF16),
            pltpu.VMEM((tiles * heads, 2 * tok, 2 * tok), F32),
            pltpu.VMEM((many, kcols), BF16),
            pltpu.VMEM((many, qcols), BF16),
            pltpu.VMEM((many, kcols), BF16),
            pltpu.VMEM((many, ranks), BF16),
            pltpu.VMEM((many, ranks), BF16),
            pltpu.VMEM((PLANE, ranks, piece), BF16),
            pltpu.VMEM((PLANE, ranks, piece), BF16),
            pltpu.VMEM((chain, ranks, piece + qcols), BF16),
            pltpu.VMEM((ranks, piece + qcols), BF16),
            pltpu.VMEM((PLANE, ranks, piece), BF16),
            pltpu.VMEM((PLANE, ranks, piece), BF16),
            pltpu.VMEM((chain, ranks, piece + kcols), BF16),
            pltpu.VMEM((ranks, piece + kcols), BF16),
            dma((6,)),
            dma((4, 3)), dma((4, 3)),
            dma((8, 4)), dma((8, 4)), dma((8,)), dma((8,)), dma((8,)), dma((8,)),
            dma((steps, 4)), dma((steps, 4)), dma((steps, 4)), dma((steps, 4)),
            dma((steps, 2)), dma((steps, 2)), dma((steps, 2)), dma((steps, 2)),
            dma((8,)), dma((8,)), dma((chain,)), dma((chain,)), dma((8,)), dma((8,)),
            dma((8,)), dma((8,)), dma((chain,)), dma((chain,)), dma((8,)), dma((8,)),
        ],
        compiler_params=pltpu.CompilerParams(
            collective_id=0, has_side_effects=True, vmem_limit_bytes=56 * 1024 * 1024
        ),
    )(
        tokens.reshape(tok, feats), trace_index, input_norm_scale,
        query_weight, key_weight, value_weight,
        query_down_weight.T, query_up_weight, value_down_weight.T, value_up_weight,
        output_gradient.reshape(tok, output_gradient.shape[2]),
    )
    aq, bq, av, bv = pl.pallas_call(
        unpack_kernel,
        out_shape=(
            jax.ShapeDtypeStruct((ranks, feats), F32),
            jax.ShapeDtypeStruct((ranks, query_weight.shape[1]), F32),
            jax.ShapeDtypeStruct((ranks, feats), F32),
            jax.ShapeDtypeStruct((ranks, value_weight.shape[1]), F32),
        ),
        in_specs=[vmem, vmem],
        out_specs=(vmem, vmem, vmem, vmem),
        compiler_params=pltpu.CompilerParams(vmem_limit_bytes=16 * 1024 * 1024),
    )(outq, outv)
    return (aq.T, bq, av.T, bv)


def solution(mesh):
    shape = mesh.shape
    planes = shape["groups"] == 1 and shape["ctx"] == 2 and shape["fsdp"] % 4 == 0 and shape["fsdp"] > 8
    return jax.shard_map(
        on_plane if planes else on_device,
        mesh=mesh,
        in_specs=(
            P(("groups", "fsdp"), "ctx", None),
            P(("groups", "fsdp"), "ctx"),
            P(),
            P("fsdp", None),
            P("fsdp", None),
            P("fsdp", None),
            P(),
            P(),
            P(),
            P(),
            P(("groups", "fsdp"), "ctx", None),
        ),
        out_specs=(P("groups", None), P("groups", None), P("groups", None), P("groups", None)),
        check_vma=False,
    )
```

```python
import functools
import math

import jax
import jax.numpy as jnp
from jax import lax
from jax.experimental import pallas as pl
from jax.experimental.pallas import tpu as pltpu
from jax.sharding import PartitionSpec as P

HEAD_SIZE = 128


CAP = 50.0
QSCALE = 1.0 / 12.0
ADAPTER_NAME = 0.5
EPS = 1e-06


def shifted(value, axis, by):
    devices = lax.axis_size(axis)
    pairs = [(i, i + by) for i in range(devices) if 0 <= i + by < devices]
    return lax.ppermute(value, axis, pairs)


def normed_rows(values, gain):
    flt = values.astype(jnp.float32)
    meansq = jnp.mean(flt * flt, axis=-1, keepdims=True)
    return (flt * lax.rsqrt(meansq + EPS) * gain.astype(jnp.float32)).astype(jnp.bfloat16)


def add_rows(left, piece):
    return jnp.dot(left, piece, preferred_element_type=jnp.float32)


def attend_head(operands, mask):
    q_head, k_head, v_head, g_head = operands
    s = jnp.einsum("igd,jd->gij", q_head, k_head, preferred_element_type=jnp.float32) * QSCALE
    t = jnp.tanh(s / CAP)
    capped = CAP * t
    expo = jnp.where(mask[None], jnp.exp(capped), jnp.float32(0.0))
    weights = expo / jnp.sum(expo, axis=-1, keepdims=True)
    weights16 = weights.astype(jnp.bfloat16)
    attended = jnp.einsum("gij,jd->igd", weights16, v_head, preferred_element_type=jnp.float32)
    dweight = jnp.einsum("igd,jd->gij", g_head, v_head, preferred_element_type=jnp.float32)
    delta = jnp.sum(g_head.astype(jnp.float32) * attended, axis=-1).T
    dscore = (weights * (dweight - delta[..., None]) * (1.0 - t * t) * QSCALE).astype(jnp.bfloat16)
    query_gradient = jnp.einsum(
        "gij,jd->igd", dscore, k_head, preferred_element_type=jnp.float32
    ).astype(jnp.bfloat16)
    value_gradient = jnp.einsum(
        "gij,igd->jd", weights16, g_head, preferred_element_type=jnp.float32
    )
    return (query_gradient, value_gradient)


def partial_attend(mask):

    def run_head(operands):
        return attend_head(operands, mask)

    return run_head


def on_device(
    tokens,
    trace_index,
    input_norm_scale,
    query_weight,
    key_weight,
    value_weight,
    query_down_weight,
    query_up_weight,
    value_down_weight,
    value_up_weight,
    output_gradient,
):
    window_width = tokens.shape[1]
    feats = tokens.shape[2]
    heads_kv = key_weight.shape[1] // HEAD_SIZE
    heads_q = query_weight.shape[1] // HEAD_SIZE
    head_group = heads_q // heads_kv
    normalized_input = normed_rows(tokens.reshape(window_width, feats), input_norm_scale)
    seg_own = trace_index.reshape(window_width).astype(jnp.bfloat16)
    seg_parts = []

    def add_keyval(piece):
        return add_rows(normalized_input, piece)

    query_frozen = add_rows(
        normalized_input, lax.all_gather(query_weight, "fsdp", axis=0, tiled=True)
    )
    k_base = add_keyval(lax.all_gather(key_weight, "fsdp", axis=0, tiled=True))
    value_frozen = add_keyval(lax.all_gather(value_weight, "fsdp", axis=0, tiled=True))
    query_reduced = jnp.dot(
        normalized_input, query_down_weight, preferred_element_type=jnp.float32
    ).astype(jnp.bfloat16)
    reduced_rows = jnp.dot(
        normalized_input, value_down_weight, preferred_element_type=jnp.float32
    ).astype(jnp.bfloat16)
    query_matrix = (
        query_frozen
        + ADAPTER_NAME * jnp.dot(query_reduced, query_up_weight, preferred_element_type=jnp.float32)
    ).astype(jnp.bfloat16)
    key_rows = k_base.astype(jnp.bfloat16)
    value_rows = (
        value_frozen
        + ADAPTER_NAME * jnp.dot(reduced_rows, value_up_weight, preferred_element_type=jnp.float32)
    ).astype(jnp.bfloat16)
    key_parts = []
    value_parts = []
    for distance in (2, 1):
        key_prev, value_prev, seg_prev = shifted((key_rows, value_rows, seg_own), "ctx", distance)
        key_parts.append(key_prev)
        value_parts.append(value_prev)
        seg_parts.append(seg_prev)
    keys_all = jnp.concatenate(key_parts + [key_rows], 0)
    values_all = jnp.concatenate(value_parts + [value_rows], 0)
    seg_keys = jnp.concatenate(seg_parts + [seg_own], 0)
    pos_q = jnp.arange(window_width, dtype=jnp.int32)[:, None]
    pos_k = jnp.arange(3 * window_width, dtype=jnp.int32)[None, :]
    position = lax.axis_index("ctx")
    mask = (
        (pos_k > pos_q)
        & (pos_k <= pos_q + 2 * window_width)
        & (seg_keys[None, :] == seg_own[:, None])
    )
    mask = mask & (
        (pos_k >= 2 * window_width) | (pos_k >= window_width) & (position >= 1) | (position >= 2)
    )
    q_heads = jnp.moveaxis(
        query_matrix.reshape(window_width, heads_kv, head_group, HEAD_SIZE), 1, 0
    )
    g_heads = jnp.moveaxis(
        output_gradient.reshape(window_width, heads_kv, head_group, HEAD_SIZE), 1, 0
    )
    k_heads = jnp.moveaxis(keys_all.reshape(3 * window_width, heads_kv, HEAD_SIZE), 1, 0)
    v_heads = jnp.moveaxis(values_all.reshape(3 * window_width, heads_kv, HEAD_SIZE), 1, 0)
    dquery_heads, dvalue_heads = lax.map(partial_attend(mask), (q_heads, k_heads, v_heads, g_heads))
    query_gradient = jnp.moveaxis(dquery_heads, 0, 1).reshape(window_width, heads_q * HEAD_SIZE)
    dvalue_triple = jnp.moveaxis(dvalue_heads, 0, 1).reshape(3 * window_width, heads_kv * HEAD_SIZE)
    value_gradient = dvalue_triple[2 * window_width :]
    for distance in (1, 2):
        begin = (2 - distance) * window_width
        value_gradient = value_gradient + shifted(
            dvalue_triple[begin : begin + window_width], "ctx", -distance
        )
    query_backward = jnp.dot(
        query_gradient, query_up_weight.T, preferred_element_type=jnp.float32
    ).astype(jnp.bfloat16)
    value_backward = jnp.dot(
        value_gradient, value_up_weight.astype(jnp.float32).T, precision=lax.Precision.HIGHEST
    )
    part_aq = jnp.dot(normalized_input.T, query_backward, preferred_element_type=jnp.float32)
    part_bq = jnp.dot(query_reduced.T, query_gradient, preferred_element_type=jnp.float32)
    part_av = jnp.dot(
        normalized_input.astype(jnp.float32).T, value_backward, precision=lax.Precision.HIGHEST
    )
    part_bv = jnp.dot(
        reduced_rows.astype(jnp.float32).T, value_gradient, precision=lax.Precision.HIGHEST
    )
    sum_aq, sum_bq, sum_av, sum_bv = lax.psum((part_aq, part_bq, part_av, part_bv), ("ctx", "fsdp"))
    token_total = lax.axis_size("ctx") * lax.axis_size("fsdp") * window_width
    coefficient = ADAPTER_NAME / math.sqrt(token_total)
    return (sum_aq * coefficient, sum_bq * coefficient, sum_av * coefficient, sum_bv * coefficient)


F32 = jnp.float32
BF16 = jnp.bfloat16
PLANE = 8


def dot(a, b, dims=((1,), (0,))):
    return lax.dot_general(a, b, (dims, ((), ())), preferred_element_type=F32)


def plane_kernel(
    chain, coefficient,
    raw, seg, gain_in, wq, wk, wv, qd, qu_in, vd, vu_in, grad,
    OUTA, OUTB, OUTV,
    N, M, WA, WV, G, SG, acc, accv, P, C, K, DQ, DV, LL,
    gain, down, qu, vu,
    PQ, RPQ, PV, RPV, RSA, RSB, RSV, TA, TB, TV,
    local_sem, w_send, w_recv, t_send, t_recv, g_sem, s_sem,
    up_send, up_recv, down_send, down_recv, vup_send, vup_recv, vdown_send, vdown_recv,
    q1_send, q1_recv, v1_send, v1_recv, a_sem, b_sem, v_sem,
):
    x = lax.axis_index("ctx")
    f = lax.axis_index("fsdp")
    z = f // 4
    y = (f // 2) % 2
    c = f % 2
    tok, feats = raw.shape
    rows = wq.shape[0]
    qcols = wq.shape[1] // PLANE
    kcols = wk.shape[1] // PLANE
    acols = qcols + kcols
    piece = feats // PLANE
    seq = 2 * tok
    sub = tok // 4
    heads = qcols // kcols
    ranks = qd.shape[0]
    middle = (z > 0) & (z < chain - 1)
    outer = (z == 0) | (z == chain - 1)

    def coords(r):
        px = 1 - x if r & 4 else x
        py = 1 - y if r & 2 else y
        pc = 1 - c if r & 1 else c
        return px, py, pc

    def head_of(r):
        px, py, pc = coords(r)
        return (px * 2 + py) * 2 + pc

    def peer(r):
        px, py, pc = coords(r)
        return {"ctx": px, "fsdp": (z * 2 + py) * 2 + pc}

    def above(pz):
        return {"ctx": x, "fsdp": (pz * 2 + y) * 2 + c}

    def tok_slot(r):
        px, py, pc = coords(r)
        return (py * 2 + pc) * 2 + px

    def tok_piece(r, low, count):
        begin = tok_slot(r) * tok + low * sub
        return pl.ds(pl.multiple_of(begin, sub), count * sub)

    def tok_rows(r):
        return pl.ds(pl.multiple_of(tok_slot(r) * tok, tok), tok)

    def remote(src, dst, send, recv, device):
        return pltpu.make_async_remote_copy(
            src_ref=src, dst_ref=dst, send_sem=send, recv_sem=recv,
            device_id=device, device_id_type=pl.DeviceIdType.MESH,
        )

    barrier = pltpu.get_barrier_semaphore()
    for r in range(1, PLANE):
        pl.semaphore_signal(barrier, inc=1, device_id=peer(r), device_id_type=pl.DeviceIdType.MESH)
    for d in range(1, chain):
        pl.semaphore_signal(
            barrier, inc=1, device_id=above((z + d) % chain), device_id_type=pl.DeviceIdType.MESH
        )

    def w_rows(r):
        px, py, pc = coords(r)
        return pl.ds(pl.multiple_of(((z * 2 + py) * 2 + pc) * rows, rows), rows)

    def w_parts(r):
        h = head_of(r)
        own = w_rows(0)
        return (
            (wq.at[:, pl.ds(pl.multiple_of(h * qcols, qcols), qcols)], WA.at[own, pl.ds(0, qcols)]),
            (wk.at[:, pl.ds(pl.multiple_of(h * kcols, kcols), kcols)], WA.at[own, pl.ds(qcols, kcols)]),
            (wv.at[:, pl.ds(pl.multiple_of(h * kcols, kcols), kcols)], WV.at[own]),
        )

    def g_cols(r):
        h = head_of(r)
        return grad.at[:, pl.ds(pl.multiple_of(h * qcols, qcols), qcols)]

    local = [pltpu.make_async_copy(a, b, local_sem.at[i]) for i, (a, b) in enumerate(w_parts(0))]
    local.append(pltpu.make_async_copy(raw, N.at[tok_rows(0)], local_sem.at[3]))
    local.append(pltpu.make_async_copy(g_cols(0), G.at[tok_rows(0)], local_sem.at[4]))
    local.append(pltpu.make_async_copy(seg, SG.at[tok_slot(0)], local_sem.at[5]))
    local.append(pltpu.make_async_copy(qd, down.at[pl.ds(0, ranks)], local_sem.at[6]))
    local.append(pltpu.make_async_copy(vd, down.at[pl.ds(ranks, ranks)], local_sem.at[7]))
    local.append(pltpu.make_async_copy(qu_in, qu, local_sem.at[8]))
    local.append(pltpu.make_async_copy(vu_in, vu, local_sem.at[9]))
    local.append(pltpu.make_async_copy(gain_in, gain, local_sem.at[10]))
    for copy in local:
        copy.start()
    for i in range(2):
        local[i].wait()
    pl.semaphore_wait(barrier, PLANE - 1 + chain - 1)

    def half_rows(plane, half):
        py = y if half == 0 else 1 - y
        return pl.ds(pl.multiple_of((plane * 4 + py * 2) * rows, 2 * rows), 2 * rows)

    def quarter_rows(plane, quarter):
        px, py, pc = coords(quarter)
        return pl.ds(pl.multiple_of((plane * 4 + py * 2 + pc) * rows, rows), rows)

    def has_up(t):
        return (z < chain - 1) & (z - t >= 0)

    def has_down(t):
        return (z > 0) & (z + t <= chain - 1)

    def from_below(t):
        return z - 1 - t >= 0

    def from_above(t):
        return z + 1 + t <= chain - 1

    def pieces_of(t):
        return range(4) if t == 0 else range(2)

    def piece_rows(plane, t, i):
        return quarter_rows(plane, i) if t == 0 else half_rows(plane, i)

    def half_of(t, i):
        return i // 2 if t == 0 else i

    def plane_rows(plane):
        return pl.ds(pl.multiple_of(plane * 4 * rows, 4 * rows), 4 * rows)

    def up_copy(t, i):
        at = WA.at[piece_rows(z - t, t, i)]
        return remote(at, at, up_send.at[t], up_recv.at[t, half_of(t, i)], above(z + 1))

    def down_copy(t, i):
        at = WA.at[piece_rows(z + t, t, i)]
        return remote(at, at, down_send.at[t], down_recv.at[t, half_of(t, i)], above(z - 1))

    def up_arrival(t, half):
        at = WA.at[half_rows(z - 1 - t, half)]
        return remote(at, at, up_send.at[t], up_recv.at[t, half], above(z - 1))

    def down_arrival(t, half):
        at = WA.at[half_rows(z + 1 + t, half)]
        return remote(at, at, down_send.at[t], down_recv.at[t, half], above(z + 1))

    def vup_copy(t, half):
        at = WV.at[half_rows(z - t, half)]
        return remote(at, at, vup_send.at[t], vup_recv.at[t, half], above(z + 1))

    def vdown_copy(t, half):
        at = WV.at[half_rows(z + t, half)]
        return remote(at, at, vdown_send.at[t], vdown_recv.at[t, half], above(z - 1))

    def vup_arrival(t, half):
        at = WV.at[half_rows(z - 1 - t, half)]
        return remote(at, at, vup_send.at[t], vup_recv.at[t, half], above(z - 1))

    def vdown_arrival(t, half):
        at = WV.at[half_rows(z + 1 + t, half)]
        return remote(at, at, vdown_send.at[t], vdown_recv.at[t, half], above(z + 1))

    def send_chain(t, i):
        @pl.when(has_up(t))
        def _():
            up_copy(t, i).start()

        @pl.when(has_down(t))
        def _():
            down_copy(t, i).start()

    def recv_half(t, half):
        @pl.when(from_below(t))
        def _():
            up_arrival(t, half).wait_recv()

        @pl.when(from_above(t))
        def _():
            down_arrival(t, half).wait_recv()

    def send_value_first(k):
        @pl.when(has_up(k - 1) & jnp.logical_not(has_up(k)))
        def _():
            for half in range(2):
                vup_copy(0, half).start()

        @pl.when(has_down(k - 1) & jnp.logical_not(has_down(k)))
        def _():
            for half in range(2):
                vdown_copy(0, half).start()

    def send_value(t, half):
        @pl.when(has_up(t))
        def _():
            vup_copy(t, half).start()

        @pl.when(has_down(t))
        def _():
            vdown_copy(t, half).start()

    def recv_value(t, half):
        @pl.when(from_below(t))
        def _():
            vup_arrival(t, half).wait_recv()

        @pl.when(from_above(t))
        def _():
            vdown_arrival(t, half).wait_recv()

    w_copies = {}
    for r in (1, 2, 3):
        w_copies[r] = [
            remote(a, b, w_send.at[i // 2], w_recv.at[r if i < 2 else 0], peer(r))
            for i, (a, b) in enumerate(w_parts(r))
        ]
    for r in (1, 2, 3):
        for i in range(2):
            w_copies[r][i].start()
    send_chain(0, 0)
    for r in (1, 2, 3):
        w_copies[r][2].start()

    t_slot = {(1, 0): 0, (4, 3): 1, (4, 0): 2, (5, 0): 3, (3, 0): 4, (7, 0): 5}
    for low in range(4):
        t_slot[2, low] = 6 + low
        t_slot[6, low] = 10

    def send_token(r_mine, r_there, hop, low=0, count=4):
        at = N.at[tok_piece(r_mine, low, count)]
        source = raw.at[pl.ds(low * sub, count * sub)] if r_mine == 0 else at
        remote(source, at, t_send.at[0], t_recv.at[t_slot[r_there, low]], peer(hop)).start()

    def wait_token(r, low=0, count=4):
        at = N.at[tok_piece(r, low, count)]
        remote(at, at, t_send.at[0], t_recv.at[t_slot[r, low]], peer(1)).wait_recv()

    send_token(0, 1, 1)
    send_token(0, 4, 4, 3, 1)
    send_token(0, 4, 4, 0, 3)
    for low in range(4):
        send_token(0, 2, 2, low, 1)
    g_copies = {}
    s_copies = {}
    for r in range(1, PLANE):
        g_copies[r] = remote(g_cols(r), G.at[tok_rows(0)], g_sem.at[0], g_sem.at[1], peer(r))
        s_copies[r] = remote(seg, SG.at[tok_slot(0)], s_sem.at[0], s_sem.at[1], peer(r))

    def wait_weight(r):
        ref = WA.at[w_rows(r)]
        remote(ref, ref, w_send.at[0], w_recv.at[r], peer(r)).wait_recv()

    def wait_values():
        ref = WV.at[pl.ds(0, 3 * rows)]
        remote(ref, ref, w_send.at[1], w_recv.at[0], peer(1)).wait_recv()

    part_rows = 4 * tok

    def part_at(part, i, height):
        py = y if part == 0 else 1 - y
        return pl.ds(pl.multiple_of(py * part_rows + i * height, height), height)

    h = head_of(0)

    def query_up():
        return qu[:, pl.ds(pl.multiple_of(h * qcols, qcols), qcols)]

    def value_up():
        return vu[:, pl.ds(pl.multiple_of(h * kcols, kcols), kcols)]

    def prepare(r):
        height = tok // 2

        @pl.loop(0, 2)
        def _(i):
            begin = tok_slot(r) * tok + i * height
            at = pl.ds(pl.multiple_of(begin, height), height)
            flt = N[at, :].astype(F32)
            meansq = jnp.sum(flt * flt, axis=-1, keepdims=True) / feats
            M[at, :] = (flt * lax.rsqrt(meansq + EPS) * gain[...].astype(F32).reshape(1, feats)).astype(BF16)

        at = tok_rows(r)
        block = M[at, :]
        low = dot(block, down[...], ((1,), (1,))).astype(BF16)
        LL[at, :] = low
        filler = jnp.zeros((ranks, qcols), BF16)
        acc[at, 0:qcols] = ADAPTER_NAME * dot(low, jnp.concatenate([query_up(), filler], axis=0))
        acc[at, qcols:] = jnp.zeros((tok, kcols), F32)
        accv[at, :] = ADAPTER_NAME * dot(low, jnp.concatenate([filler[:, 0:kcols], value_up()], axis=0))

    def add_piece(plane, half, part):
        chosen = half_rows(plane, half)

        @pl.loop(0, part_rows // seq)
        def _(i):
            at = part_at(part, i, seq)
            acc[at, :] = acc[at, :] + dot(M[at, chosen], WA[chosen, :])

    def add_step(t, half, part):
        @pl.when(from_below(t))
        def _():
            add_piece(z - 1 - t, half, part)

        @pl.when(from_above(t))
        def _():
            add_piece(z + 1 + t, half, part)

    def add_value_piece(plane, half):
        chosen = half_rows(plane, half)

        @pl.loop(0, 2 * part_rows // seq)
        def _(i):
            at = pl.ds(pl.multiple_of(i * seq, seq), seq)
            accv[at, :] = accv[at, :] + dot(M[at, chosen], WV[chosen, :])

    def add_value(t, half):
        @pl.when(from_below(t))
        def _():
            add_value_piece(z - 1 - t, half)

        @pl.when(from_above(t))
        def _():
            add_value_piece(z + 1 + t, half)

    wait_weight(1)
    send_chain(0, 1)
    for r in range(1, PLANE):
        s_copies[r].start()
    local[3].wait()
    for i in range(6, 11):
        local[i].wait()
    prepare(0)
    wait_token(1)
    prepare(1)
    wait_weight(2)
    send_chain(0, 2)
    wait_weight(3)
    send_chain(0, 3)
    recv_half(0, 0)
    send_chain(1, 0)
    wait_token(2, 0, 1)
    send_token(2, 6, 4, 0, 1)
    recv_half(0, 1)
    send_chain(1, 1)
    local[2].wait()
    wait_values()
    send_value_first(1)
    wait_token(2, 1, 1)
    send_token(2, 6, 4, 1, 1)
    wait_token(4, 3, 1)
    send_token(4, 6, 2, 3, 1)
    wait_token(4, 0, 3)
    send_token(4, 5, 1)
    prepare(4)
    wait_token(2, 2, 1)
    send_token(2, 6, 4, 2, 1)
    for r in (6, 7, 4, 5, 2, 3, 1):
        g_copies[r].start()
    wait_token(5)
    prepare(5)
    recv_half(1, 0)
    send_chain(2, 0)
    for half in range(2):
        add_piece(z, half, 0)
    for half in range(2):
        add_step(0, half, 0)
    wait_token(2, 3, 1)
    send_token(2, 3, 1)
    prepare(2)
    wait_token(3)
    prepare(3)
    recv_half(1, 1)
    send_chain(2, 1)
    for k in range(2, chain):
        send_value_first(k)
    for half in range(2):
        add_step(1, half, 0)
    wait_token(6)
    send_token(6, 7, 1)
    prepare(6)
    wait_token(7)
    prepare(7)

    @pl.when(middle)
    def _():
        for half in range(2):
            recv_value(0, half)
            send_value(1, half)

    for half in range(2):
        add_piece(z, half, 1)
    for t in range(2):
        for half in range(2):
            add_step(t, half, 1)
    for t in range(2, chain - 1):
        for half in range(2):
            recv_half(t, half)
            if t + 1 < chain - 1:
                send_chain(t + 1, half)
            for part in range(2):
                add_step(t, half, part)

    tiles = PLANE * tok // seq
    local[4].wait()
    local[5].wait()
    g_others = G.at[pl.ds(0, (PLANE - 1) * tok)]
    g_all_copies = remote(g_others, g_others, g_sem.at[0], g_sem.at[1], peer(1))
    g_all_copies.wait_recv()
    s_others = SG.at[pl.ds(0, PLANE - 1)]
    s_all_copies = remote(s_others, s_others, s_sem.at[0], s_sem.at[1], peer(1))
    s_all_copies.wait_recv()

    pos_i = lax.broadcasted_iota(jnp.int32, (seq, seq), 0)
    pos_j = lax.broadcasted_iota(jnp.int32, (seq, seq), 1)
    band = (pos_j <= pos_i) & (pos_j > pos_i - 2 * tok)

    @pl.loop(0, tiles, unroll=2)
    def _(i):
        at = pl.ds(pl.multiple_of(i * seq, seq), seq)
        q_all = acc[at, 0:qcols].astype(BF16)
        k = acc[at, qcols:].astype(BF16)
        K[at, :] = k
        g_all = G[at, :]
        traces = [SG[2 * i].astype(F32), SG[2 * i + 1].astype(F32)]
        along = jnp.concatenate(traces, axis=1)
        turned = [jnp.broadcast_to(own, (tok, tok)).T for own in traces]
        across = jnp.concatenate([jnp.concatenate([own, own], axis=1) for own in turned], axis=0)
        mask = band & (across == along)
        dv = jnp.zeros((seq, kcols), F32)
        for n in range(heads):
            q = q_all[:, n * kcols:(n + 1) * kcols]
            g = g_all[:, n * kcols:(n + 1) * kcols]
            t = jnp.tanh(dot(q, k, ((1,), (1,))) * (QSCALE / CAP))
            expo = jnp.where(mask, jnp.exp(CAP * t), 0.0)
            weights = expo * (1.0 / jnp.sum(expo, axis=-1, keepdims=True))
            weights16 = weights.astype(BF16)
            P[i * heads + n] = weights16
            C[i * heads + n] = weights * (1.0 - t * t)
            dv = dv + dot(weights16, g, ((0,), (0,)))
        DV[at, :] = dv.astype(BF16)

    @pl.when(middle)
    def _():
        for t in range(1, chain - 1):
            for half in range(2):
                recv_value(t, half)
                if t + 1 < chain - 1:
                    send_value(t + 1, half)

    half_tokens = PLANE * tok // 2

    def token_half(half):
        return pl.ds(half * half_tokens, half_tokens)

    def send_pull(half, up, change, mine, arrived, send, recv):
        mine[half] = dot(up, change[token_half(half), :], ((1,), (1,))).astype(BF16)
        for r in (7, 6, 5, 4, 3, 2, 1):
            remote(mine.at[half], arrived.at[half, r], send.at[half], recv.at[half], peer(r)).start()

    def pulls(half, arrived, send, recv):
        at = arrived.at[half, pl.ds(1, PLANE - 1)]
        return remote(at, at, send.at[half], recv.at[half], peer(1))

    own_columns = pl.ds(pl.multiple_of(h * piece, piece), piece)

    def down_gradient(mine, arrived, send, recv):
        total = jnp.zeros((ranks, piece), F32)
        for half in range(2):
            pulls(half, arrived, send, recv).wait_recv()
            pull = mine[half].astype(F32)
            for r in range(1, PLANE):
                pull = pull + arrived[half, r].astype(F32)
            total = total + dot(pull.astype(BF16), M[token_half(half), own_columns])
        return total.astype(BF16)

    def share(sums, sem):
        own = sums.at[z]
        for d in range(1, chain):
            remote(own, own, sem.at[0], sem.at[1], above((z + d) % chain)).start()

    def shares(sums, sem):
        at = sums.at[pl.ds(0, chain - 1)]
        return remote(at, at, sem.at[0], sem.at[1], peer(1))

    def shared(sums, sem):
        shares(sums, sem).wait_recv()
        total = sums[0].astype(F32)
        for d in range(1, chain):
            total = total + sums[d].astype(F32)
        return (total * coefficient).astype(BF16)

    def spread(total, mine, out, sem):
        mine[...] = total
        for r in (7, 6, 5, 4, 3, 2, 1):
            remote(mine, out.at[h], sem.at[2], sem.at[3], peer(r)).start()
        out[h] = total

    def spreads(out, sem):
        at = out.at[pl.ds(0, PLANE - 1)]
        return remote(at, at, sem.at[2], sem.at[3], peer(1))

    for half in range(2):
        send_pull(half, value_up(), DV, PV, RPV, v1_send, v1_recv)
    low_gradient = dot(LL[...], DV[...], ((0,), (0,)))
    RSV.at[z][:, piece:] = low_gradient[ranks:, :].astype(BF16)
    for half in range(2):
        add_value_piece(z, half)
    for t in range(chain - 2):
        for half in range(2):
            @pl.when(outer)
            def _():
                recv_value(t, half)

            add_value(t, half)
    RSV.at[z][:, 0:piece] = down_gradient(PV, RPV, v1_send, v1_recv)
    share(RSV, v_sem)
    for half in range(2):
        @pl.when(outer)
        def _():
            recv_value(chain - 2, half)

        add_value(chain - 2, half)

    for half in range(2):
        for i in range(half * tiles // 2, (half + 1) * tiles // 2):
            at = pl.ds(i * seq, seq)
            v = accv[at, :].astype(BF16)
            k = K[at, :]
            for n in range(heads):
                g = G[at, n * kcols:(n + 1) * kcols]
                dweight = dot(g, v, ((1,), (1,)))
                delta = jnp.sum(P[i * heads + n].astype(F32) * dweight, axis=-1, keepdims=True)
                dscore = (C[i * heads + n] * (dweight - delta)).astype(BF16)
                DQ[at, n * kcols:(n + 1) * kcols] = (dot(dscore, k) * QSCALE).astype(BF16)
        send_pull(half, query_up(), DQ, PQ, RPQ, q1_send, q1_recv)

    low_gradient = dot(LL[...], DQ[...], ((0,), (0,)))
    RSB[z] = low_gradient[0:ranks, :].astype(BF16)
    share(RSB, b_sem)
    spread(shared(RSV, v_sem), TV, OUTV, v_sem)
    RSA[z] = down_gradient(PQ, RPQ, q1_send, q1_recv)
    share(RSA, a_sem)
    spread(shared(RSB, b_sem), TB, OUTB, b_sem)
    spread(shared(RSA, a_sem), TA, OUTA, a_sem)
    results = ((OUTV, v_sem), (OUTB, b_sem), (OUTA, a_sem))
    for out, sem in results:
        spreads(out, sem).wait_recv()

    at = WA.at[pl.ds(0, 3 * rows)]
    remote(at, at, w_send.at[0], w_recv.at[1], peer(1)).wait_send()
    at = WV.at[pl.ds(0, 3 * rows)]
    remote(at, at, w_send.at[1], w_recv.at[0], peer(1)).wait_send()
    at = N.at[pl.ds(0, (PLANE - 1) * tok)]
    remote(at, at, t_send.at[0], t_recv.at[0], peer(1)).wait_send()
    g_all_copies.wait_send()
    s_all_copies.wait_send()
    for t in range(chain - 1):
        @pl.when(has_up(t))
        def _():
            at = WA.at[plane_rows(z - t)]
            remote(at, at, up_send.at[t], up_recv.at[t, 0], above(z + 1)).wait_send()
            at = WV.at[plane_rows(z - t)]
            remote(at, at, vup_send.at[t], vup_recv.at[t, 0], above(z + 1)).wait_send()

        @pl.when(has_down(t))
        def _():
            at = WA.at[plane_rows(z + t)]
            remote(at, at, down_send.at[t], down_recv.at[t, 0], above(z - 1)).wait_send()
            at = WV.at[plane_rows(z + t)]
            remote(at, at, vdown_send.at[t], vdown_recv.at[t, 0], above(z - 1)).wait_send()
    for half in range(2):
        pulls(half, RPV, v1_send, v1_recv).wait_send()
        pulls(half, RPQ, q1_send, q1_recv).wait_send()
    for sums, sem in ((RSV, v_sem), (RSB, b_sem), (RSA, a_sem)):
        shares(sums, sem).wait_send()
    for out, sem in results:
        spreads(out, sem).wait_send()


def unpack_kernel(outa, outb, outv, out_aq, out_bq, out_av, out_bv):
    feats = out_aq.shape[1]
    piece = feats // PLANE
    qcols = out_bq.shape[1] // PLANE
    kcols = out_bv.shape[1] // PLANE
    for h in range(PLANE):
        out_aq[:, h * piece:(h + 1) * piece] = outa[h].astype(F32)
        out_bq[:, h * qcols:(h + 1) * qcols] = outb[h].astype(F32)
        value = outv[h].astype(F32)
        out_av[:, h * piece:(h + 1) * piece] = value[:, 0:piece]
        out_bv[:, h * kcols:(h + 1) * kcols] = value[:, piece:]


def on_plane(
    tokens,
    trace_index,
    input_norm_scale,
    query_weight,
    key_weight,
    value_weight,
    query_down_weight,
    query_up_weight,
    value_down_weight,
    value_up_weight,
    output_gradient,
):
    tok = tokens.shape[1]
    feats = tokens.shape[2]
    fsdp = lax.axis_size("fsdp")
    chain = fsdp // 4
    ranks = query_down_weight.shape[1]
    qcols = query_weight.shape[1] // PLANE
    kcols = key_weight.shape[1] // PLANE
    piece = feats // PLANE
    many = PLANE * tok
    token_total = lax.axis_size("ctx") * fsdp * tok
    coefficient = ADAPTER_NAME / math.sqrt(token_total)
    hbm = pl.BlockSpec(memory_space=pltpu.HBM)
    vmem = pl.BlockSpec(memory_space=pltpu.VMEM)
    dma = pltpu.SemaphoreType.DMA
    steps = chain - 1
    tiles = many // (2 * tok)
    heads = qcols // kcols
    outa, outb, outv = pl.pallas_call(
        functools.partial(plane_kernel, chain, coefficient),
        out_shape=(
            pltpu.VMEM((PLANE, ranks, piece), BF16),
            pltpu.VMEM((PLANE, ranks, qcols), BF16),
            pltpu.VMEM((PLANE, ranks, piece + kcols), BF16),
        ),
        in_specs=[hbm] * 11,
        out_specs=(vmem, vmem, vmem),
        scratch_shapes=[
            pltpu.VMEM((many, feats), BF16),
            pltpu.VMEM((many, feats), BF16),
            pltpu.VMEM((feats, qcols + kcols), BF16),
            pltpu.VMEM((feats, kcols), BF16),
            pltpu.VMEM((many, qcols), BF16),
            pltpu.VMEM((PLANE, 1, tok), jnp.int32),
            pltpu.VMEM((many, qcols + kcols), F32),
            pltpu.VMEM((many, kcols), F32),
            pltpu.VMEM((tiles * heads, 2 * tok, 2 * tok), BF16),
            pltpu.VMEM((tiles * heads, 2 * tok, 2 * tok), F32),
            pltpu.VMEM((many, kcols), BF16),
            pltpu.VMEM((many, qcols), BF16),
            pltpu.VMEM((many, kcols), BF16),
            pltpu.VMEM((many, 2 * ranks), BF16),
            pltpu.VMEM((feats,), BF16),
            pltpu.VMEM((2 * ranks, feats), BF16),
            pltpu.VMEM((ranks, query_weight.shape[1]), BF16),
            pltpu.VMEM((ranks, value_weight.shape[1]), BF16),
            pltpu.VMEM((2, ranks, many // 2), BF16),
            pltpu.VMEM((2, PLANE, ranks, many // 2), BF16),
            pltpu.VMEM((2, ranks, many // 2), BF16),
            pltpu.VMEM((2, PLANE, ranks, many // 2), BF16),
            pltpu.VMEM((chain, ranks, piece), BF16),
            pltpu.VMEM((chain, ranks, qcols), BF16),
            pltpu.VMEM((chain, ranks, piece + kcols), BF16),
            pltpu.VMEM((ranks, piece), BF16),
            pltpu.VMEM((ranks, qcols), BF16),
            pltpu.VMEM((ranks, piece + kcols), BF16),
            dma((11,)),
            dma((2,)), dma((4,)), dma((1,)), dma((11,)), dma((2,)), dma((2,)),
            dma((steps,)), dma((steps, 2)), dma((steps,)), dma((steps, 2)),
            dma((steps,)), dma((steps, 2)), dma((steps,)), dma((steps, 2)),
            dma((2,)), dma((2,)), dma((2,)), dma((2,)), dma((4,)), dma((4,)), dma((4,)),
        ],
        compiler_params=pltpu.CompilerParams(
            collective_id=0, has_side_effects=True, vmem_limit_bytes=56 * 1024 * 1024
        ),
    )(
        tokens.reshape(tok, feats), trace_index, input_norm_scale,
        query_weight, key_weight, value_weight,
        query_down_weight.T, query_up_weight, value_down_weight.T, value_up_weight,
        output_gradient.reshape(tok, output_gradient.shape[2]),
    )
    aq, bq, av, bv = pl.pallas_call(
        unpack_kernel,
        out_shape=(
            jax.ShapeDtypeStruct((ranks, feats), F32),
            jax.ShapeDtypeStruct((ranks, query_weight.shape[1]), F32),
            jax.ShapeDtypeStruct((ranks, feats), F32),
            jax.ShapeDtypeStruct((ranks, value_weight.shape[1]), F32),
        ),
        in_specs=[vmem, vmem, vmem],
        out_specs=(vmem, vmem, vmem, vmem),
        compiler_params=pltpu.CompilerParams(vmem_limit_bytes=16 * 1024 * 1024),
    )(outa, outb, outv)
    return (aq.T, bq, av.T, bv)


def solution(mesh):
    shape = mesh.shape
    planes = shape["groups"] == 1 and shape["ctx"] == 2 and shape["fsdp"] % 4 == 0 and shape["fsdp"] > 8
    return jax.shard_map(
        on_plane if planes else on_device,
        mesh=mesh,
        in_specs=(
            P(("groups", "fsdp"), "ctx", None),
            P(("groups", "fsdp"), "ctx"),
            P(),
            P("fsdp", None),
            P("fsdp", None),
            P("fsdp", None),
            P(),
            P(),
            P(),
            P(),
            P(("groups", "fsdp"), "ctx", None),
        ),
        out_specs=(P("groups", None), P("groups", None), P("groups", None), P("groups", None)),
        check_vma=False,
    )
```

```python
import functools
import math

import jax
import jax.numpy as jnp
from jax import lax
from jax.experimental import pallas as pl
from jax.experimental.pallas import tpu as pltpu
from jax.sharding import PartitionSpec as P

HEAD_SIZE = 128


CAP = 50.0
QSCALE = 1.0 / 12.0
ADAPTER_NAME = 0.5
EPS = 1e-06


def shifted(value, axis, by):
    devices = lax.axis_size(axis)
    pairs = [(i, i + by) for i in range(devices) if 0 <= i + by < devices]
    return lax.ppermute(value, axis, pairs)


def normed_rows(values, gain):
    flt = values.astype(jnp.float32)
    meansq = jnp.mean(flt * flt, axis=-1, keepdims=True)
    return (flt * lax.rsqrt(meansq + EPS) * gain.astype(jnp.float32)).astype(jnp.bfloat16)


def add_rows(left, piece):
    return jnp.dot(left, piece, preferred_element_type=jnp.float32)


def attend_head(operands, mask):
    q_head, k_head, v_head, g_head = operands
    s = jnp.einsum("igd,jd->gij", q_head, k_head, preferred_element_type=jnp.float32) * QSCALE
    t = jnp.tanh(s / CAP)
    capped = CAP * t
    expo = jnp.where(mask[None], jnp.exp(capped), jnp.float32(0.0))
    weights = expo / jnp.sum(expo, axis=-1, keepdims=True)
    weights16 = weights.astype(jnp.bfloat16)
    attended = jnp.einsum("gij,jd->igd", weights16, v_head, preferred_element_type=jnp.float32)
    dweight = jnp.einsum("igd,jd->gij", g_head, v_head, preferred_element_type=jnp.float32)
    delta = jnp.sum(g_head.astype(jnp.float32) * attended, axis=-1).T
    dscore = (weights * (dweight - delta[..., None]) * (1.0 - t * t) * QSCALE).astype(jnp.bfloat16)
    query_gradient = jnp.einsum(
        "gij,jd->igd", dscore, k_head, preferred_element_type=jnp.float32
    ).astype(jnp.bfloat16)
    value_gradient = jnp.einsum(
        "gij,igd->jd", weights16, g_head, preferred_element_type=jnp.float32
    )
    return (query_gradient, value_gradient)


def partial_attend(mask):

    def run_head(operands):
        return attend_head(operands, mask)

    return run_head


def on_device(
    tokens,
    trace_index,
    input_norm_scale,
    query_weight,
    key_weight,
    value_weight,
    query_down_weight,
    query_up_weight,
    value_down_weight,
    value_up_weight,
    output_gradient,
):
    window_width = tokens.shape[1]
    feats = tokens.shape[2]
    heads_kv = key_weight.shape[1] // HEAD_SIZE
    heads_q = query_weight.shape[1] // HEAD_SIZE
    head_group = heads_q // heads_kv
    normalized_input = normed_rows(tokens.reshape(window_width, feats), input_norm_scale)
    seg_own = trace_index.reshape(window_width).astype(jnp.bfloat16)
    seg_parts = []

    def add_keyval(piece):
        return add_rows(normalized_input, piece)

    query_frozen = add_rows(
        normalized_input, lax.all_gather(query_weight, "fsdp", axis=0, tiled=True)
    )
    k_base = add_keyval(lax.all_gather(key_weight, "fsdp", axis=0, tiled=True))
    value_frozen = add_keyval(lax.all_gather(value_weight, "fsdp", axis=0, tiled=True))
    query_reduced = jnp.dot(
        normalized_input, query_down_weight, preferred_element_type=jnp.float32
    ).astype(jnp.bfloat16)
    reduced_rows = jnp.dot(
        normalized_input, value_down_weight, preferred_element_type=jnp.float32
    ).astype(jnp.bfloat16)
    query_matrix = (
        query_frozen
        + ADAPTER_NAME * jnp.dot(query_reduced, query_up_weight, preferred_element_type=jnp.float32)
    ).astype(jnp.bfloat16)
    key_rows = k_base.astype(jnp.bfloat16)
    value_rows = (
        value_frozen
        + ADAPTER_NAME * jnp.dot(reduced_rows, value_up_weight, preferred_element_type=jnp.float32)
    ).astype(jnp.bfloat16)
    key_parts = []
    value_parts = []
    for distance in (2, 1):
        key_prev, value_prev, seg_prev = shifted((key_rows, value_rows, seg_own), "ctx", distance)
        key_parts.append(key_prev)
        value_parts.append(value_prev)
        seg_parts.append(seg_prev)
    keys_all = jnp.concatenate(key_parts + [key_rows], 0)
    values_all = jnp.concatenate(value_parts + [value_rows], 0)
    seg_keys = jnp.concatenate(seg_parts + [seg_own], 0)
    pos_q = jnp.arange(window_width, dtype=jnp.int32)[:, None]
    pos_k = jnp.arange(3 * window_width, dtype=jnp.int32)[None, :]
    position = lax.axis_index("ctx")
    mask = (
        (pos_k > pos_q)
        & (pos_k <= pos_q + 2 * window_width)
        & (seg_keys[None, :] == seg_own[:, None])
    )
    mask = mask & (
        (pos_k >= 2 * window_width) | (pos_k >= window_width) & (position >= 1) | (position >= 2)
    )
    q_heads = jnp.moveaxis(
        query_matrix.reshape(window_width, heads_kv, head_group, HEAD_SIZE), 1, 0
    )
    g_heads = jnp.moveaxis(
        output_gradient.reshape(window_width, heads_kv, head_group, HEAD_SIZE), 1, 0
    )
    k_heads = jnp.moveaxis(keys_all.reshape(3 * window_width, heads_kv, HEAD_SIZE), 1, 0)
    v_heads = jnp.moveaxis(values_all.reshape(3 * window_width, heads_kv, HEAD_SIZE), 1, 0)
    dquery_heads, dvalue_heads = lax.map(partial_attend(mask), (q_heads, k_heads, v_heads, g_heads))
    query_gradient = jnp.moveaxis(dquery_heads, 0, 1).reshape(window_width, heads_q * HEAD_SIZE)
    dvalue_triple = jnp.moveaxis(dvalue_heads, 0, 1).reshape(3 * window_width, heads_kv * HEAD_SIZE)
    value_gradient = dvalue_triple[2 * window_width :]
    for distance in (1, 2):
        begin = (2 - distance) * window_width
        value_gradient = value_gradient + shifted(
            dvalue_triple[begin : begin + window_width], "ctx", -distance
        )
    query_backward = jnp.dot(
        query_gradient, query_up_weight.T, preferred_element_type=jnp.float32
    ).astype(jnp.bfloat16)
    value_backward = jnp.dot(
        value_gradient, value_up_weight.astype(jnp.float32).T, precision=lax.Precision.HIGHEST
    )
    part_aq = jnp.dot(normalized_input.T, query_backward, preferred_element_type=jnp.float32)
    part_bq = jnp.dot(query_reduced.T, query_gradient, preferred_element_type=jnp.float32)
    part_av = jnp.dot(
        normalized_input.astype(jnp.float32).T, value_backward, precision=lax.Precision.HIGHEST
    )
    part_bv = jnp.dot(
        reduced_rows.astype(jnp.float32).T, value_gradient, precision=lax.Precision.HIGHEST
    )
    sum_aq, sum_bq, sum_av, sum_bv = lax.psum((part_aq, part_bq, part_av, part_bv), ("ctx", "fsdp"))
    token_total = lax.axis_size("ctx") * lax.axis_size("fsdp") * window_width
    coefficient = ADAPTER_NAME / math.sqrt(token_total)
    return (sum_aq * coefficient, sum_bq * coefficient, sum_av * coefficient, sum_bv * coefficient)


F32 = jnp.float32
BF16 = jnp.bfloat16
PLANE = 8


def dot(a, b, dims=((1,), (0,))):
    return lax.dot_general(a, b, (dims, ((), ())), preferred_element_type=F32)


def plane_kernel(
    chain, coefficient,
    raw, seg, gain_in, wq, wk, wv, qd, qu_in, vd, vu_in, grad,
    OUTA, OUTB, OUTV,
    N, M, WA, WV, G, SG, acc, accv, P, C, K, DQ, DV, LL,
    gain, down, qu, vu,
    PQ, PV, RSA, RSB, RSV, TA, TB, TV,
    local_sem, w_send, w_recv, t_send, t_recv, g_sem, s_sem,
    up_send, up_recv, down_send, down_recv, vup_send, vup_recv, vdown_send, vdown_recv,
    q1_send, q1_recv, v1_send, v1_recv, a_sem, b_sem, v_sem,
):
    x = lax.axis_index("ctx")
    f = lax.axis_index("fsdp")
    z = f // 4
    y = (f // 2) % 2
    c = f % 2
    tok, feats = raw.shape
    rows = wq.shape[0]
    qcols = wq.shape[1] // PLANE
    kcols = wk.shape[1] // PLANE
    acols = qcols + kcols
    piece = feats // PLANE
    seq = 2 * tok
    sub = tok // 4
    heads = qcols // kcols
    ranks = qd.shape[0]
    middle = (z > 0) & (z < chain - 1)
    outer = (z == 0) | (z == chain - 1)

    def coords(r):
        px = 1 - x if r & 4 else x
        py = 1 - y if r & 2 else y
        pc = 1 - c if r & 1 else c
        return px, py, pc

    def head_of(r):
        px, py, pc = coords(r)
        return (px * 2 + py) * 2 + pc

    def peer(r):
        px, py, pc = coords(r)
        return {"ctx": px, "fsdp": (z * 2 + py) * 2 + pc}

    def above(pz):
        return {"ctx": x, "fsdp": (pz * 2 + y) * 2 + c}

    def tok_slot(r):
        px, py, pc = coords(r)
        return (py * 2 + pc) * 2 + px

    def tok_piece(r, low, count):
        begin = tok_slot(r) * tok + low * sub
        return pl.ds(pl.multiple_of(begin, sub), count * sub)

    def tok_rows(r):
        return pl.ds(pl.multiple_of(tok_slot(r) * tok, tok), tok)

    def remote(src, dst, send, recv, device):
        return pltpu.make_async_remote_copy(
            src_ref=src, dst_ref=dst, send_sem=send, recv_sem=recv,
            device_id=device, device_id_type=pl.DeviceIdType.MESH,
        )

    barrier = pltpu.get_barrier_semaphore()
    for r in range(1, PLANE):
        pl.semaphore_signal(barrier, inc=1, device_id=peer(r), device_id_type=pl.DeviceIdType.MESH)
    for d in range(1, chain):
        pl.semaphore_signal(
            barrier, inc=1, device_id=above((z + d) % chain), device_id_type=pl.DeviceIdType.MESH
        )

    def w_rows(r):
        px, py, pc = coords(r)
        return pl.ds(pl.multiple_of(((z * 2 + py) * 2 + pc) * rows, rows), rows)

    def w_parts(r):
        h = head_of(r)
        own = w_rows(0)
        return (
            (wq.at[:, pl.ds(pl.multiple_of(h * qcols, qcols), qcols)], WA.at[own, pl.ds(0, qcols)]),
            (wk.at[:, pl.ds(pl.multiple_of(h * kcols, kcols), kcols)], WA.at[own, pl.ds(qcols, kcols)]),
            (wv.at[:, pl.ds(pl.multiple_of(h * kcols, kcols), kcols)], WV.at[own]),
        )

    def g_cols(r):
        h = head_of(r)
        return grad.at[:, pl.ds(pl.multiple_of(h * qcols, qcols), qcols)]

    local = [pltpu.make_async_copy(a, b, local_sem.at[i]) for i, (a, b) in enumerate(w_parts(0))]
    local.append(pltpu.make_async_copy(raw, N.at[tok_rows(0)], local_sem.at[3]))
    local.append(pltpu.make_async_copy(g_cols(0), G.at[tok_rows(0)], local_sem.at[4]))
    local.append(pltpu.make_async_copy(seg, SG.at[tok_slot(0)], local_sem.at[5]))
    local.append(pltpu.make_async_copy(qd, down.at[pl.ds(0, ranks)], local_sem.at[6]))
    local.append(pltpu.make_async_copy(vd, down.at[pl.ds(ranks, ranks)], local_sem.at[7]))
    local.append(pltpu.make_async_copy(qu_in, qu, local_sem.at[8]))
    local.append(pltpu.make_async_copy(vu_in, vu, local_sem.at[9]))
    local.append(pltpu.make_async_copy(gain_in, gain, local_sem.at[10]))
    for copy in local:
        copy.start()
    for i in range(2):
        local[i].wait()
    pl.semaphore_wait(barrier, PLANE - 1 + chain - 1)

    def half_rows(plane, half):
        py = y if half == 0 else 1 - y
        return pl.ds(pl.multiple_of((plane * 4 + py * 2) * rows, 2 * rows), 2 * rows)

    def quarter_rows(plane, quarter):
        px, py, pc = coords(quarter)
        return pl.ds(pl.multiple_of((plane * 4 + py * 2 + pc) * rows, rows), rows)

    def has_up(t):
        return (z < chain - 1) & (z - t >= 0)

    def has_down(t):
        return (z > 0) & (z + t <= chain - 1)

    def from_below(t):
        return z - 1 - t >= 0

    def from_above(t):
        return z + 1 + t <= chain - 1

    def pieces_of(t):
        return range(4) if t == 0 else range(2)

    def piece_rows(plane, t, i):
        return quarter_rows(plane, i) if t == 0 else half_rows(plane, i)

    def half_of(t, i):
        return i // 2 if t == 0 else i

    def plane_rows(plane):
        return pl.ds(pl.multiple_of(plane * 4 * rows, 4 * rows), 4 * rows)

    def up_copy(t, i):
        at = WA.at[piece_rows(z - t, t, i)]
        return remote(at, at, up_send.at[t], up_recv.at[t, half_of(t, i)], above(z + 1))

    def down_copy(t, i):
        at = WA.at[piece_rows(z + t, t, i)]
        return remote(at, at, down_send.at[t], down_recv.at[t, half_of(t, i)], above(z - 1))

    def up_arrival(t, half):
        at = WA.at[half_rows(z - 1 - t, half)]
        return remote(at, at, up_send.at[t], up_recv.at[t, half], above(z - 1))

    def down_arrival(t, half):
        at = WA.at[half_rows(z + 1 + t, half)]
        return remote(at, at, down_send.at[t], down_recv.at[t, half], above(z + 1))

    def vup_copy(t, half):
        at = WV.at[half_rows(z - t, half)]
        return remote(at, at, vup_send.at[t], vup_recv.at[t, half], above(z + 1))

    def vdown_copy(t, half):
        at = WV.at[half_rows(z + t, half)]
        return remote(at, at, vdown_send.at[t], vdown_recv.at[t, half], above(z - 1))

    def vup_arrival(t, half):
        at = WV.at[half_rows(z - 1 - t, half)]
        return remote(at, at, vup_send.at[t], vup_recv.at[t, half], above(z - 1))

    def vdown_arrival(t, half):
        at = WV.at[half_rows(z + 1 + t, half)]
        return remote(at, at, vdown_send.at[t], vdown_recv.at[t, half], above(z + 1))

    def send_chain(t, i):
        @pl.when(has_up(t))
        def _():
            up_copy(t, i).start()

        @pl.when(has_down(t))
        def _():
            down_copy(t, i).start()

    def recv_half(t, half):
        @pl.when(from_below(t))
        def _():
            up_arrival(t, half).wait_recv()

        @pl.when(from_above(t))
        def _():
            down_arrival(t, half).wait_recv()

    def send_value_first(k):
        @pl.when(has_up(k - 1) & jnp.logical_not(has_up(k)))
        def _():
            for half in range(2):
                vup_copy(0, half).start()

        @pl.when(has_down(k - 1) & jnp.logical_not(has_down(k)))
        def _():
            for half in range(2):
                vdown_copy(0, half).start()

    def send_value(t, half):
        @pl.when(has_up(t))
        def _():
            vup_copy(t, half).start()

        @pl.when(has_down(t))
        def _():
            vdown_copy(t, half).start()

    def recv_value(t, half):
        @pl.when(from_below(t))
        def _():
            vup_arrival(t, half).wait_recv()

        @pl.when(from_above(t))
        def _():
            vdown_arrival(t, half).wait_recv()

    w_copies = {}
    for r in (1, 2, 3):
        w_copies[r] = [
            remote(a, b, w_send.at[i // 2], w_recv.at[r if i < 2 else 0], peer(r))
            for i, (a, b) in enumerate(w_parts(r))
        ]
    for r in (1, 2, 3):
        for i in range(2):
            w_copies[r][i].start()
    send_chain(0, 0)
    for r in (1, 2, 3):
        w_copies[r][2].start()

    t_slot = {(1, 0): 0, (4, 3): 1, (4, 0): 2, (5, 0): 3, (3, 0): 4, (7, 0): 5}
    for low in range(4):
        t_slot[2, low] = 6 + low
        t_slot[6, low] = 10

    def send_token(r_mine, r_there, hop, low=0, count=4):
        at = N.at[tok_piece(r_mine, low, count)]
        source = raw.at[pl.ds(low * sub, count * sub)] if r_mine == 0 else at
        remote(source, at, t_send.at[0], t_recv.at[t_slot[r_there, low]], peer(hop)).start()

    def wait_token(r, low=0, count=4):
        at = N.at[tok_piece(r, low, count)]
        remote(at, at, t_send.at[0], t_recv.at[t_slot[r, low]], peer(1)).wait_recv()

    send_token(0, 1, 1)
    send_token(0, 4, 4, 3, 1)
    send_token(0, 4, 4, 0, 3)
    for low in range(4):
        send_token(0, 2, 2, low, 1)
    g_copies = {}
    s_copies = {}
    for r in range(1, PLANE):
        g_copies[r] = remote(g_cols(r), G.at[tok_rows(0)], g_sem.at[0], g_sem.at[1], peer(r))
        s_copies[r] = remote(seg, SG.at[tok_slot(0)], s_sem.at[0], s_sem.at[1], peer(r))

    def wait_weight(r):
        ref = WA.at[w_rows(r)]
        remote(ref, ref, w_send.at[0], w_recv.at[r], peer(r)).wait_recv()

    def wait_values():
        ref = WV.at[pl.ds(0, 3 * rows)]
        remote(ref, ref, w_send.at[1], w_recv.at[0], peer(1)).wait_recv()

    part_rows = 4 * tok

    def part_at(part, i, height):
        py = y if part == 0 else 1 - y
        return pl.ds(pl.multiple_of(py * part_rows + i * height, height), height)

    h = head_of(0)

    def query_up():
        return qu[:, pl.ds(pl.multiple_of(h * qcols, qcols), qcols)]

    def value_up():
        return vu[:, pl.ds(pl.multiple_of(h * kcols, kcols), kcols)]

    def prepare(r):
        height = tok // 2

        @pl.loop(0, 2)
        def _(i):
            begin = tok_slot(r) * tok + i * height
            at = pl.ds(pl.multiple_of(begin, height), height)
            flt = N[at, :].astype(F32)
            meansq = jnp.sum(flt * flt, axis=-1, keepdims=True) / feats
            M[at, :] = (flt * lax.rsqrt(meansq + EPS) * gain[...].astype(F32).reshape(1, feats)).astype(BF16)

        at = tok_rows(r)
        block = M[at, :]
        low = dot(block, down[...], ((1,), (1,))).astype(BF16)
        LL[at, :] = low
        filler = jnp.zeros((ranks, qcols), BF16)
        acc[at, 0:qcols] = ADAPTER_NAME * dot(low, jnp.concatenate([query_up(), filler], axis=0))
        acc[at, qcols:] = jnp.zeros((tok, kcols), F32)
        accv[at, :] = ADAPTER_NAME * dot(low, jnp.concatenate([filler[:, 0:kcols], value_up()], axis=0))

    def add_piece(plane, half, part):
        chosen = half_rows(plane, half)

        @pl.loop(0, part_rows // seq)
        def _(i):
            at = part_at(part, i, seq)
            acc[at, :] = acc[at, :] + dot(M[at, chosen], WA[chosen, :])

    def add_near(part):
        low = jnp.maximum(z - 2, 0)
        high = jnp.minimum(z + 2, chain - 1)
        for count in range(3, min(chain, 5) + 1):
            @pl.when(high - low == count - 1)
            def _():
                chosen = pl.ds(pl.multiple_of(low * 4 * rows, 4 * rows), count * 4 * rows)

                @pl.loop(0, part_rows // seq)
                def _(i):
                    at = part_at(part, i, seq)
                    acc[at, :] = acc[at, :] + dot(M[at, chosen], WA[chosen, :])

    def add_step(t, half, part):
        @pl.when(from_below(t))
        def _():
            add_piece(z - 1 - t, half, part)

        @pl.when(from_above(t))
        def _():
            add_piece(z + 1 + t, half, part)

    def add_value_piece(plane, half):
        chosen = plane_rows(plane) if half is None else half_rows(plane, half)

        @pl.loop(0, 2 * part_rows // seq)
        def _(i):
            at = pl.ds(pl.multiple_of(i * seq, seq), seq)
            accv[at, :] = accv[at, :] + dot(M[at, chosen], WV[chosen, :])

    def add_value(t, half):
        @pl.when(from_below(t))
        def _():
            add_value_piece(z - 1 - t, half)

        @pl.when(from_above(t))
        def _():
            add_value_piece(z + 1 + t, half)

    wait_weight(1)
    send_chain(0, 1)
    for r in range(1, PLANE):
        s_copies[r].start()
    local[3].wait()
    for i in range(6, 11):
        local[i].wait()
    prepare(0)
    wait_token(1)
    prepare(1)
    wait_weight(2)
    send_chain(0, 2)
    wait_weight(3)
    send_chain(0, 3)
    recv_half(0, 0)
    send_chain(1, 0)
    wait_token(2, 0, 1)
    send_token(2, 6, 4, 0, 1)
    recv_half(0, 1)
    send_chain(1, 1)
    local[2].wait()
    wait_values()
    send_value_first(1)
    wait_token(2, 1, 1)
    send_token(2, 6, 4, 1, 1)
    wait_token(4, 3, 1)
    send_token(4, 6, 2, 3, 1)
    wait_token(4, 0, 3)
    send_token(4, 5, 1)
    prepare(4)
    wait_token(2, 2, 1)
    send_token(2, 6, 4, 2, 1)
    for r in (6, 7, 4, 5, 2, 3, 1):
        g_copies[r].start()
    wait_token(5)
    prepare(5)
    recv_half(1, 0)
    send_chain(2, 0)
    wait_token(2, 3, 1)
    send_token(2, 3, 1)
    prepare(2)
    wait_token(3)
    prepare(3)
    recv_half(1, 1)
    send_chain(2, 1)
    for k in range(2, chain):
        send_value_first(k)
    add_near(0)
    wait_token(6)
    send_token(6, 7, 1)
    prepare(6)
    wait_token(7)
    prepare(7)

    @pl.when(middle)
    def _():
        for half in range(2):
            recv_value(0, half)
            send_value(1, half)

    add_near(1)
    for t in range(2, chain - 1):
        for half in range(2):
            recv_half(t, half)
            if t + 1 < chain - 1:
                send_chain(t + 1, half)
            for part in range(2):
                add_step(t, half, part)

    tiles = PLANE * tok // seq
    local[4].wait()
    local[5].wait()
    g_others = G.at[pl.ds(0, (PLANE - 1) * tok)]
    g_all_copies = remote(g_others, g_others, g_sem.at[0], g_sem.at[1], peer(1))
    g_all_copies.wait_recv()
    s_others = SG.at[pl.ds(0, PLANE - 1)]
    s_all_copies = remote(s_others, s_others, s_sem.at[0], s_sem.at[1], peer(1))
    s_all_copies.wait_recv()

    pos_i = lax.broadcasted_iota(jnp.int32, (seq, seq), 0)
    pos_j = lax.broadcasted_iota(jnp.int32, (seq, seq), 1)
    band = (pos_j <= pos_i) & (pos_j > pos_i - 2 * tok)

    @pl.loop(0, tiles, unroll=2)
    def _(i):
        at = pl.ds(pl.multiple_of(i * seq, seq), seq)
        q_all = acc[at, 0:qcols].astype(BF16)
        k = acc[at, qcols:].astype(BF16)
        K[at, :] = k
        g_all = G[at, :]
        traces = [SG[2 * i].astype(F32), SG[2 * i + 1].astype(F32)]
        along = jnp.concatenate(traces, axis=1)
        turned = [jnp.broadcast_to(own, (tok, tok)).T for own in traces]
        across = jnp.concatenate([jnp.concatenate([own, own], axis=1) for own in turned], axis=0)
        mask = band & (across == along)
        dv = jnp.zeros((seq, kcols), F32)
        for n in range(heads):
            q = q_all[:, n * kcols:(n + 1) * kcols]
            g = g_all[:, n * kcols:(n + 1) * kcols]
            t = jnp.tanh(dot(q, k, ((1,), (1,))) * (QSCALE / CAP))
            expo = jnp.where(mask, jnp.exp(CAP * t), 0.0)
            weights = expo * (1.0 / jnp.sum(expo, axis=-1, keepdims=True))
            weights16 = weights.astype(BF16)
            P[i * heads + n] = weights16
            C[i * heads + n] = weights * (1.0 - t * t)
            dv = dv + dot(weights16, g, ((0,), (0,)))
        DV[at, :] = dv.astype(BF16)

    @pl.when(middle)
    def _():
        for t in range(1, chain - 1):
            for half in range(2):
                recv_value(t, half)
                if t + 1 < chain - 1:
                    send_value(t + 1, half)

    half_tokens = PLANE * tok // 2

    def token_half(half):
        return pl.ds(half * half_tokens, half_tokens)

    def send_pull(half, up, change, gathered, send, recv):
        own = gathered.at[half, h]
        own[...] = dot(up, change[token_half(half), :], ((1,), (1,))).astype(BF16)
        for r in (7, 6, 5, 4, 3, 2, 1):
            remote(own, own, send.at[half], recv.at[half], peer(r)).start()

    def pulls(half, gathered, send, recv):
        at = gathered.at[half, pl.ds(0, PLANE - 1)]
        return remote(at, at, send.at[half], recv.at[half], peer(1))

    def down_gradient(columns, width, gathered, send, recv):
        total = jnp.zeros((ranks, width), F32)
        for half in range(2):
            pulls(half, gathered, send, recv).wait_recv()
            pull = gathered[half, 0].astype(F32)
            for r in range(1, PLANE):
                pull = pull + gathered[half, r].astype(F32)
            total = total + dot(pull.astype(BF16), M[token_half(half), columns])
        return total.astype(BF16)

    def share(sums, sem):
        own = sums.at[z]
        for d in range(1, chain):
            remote(own, own, sem.at[0], sem.at[1], above((z + d) % chain)).start()

    def shares(sums, sem):
        at = sums.at[pl.ds(0, chain - 1)]
        return remote(at, at, sem.at[0], sem.at[1], peer(1))

    def shared(sums, sem):
        shares(sums, sem).wait_recv()
        total = sums[0].astype(F32)
        for d in range(1, chain):
            total = total + sums[d].astype(F32)
        return (total * coefficient).astype(BF16)

    def spread(total, mine, out, sem):
        mine[...] = total
        for r in (7, 6, 5, 4, 3, 2, 1):
            remote(mine, out.at[h], sem.at[2], sem.at[3], peer(r)).start()
        out[h] = total

    def spreads(out, sem):
        at = out.at[pl.ds(0, PLANE - 1)]
        return remote(at, at, sem.at[2], sem.at[3], peer(1))

    for half in range(2):
        send_pull(half, value_up(), DV, PV, v1_send, v1_recv)
    low_gradient = dot(LL[...], DV[...], ((0,), (0,)))
    RSV.at[z][:, piece:] = low_gradient[ranks:, :].astype(BF16)
    add_value_piece(z, None)
    for t in range(chain - 2):
        @pl.when(outer)
        def _():
            for half in range(2):
                recv_value(t, half)

        add_value(t, None)
    own_columns = pl.ds(pl.multiple_of(h * piece, piece), piece)
    RSV.at[z][:, 0:piece] = down_gradient(own_columns, piece, PV, v1_send, v1_recv)
    share(RSV, v_sem)
    for half in range(2):
        @pl.when(outer)
        def _():
            recv_value(chain - 2, half)

        add_value(chain - 2, half)

    for half in range(2):
        for i in range(half * tiles // 2, (half + 1) * tiles // 2):
            at = pl.ds(i * seq, seq)
            v = accv[at, :].astype(BF16)
            k = K[at, :]
            for n in range(heads):
                g = G[at, n * kcols:(n + 1) * kcols]
                dweight = dot(g, v, ((1,), (1,)))
                delta = jnp.sum(P[i * heads + n].astype(F32) * dweight, axis=-1, keepdims=True)
                dscore = (C[i * heads + n] * (dweight - delta)).astype(BF16)
                DQ[at, n * kcols:(n + 1) * kcols] = (dot(dscore, k) * QSCALE).astype(BF16)
        send_pull(half, query_up(), DQ, PQ, q1_send, q1_recv)

    low_gradient = dot(LL[...], DQ[...], ((0,), (0,)))
    RSB[z] = low_gradient[0:ranks, :].astype(BF16)
    share(RSB, b_sem)
    spread(shared(RSV, v_sem), TV, OUTV, v_sem)
    width = feats // 2
    core_columns = pl.ds(pl.multiple_of(c * width, width), width)
    RSA[z] = down_gradient(core_columns, width, PQ, q1_send, q1_recv)
    share(RSA, a_sem)
    spread(shared(RSB, b_sem), TB, OUTB, b_sem)
    TA[...] = shared(RSA, a_sem)
    core_copy = remote(TA, OUTA.at[c], a_sem.at[2], a_sem.at[3], peer(1))
    core_copy.start()
    OUTA[c] = TA[...]
    results = ((OUTV, v_sem), (OUTB, b_sem))
    for out, sem in results:
        spreads(out, sem).wait_recv()
    at = OUTA.at[1 - c]
    remote(at, at, a_sem.at[2], a_sem.at[3], peer(1)).wait_recv()

    at = WA.at[pl.ds(0, 3 * rows)]
    remote(at, at, w_send.at[0], w_recv.at[1], peer(1)).wait_send()
    at = WV.at[pl.ds(0, 3 * rows)]
    remote(at, at, w_send.at[1], w_recv.at[0], peer(1)).wait_send()
    at = N.at[pl.ds(0, (PLANE - 1) * tok)]
    remote(at, at, t_send.at[0], t_recv.at[0], peer(1)).wait_send()
    g_all_copies.wait_send()
    s_all_copies.wait_send()
    for t in range(chain - 1):
        @pl.when(has_up(t))
        def _():
            at = WA.at[plane_rows(z - t)]
            remote(at, at, up_send.at[t], up_recv.at[t, 0], above(z + 1)).wait_send()
            at = WV.at[plane_rows(z - t)]
            remote(at, at, vup_send.at[t], vup_recv.at[t, 0], above(z + 1)).wait_send()

        @pl.when(has_down(t))
        def _():
            at = WA.at[plane_rows(z + t)]
            remote(at, at, down_send.at[t], down_recv.at[t, 0], above(z - 1)).wait_send()
            at = WV.at[plane_rows(z + t)]
            remote(at, at, vdown_send.at[t], vdown_recv.at[t, 0], above(z - 1)).wait_send()
    for half in range(2):
        pulls(half, PV, v1_send, v1_recv).wait_send()
        pulls(half, PQ, q1_send, q1_recv).wait_send()
    for sums, sem in ((RSV, v_sem), (RSB, b_sem), (RSA, a_sem)):
        shares(sums, sem).wait_send()
    for out, sem in results:
        spreads(out, sem).wait_send()
    core_copy.wait_send()


def unpack_kernel(outa, outb, outv, out_aq, out_bq, out_av, out_bv):
    feats = out_aq.shape[1]
    piece = feats // PLANE
    qcols = out_bq.shape[1] // PLANE
    kcols = out_bv.shape[1] // PLANE
    for core in range(2):
        out_aq[:, core * feats // 2:(core + 1) * feats // 2] = outa[core].astype(F32)
    for h in range(PLANE):
        out_bq[:, h * qcols:(h + 1) * qcols] = outb[h].astype(F32)
        value = outv[h].astype(F32)
        out_av[:, h * piece:(h + 1) * piece] = value[:, 0:piece]
        out_bv[:, h * kcols:(h + 1) * kcols] = value[:, piece:]


def on_plane(
    tokens,
    trace_index,
    input_norm_scale,
    query_weight,
    key_weight,
    value_weight,
    query_down_weight,
    query_up_weight,
    value_down_weight,
    value_up_weight,
    output_gradient,
):
    tok = tokens.shape[1]
    feats = tokens.shape[2]
    fsdp = lax.axis_size("fsdp")
    chain = fsdp // 4
    ranks = query_down_weight.shape[1]
    qcols = query_weight.shape[1] // PLANE
    kcols = key_weight.shape[1] // PLANE
    piece = feats // PLANE
    many = PLANE * tok
    token_total = lax.axis_size("ctx") * fsdp * tok
    coefficient = ADAPTER_NAME / math.sqrt(token_total)
    hbm = pl.BlockSpec(memory_space=pltpu.HBM)
    vmem = pl.BlockSpec(memory_space=pltpu.VMEM)
    dma = pltpu.SemaphoreType.DMA
    steps = chain - 1
    tiles = many // (2 * tok)
    heads = qcols // kcols
    outa, outb, outv = pl.pallas_call(
        functools.partial(plane_kernel, chain, coefficient),
        out_shape=(
            pltpu.VMEM((2, ranks, feats // 2), BF16),
            pltpu.VMEM((PLANE, ranks, qcols), BF16),
            pltpu.VMEM((PLANE, ranks, piece + kcols), BF16),
        ),
        in_specs=[hbm] * 11,
        out_specs=(vmem, vmem, vmem),
        scratch_shapes=[
            pltpu.VMEM((many, feats), BF16),
            pltpu.VMEM((many, feats), BF16),
            pltpu.VMEM((feats, qcols + kcols), BF16),
            pltpu.VMEM((feats, kcols), BF16),
            pltpu.VMEM((many, qcols), BF16),
            pltpu.VMEM((PLANE, 1, tok), jnp.int32),
            pltpu.VMEM((many, qcols + kcols), F32),
            pltpu.VMEM((many, kcols), F32),
            pltpu.VMEM((tiles * heads, 2 * tok, 2 * tok), BF16),
            pltpu.VMEM((tiles * heads, 2 * tok, 2 * tok), F32),
            pltpu.VMEM((many, kcols), BF16),
            pltpu.VMEM((many, qcols), BF16),
            pltpu.VMEM((many, kcols), BF16),
            pltpu.VMEM((many, 2 * ranks), BF16),
            pltpu.VMEM((feats,), BF16),
            pltpu.VMEM((2 * ranks, feats), BF16),
            pltpu.VMEM((ranks, query_weight.shape[1]), BF16),
            pltpu.VMEM((ranks, value_weight.shape[1]), BF16),
            pltpu.VMEM((2, PLANE, ranks, many // 2), BF16),
            pltpu.VMEM((2, PLANE, ranks, many // 2), BF16),
            pltpu.VMEM((chain, ranks, feats // 2), BF16),
            pltpu.VMEM((chain, ranks, qcols), BF16),
            pltpu.VMEM((chain, ranks, piece + kcols), BF16),
            pltpu.VMEM((ranks, feats // 2), BF16),
            pltpu.VMEM((ranks, qcols), BF16),
            pltpu.VMEM((ranks, piece + kcols), BF16),
            dma((11,)),
            dma((2,)), dma((4,)), dma((1,)), dma((11,)), dma((2,)), dma((2,)),
            dma((steps,)), dma((steps, 2)), dma((steps,)), dma((steps, 2)),
            dma((steps,)), dma((steps, 2)), dma((steps,)), dma((steps, 2)),
            dma((2,)), dma((2,)), dma((2,)), dma((2,)), dma((4,)), dma((4,)), dma((4,)),
        ],
        compiler_params=pltpu.CompilerParams(
            collective_id=0, has_side_effects=True, vmem_limit_bytes=56 * 1024 * 1024
        ),
    )(
        tokens.reshape(tok, feats), trace_index, input_norm_scale,
        query_weight, key_weight, value_weight,
        query_down_weight.T, query_up_weight, value_down_weight.T, value_up_weight,
        output_gradient.reshape(tok, output_gradient.shape[2]),
    )
    aq, bq, av, bv = pl.pallas_call(
        unpack_kernel,
        out_shape=(
            jax.ShapeDtypeStruct((ranks, feats), F32),
            jax.ShapeDtypeStruct((ranks, query_weight.shape[1]), F32),
            jax.ShapeDtypeStruct((ranks, feats), F32),
            jax.ShapeDtypeStruct((ranks, value_weight.shape[1]), F32),
        ),
        in_specs=[vmem, vmem, vmem],
        out_specs=(vmem, vmem, vmem, vmem),
        compiler_params=pltpu.CompilerParams(vmem_limit_bytes=16 * 1024 * 1024),
    )(outa, outb, outv)
    return (aq.T, bq, av.T, bv)


def solution(mesh):
    shape = mesh.shape
    planes = shape["groups"] == 1 and shape["ctx"] == 2 and shape["fsdp"] % 4 == 0 and shape["fsdp"] > 8
    return jax.shard_map(
        on_plane if planes else on_device,
        mesh=mesh,
        in_specs=(
            P(("groups", "fsdp"), "ctx", None),
            P(("groups", "fsdp"), "ctx"),
            P(),
            P("fsdp", None),
            P("fsdp", None),
            P("fsdp", None),
            P(),
            P(),
            P(),
            P(),
            P(("groups", "fsdp"), "ctx", None),
        ),
        out_specs=(P("groups", None), P("groups", None), P("groups", None), P("groups", None)),
        check_vma=False,
    )
```

```python
import functools
import math

import jax
import jax.numpy as jnp
from jax import lax
from jax.experimental import pallas as pl
from jax.experimental.pallas import tpu as pltpu
from jax.sharding import PartitionSpec as P

HEAD_SIZE = 128


CAP = 50.0
QSCALE = 1.0 / 12.0
ADAPTER_NAME = 0.5
EPS = 1e-06


def shifted(value, axis, by):
    devices = lax.axis_size(axis)
    pairs = [(i, i + by) for i in range(devices) if 0 <= i + by < devices]
    return lax.ppermute(value, axis, pairs)


def normed_rows(values, gain):
    flt = values.astype(jnp.float32)
    meansq = jnp.mean(flt * flt, axis=-1, keepdims=True)
    return (flt * lax.rsqrt(meansq + EPS) * gain.astype(jnp.float32)).astype(jnp.bfloat16)


def add_rows(left, piece):
    return jnp.dot(left, piece, preferred_element_type=jnp.float32)


def attend_head(operands, mask):
    q_head, k_head, v_head, g_head = operands
    s = jnp.einsum("igd,jd->gij", q_head, k_head, preferred_element_type=jnp.float32) * QSCALE
    t = jnp.tanh(s / CAP)
    capped = CAP * t
    expo = jnp.where(mask[None], jnp.exp(capped), jnp.float32(0.0))
    weights = expo / jnp.sum(expo, axis=-1, keepdims=True)
    weights16 = weights.astype(jnp.bfloat16)
    attended = jnp.einsum("gij,jd->igd", weights16, v_head, preferred_element_type=jnp.float32)
    dweight = jnp.einsum("igd,jd->gij", g_head, v_head, preferred_element_type=jnp.float32)
    delta = jnp.sum(g_head.astype(jnp.float32) * attended, axis=-1).T
    dscore = (weights * (dweight - delta[..., None]) * (1.0 - t * t) * QSCALE).astype(jnp.bfloat16)
    query_gradient = jnp.einsum(
        "gij,jd->igd", dscore, k_head, preferred_element_type=jnp.float32
    ).astype(jnp.bfloat16)
    value_gradient = jnp.einsum(
        "gij,igd->jd", weights16, g_head, preferred_element_type=jnp.float32
    )
    return (query_gradient, value_gradient)


def partial_attend(mask):

    def run_head(operands):
        return attend_head(operands, mask)

    return run_head


def on_device(
    tokens,
    trace_index,
    input_norm_scale,
    query_weight,
    key_weight,
    value_weight,
    query_down_weight,
    query_up_weight,
    value_down_weight,
    value_up_weight,
    output_gradient,
):
    window_width = tokens.shape[1]
    feats = tokens.shape[2]
    heads_kv = key_weight.shape[1] // HEAD_SIZE
    heads_q = query_weight.shape[1] // HEAD_SIZE
    head_group = heads_q // heads_kv
    normalized_input = normed_rows(tokens.reshape(window_width, feats), input_norm_scale)
    seg_own = trace_index.reshape(window_width).astype(jnp.bfloat16)
    seg_parts = []

    def add_keyval(piece):
        return add_rows(normalized_input, piece)

    query_frozen = add_rows(
        normalized_input, lax.all_gather(query_weight, "fsdp", axis=0, tiled=True)
    )
    k_base = add_keyval(lax.all_gather(key_weight, "fsdp", axis=0, tiled=True))
    value_frozen = add_keyval(lax.all_gather(value_weight, "fsdp", axis=0, tiled=True))
    query_reduced = jnp.dot(
        normalized_input, query_down_weight, preferred_element_type=jnp.float32
    ).astype(jnp.bfloat16)
    reduced_rows = jnp.dot(
        normalized_input, value_down_weight, preferred_element_type=jnp.float32
    ).astype(jnp.bfloat16)
    query_matrix = (
        query_frozen
        + ADAPTER_NAME * jnp.dot(query_reduced, query_up_weight, preferred_element_type=jnp.float32)
    ).astype(jnp.bfloat16)
    key_rows = k_base.astype(jnp.bfloat16)
    value_rows = (
        value_frozen
        + ADAPTER_NAME * jnp.dot(reduced_rows, value_up_weight, preferred_element_type=jnp.float32)
    ).astype(jnp.bfloat16)
    key_parts = []
    value_parts = []
    for distance in (2, 1):
        key_prev, value_prev, seg_prev = shifted((key_rows, value_rows, seg_own), "ctx", distance)
        key_parts.append(key_prev)
        value_parts.append(value_prev)
        seg_parts.append(seg_prev)
    keys_all = jnp.concatenate(key_parts + [key_rows], 0)
    values_all = jnp.concatenate(value_parts + [value_rows], 0)
    seg_keys = jnp.concatenate(seg_parts + [seg_own], 0)
    pos_q = jnp.arange(window_width, dtype=jnp.int32)[:, None]
    pos_k = jnp.arange(3 * window_width, dtype=jnp.int32)[None, :]
    position = lax.axis_index("ctx")
    mask = (
        (pos_k > pos_q)
        & (pos_k <= pos_q + 2 * window_width)
        & (seg_keys[None, :] == seg_own[:, None])
    )
    mask = mask & (
        (pos_k >= 2 * window_width) | (pos_k >= window_width) & (position >= 1) | (position >= 2)
    )
    q_heads = jnp.moveaxis(
        query_matrix.reshape(window_width, heads_kv, head_group, HEAD_SIZE), 1, 0
    )
    g_heads = jnp.moveaxis(
        output_gradient.reshape(window_width, heads_kv, head_group, HEAD_SIZE), 1, 0
    )
    k_heads = jnp.moveaxis(keys_all.reshape(3 * window_width, heads_kv, HEAD_SIZE), 1, 0)
    v_heads = jnp.moveaxis(values_all.reshape(3 * window_width, heads_kv, HEAD_SIZE), 1, 0)
    dquery_heads, dvalue_heads = lax.map(partial_attend(mask), (q_heads, k_heads, v_heads, g_heads))
    query_gradient = jnp.moveaxis(dquery_heads, 0, 1).reshape(window_width, heads_q * HEAD_SIZE)
    dvalue_triple = jnp.moveaxis(dvalue_heads, 0, 1).reshape(3 * window_width, heads_kv * HEAD_SIZE)
    value_gradient = dvalue_triple[2 * window_width :]
    for distance in (1, 2):
        begin = (2 - distance) * window_width
        value_gradient = value_gradient + shifted(
            dvalue_triple[begin : begin + window_width], "ctx", -distance
        )
    query_backward = jnp.dot(
        query_gradient, query_up_weight.T, preferred_element_type=jnp.float32
    ).astype(jnp.bfloat16)
    value_backward = jnp.dot(
        value_gradient, value_up_weight.astype(jnp.float32).T, precision=lax.Precision.HIGHEST
    )
    part_aq = jnp.dot(normalized_input.T, query_backward, preferred_element_type=jnp.float32)
    part_bq = jnp.dot(query_reduced.T, query_gradient, preferred_element_type=jnp.float32)
    part_av = jnp.dot(
        normalized_input.astype(jnp.float32).T, value_backward, precision=lax.Precision.HIGHEST
    )
    part_bv = jnp.dot(
        reduced_rows.astype(jnp.float32).T, value_gradient, precision=lax.Precision.HIGHEST
    )
    sum_aq, sum_bq, sum_av, sum_bv = lax.psum((part_aq, part_bq, part_av, part_bv), ("ctx", "fsdp"))
    token_total = lax.axis_size("ctx") * lax.axis_size("fsdp") * window_width
    coefficient = ADAPTER_NAME / math.sqrt(token_total)
    return (sum_aq * coefficient, sum_bq * coefficient, sum_av * coefficient, sum_bv * coefficient)


F32 = jnp.float32
BF16 = jnp.bfloat16
PLANE = 8


def dot(a, b, dims=((1,), (0,))):
    return lax.dot_general(a, b, (dims, ((), ())), preferred_element_type=F32)


def plane_kernel(
    chain, coefficient,
    raw, seg, gain_in, wq, wk, wv, qd, qu_in, vd, vu_in, grad,
    OUTA, OUTV,
    N, M, WA, WV, G, SG, acc, accv, P, C, K, DQ, DV, LL,
    gain, down, qu, vu,
    PQ, PV, RSA, RSV, TA, TV,
    local_sem, w_send, w_recv, t_send, t_recv, g_sem, s_sem,
    up_send, up_recv, down_send, down_recv, vup_send, vup_recv, vdown_send, vdown_recv,
    q1_send, q1_recv, v1_send, v1_recv, a_sem, v_sem,
):
    x = lax.axis_index("ctx")
    f = lax.axis_index("fsdp")
    z = f // 4
    y = (f // 2) % 2
    c = f % 2
    tok, feats = raw.shape
    rows = wq.shape[0]
    qcols = wq.shape[1] // PLANE
    kcols = wk.shape[1] // PLANE
    acols = qcols + kcols
    piece = feats // PLANE
    seq = 2 * tok
    sub = tok // 4
    heads = qcols // kcols
    ranks = qd.shape[0]
    middle = (z > 0) & (z < chain - 1)
    outer = (z == 0) | (z == chain - 1)

    def coords(r):
        px = 1 - x if r & 4 else x
        py = 1 - y if r & 2 else y
        pc = 1 - c if r & 1 else c
        return px, py, pc

    def head_of(r):
        px, py, pc = coords(r)
        return (px * 2 + py) * 2 + pc

    def peer(r):
        px, py, pc = coords(r)
        return {"ctx": px, "fsdp": (z * 2 + py) * 2 + pc}

    def above(pz):
        return {"ctx": x, "fsdp": (pz * 2 + y) * 2 + c}

    def tok_slot(r):
        px, py, pc = coords(r)
        return (py * 2 + pc) * 2 + px

    def tok_piece(r, low, count):
        begin = tok_slot(r) * tok + low * sub
        return pl.ds(pl.multiple_of(begin, sub), count * sub)

    def tok_rows(r):
        return pl.ds(pl.multiple_of(tok_slot(r) * tok, tok), tok)

    def remote(src, dst, send, recv, device):
        return pltpu.make_async_remote_copy(
            src_ref=src, dst_ref=dst, send_sem=send, recv_sem=recv,
            device_id=device, device_id_type=pl.DeviceIdType.MESH,
        )

    barrier = pltpu.get_barrier_semaphore()
    for r in range(1, PLANE):
        pl.semaphore_signal(barrier, inc=1, device_id=peer(r), device_id_type=pl.DeviceIdType.MESH)
    for d in range(1, chain):
        pl.semaphore_signal(
            barrier, inc=1, device_id=above((z + d) % chain), device_id_type=pl.DeviceIdType.MESH
        )

    def w_rows(r):
        px, py, pc = coords(r)
        return pl.ds(pl.multiple_of(((z * 2 + py) * 2 + pc) * rows, rows), rows)

    def w_parts(r):
        h = head_of(r)
        own = w_rows(0)
        return (
            (wq.at[:, pl.ds(pl.multiple_of(h * qcols, qcols), qcols)], WA.at[own, pl.ds(0, qcols)]),
            (wk.at[:, pl.ds(pl.multiple_of(h * kcols, kcols), kcols)], WA.at[own, pl.ds(qcols, kcols)]),
            (wv.at[:, pl.ds(pl.multiple_of(h * kcols, kcols), kcols)], WV.at[own]),
        )

    def g_cols(r):
        h = head_of(r)
        return grad.at[:, pl.ds(pl.multiple_of(h * qcols, qcols), qcols)]

    local = [pltpu.make_async_copy(a, b, local_sem.at[i]) for i, (a, b) in enumerate(w_parts(0))]
    local.append(pltpu.make_async_copy(raw, N.at[tok_rows(0)], local_sem.at[3]))
    local.append(pltpu.make_async_copy(g_cols(0), G.at[tok_rows(0)], local_sem.at[4]))
    local.append(pltpu.make_async_copy(seg, SG.at[tok_slot(0)], local_sem.at[5]))
    local.append(pltpu.make_async_copy(qd, down.at[pl.ds(0, ranks)], local_sem.at[6]))
    local.append(pltpu.make_async_copy(vd, down.at[pl.ds(ranks, ranks)], local_sem.at[7]))
    local.append(pltpu.make_async_copy(qu_in, qu, local_sem.at[8]))
    local.append(pltpu.make_async_copy(vu_in, vu, local_sem.at[9]))
    local.append(pltpu.make_async_copy(gain_in, gain, local_sem.at[10]))
    for copy in local:
        copy.start()
    for i in range(2):
        local[i].wait()
    pl.semaphore_wait(barrier, PLANE - 1 + chain - 1)

    def half_rows(plane, half):
        py = y if half == 0 else 1 - y
        return pl.ds(pl.multiple_of((plane * 4 + py * 2) * rows, 2 * rows), 2 * rows)

    def quarter_rows(plane, quarter):
        px, py, pc = coords(quarter)
        return pl.ds(pl.multiple_of((plane * 4 + py * 2 + pc) * rows, rows), rows)

    def has_up(t):
        return (z < chain - 1) & (z - t >= 0)

    def has_down(t):
        return (z > 0) & (z + t <= chain - 1)

    def from_below(t):
        return z - 1 - t >= 0

    def from_above(t):
        return z + 1 + t <= chain - 1

    def pieces_of(t):
        return range(4) if t == 0 else range(2)

    def piece_rows(plane, t, i):
        return quarter_rows(plane, i) if t == 0 else half_rows(plane, i)

    def half_of(t, i):
        return i // 2 if t == 0 else i

    def plane_rows(plane):
        return pl.ds(pl.multiple_of(plane * 4 * rows, 4 * rows), 4 * rows)

    def up_copy(t, i):
        at = WA.at[piece_rows(z - t, t, i)]
        return remote(at, at, up_send.at[t], up_recv.at[t, half_of(t, i)], above(z + 1))

    def down_copy(t, i):
        at = WA.at[piece_rows(z + t, t, i)]
        return remote(at, at, down_send.at[t], down_recv.at[t, half_of(t, i)], above(z - 1))

    def up_arrival(t, half):
        at = WA.at[half_rows(z - 1 - t, half)]
        return remote(at, at, up_send.at[t], up_recv.at[t, half], above(z - 1))

    def down_arrival(t, half):
        at = WA.at[half_rows(z + 1 + t, half)]
        return remote(at, at, down_send.at[t], down_recv.at[t, half], above(z + 1))

    def vup_copy(t, half):
        at = WV.at[half_rows(z - t, half)]
        return remote(at, at, vup_send.at[t], vup_recv.at[t, half], above(z + 1))

    def vdown_copy(t, half):
        at = WV.at[half_rows(z + t, half)]
        return remote(at, at, vdown_send.at[t], vdown_recv.at[t, half], above(z - 1))

    def vup_arrival(t, half):
        at = WV.at[half_rows(z - 1 - t, half)]
        return remote(at, at, vup_send.at[t], vup_recv.at[t, half], above(z - 1))

    def vdown_arrival(t, half):
        at = WV.at[half_rows(z + 1 + t, half)]
        return remote(at, at, vdown_send.at[t], vdown_recv.at[t, half], above(z + 1))

    def send_chain(t, i):
        @pl.when(has_up(t))
        def _():
            up_copy(t, i).start()

        @pl.when(has_down(t))
        def _():
            down_copy(t, i).start()

    def recv_half(t, half):
        @pl.when(from_below(t))
        def _():
            up_arrival(t, half).wait_recv()

        @pl.when(from_above(t))
        def _():
            down_arrival(t, half).wait_recv()

    def send_value_first(k):
        @pl.when(has_up(k - 1) & jnp.logical_not(has_up(k)))
        def _():
            for half in range(2):
                vup_copy(0, half).start()

        @pl.when(has_down(k - 1) & jnp.logical_not(has_down(k)))
        def _():
            for half in range(2):
                vdown_copy(0, half).start()

    def send_value(t, half):
        @pl.when(has_up(t))
        def _():
            vup_copy(t, half).start()

        @pl.when(has_down(t))
        def _():
            vdown_copy(t, half).start()

    def recv_value(t, half):
        @pl.when(from_below(t))
        def _():
            vup_arrival(t, half).wait_recv()

        @pl.when(from_above(t))
        def _():
            vdown_arrival(t, half).wait_recv()

    w_copies = {}
    for r in (1, 2, 3):
        w_copies[r] = [
            remote(a, b, w_send.at[i // 2], w_recv.at[r if i < 2 else 0], peer(r))
            for i, (a, b) in enumerate(w_parts(r))
        ]
    for r in (1, 2, 3):
        for i in range(2):
            w_copies[r][i].start()
    send_chain(0, 0)
    for r in (1, 2, 3):
        w_copies[r][2].start()

    t_slot = {(1, 0): 0, (4, 3): 1, (4, 0): 2, (5, 0): 3, (3, 0): 4, (7, 0): 5}
    for low in range(4):
        t_slot[2, low] = 6 + low
        t_slot[6, low] = 10

    def send_token(r_mine, r_there, hop, low=0, count=4):
        at = N.at[tok_piece(r_mine, low, count)]
        source = raw.at[pl.ds(low * sub, count * sub)] if r_mine == 0 else at
        remote(source, at, t_send.at[0], t_recv.at[t_slot[r_there, low]], peer(hop)).start()

    def wait_token(r, low=0, count=4):
        at = N.at[tok_piece(r, low, count)]
        remote(at, at, t_send.at[0], t_recv.at[t_slot[r, low]], peer(1)).wait_recv()

    send_token(0, 1, 1)
    send_token(0, 4, 4, 3, 1)
    send_token(0, 4, 4, 0, 3)
    for low in range(4):
        send_token(0, 2, 2, low, 1)
    g_copies = {}
    s_copies = {}
    for r in range(1, PLANE):
        g_copies[r] = remote(g_cols(r), G.at[tok_rows(0)], g_sem.at[0], g_sem.at[1], peer(r))
        s_copies[r] = remote(seg, SG.at[tok_slot(0)], s_sem.at[0], s_sem.at[1], peer(r))

    def wait_weight(r):
        ref = WA.at[w_rows(r)]
        remote(ref, ref, w_send.at[0], w_recv.at[r], peer(r)).wait_recv()

    def wait_values():
        ref = WV.at[pl.ds(0, 3 * rows)]
        remote(ref, ref, w_send.at[1], w_recv.at[0], peer(1)).wait_recv()

    part_rows = 4 * tok

    def part_at(part, i, height):
        py = y if part == 0 else 1 - y
        return pl.ds(pl.multiple_of(py * part_rows + i * height, height), height)

    h = head_of(0)

    def query_up():
        return qu[:, pl.ds(pl.multiple_of(h * qcols, qcols), qcols)]

    def value_up():
        return vu[:, pl.ds(pl.multiple_of(h * kcols, kcols), kcols)]

    def prepare(r):
        height = tok // 2

        @pl.loop(0, 2)
        def _(i):
            begin = tok_slot(r) * tok + i * height
            at = pl.ds(pl.multiple_of(begin, height), height)
            flt = N[at, :].astype(F32)
            meansq = jnp.sum(flt * flt, axis=-1, keepdims=True) / feats
            M[at, :] = (flt * lax.rsqrt(meansq + EPS) * gain[...].astype(F32).reshape(1, feats)).astype(BF16)

        at = tok_rows(r)
        block = M[at, :]
        low = dot(block, down[...], ((1,), (1,))).astype(BF16)
        LL[at, :] = low
        filler = jnp.zeros((ranks, qcols), BF16)
        acc[at, 0:qcols] = ADAPTER_NAME * dot(low, jnp.concatenate([query_up(), filler], axis=0))
        acc[at, qcols:] = jnp.zeros((tok, kcols), F32)
        accv[at, :] = ADAPTER_NAME * dot(low, jnp.concatenate([filler[:, 0:kcols], value_up()], axis=0))

    def add_piece(plane, half, part):
        chosen = half_rows(plane, half)

        @pl.loop(0, part_rows // seq)
        def _(i):
            at = part_at(part, i, seq)
            acc[at, :] = acc[at, :] + dot(M[at, chosen], WA[chosen, :])

    def add_near(part):
        low = jnp.maximum(z - 2, 0)
        high = jnp.minimum(z + 2, chain - 1)
        for count in range(3, min(chain, 5) + 1):
            @pl.when(high - low == count - 1)
            def _():
                chosen = pl.ds(pl.multiple_of(low * 4 * rows, 4 * rows), count * 4 * rows)

                @pl.loop(0, part_rows // seq)
                def _(i):
                    at = part_at(part, i, seq)
                    acc[at, :] = acc[at, :] + dot(M[at, chosen], WA[chosen, :])

    def add_step(t, half, part):
        @pl.when(from_below(t))
        def _():
            add_piece(z - 1 - t, half, part)

        @pl.when(from_above(t))
        def _():
            add_piece(z + 1 + t, half, part)

    def add_value_piece(plane, half):
        chosen = plane_rows(plane) if half is None else half_rows(plane, half)

        @pl.loop(0, 2 * part_rows // seq)
        def _(i):
            at = pl.ds(pl.multiple_of(i * seq, seq), seq)
            accv[at, :] = accv[at, :] + dot(M[at, chosen], WV[chosen, :])

    def add_value(t, half):
        @pl.when(from_below(t))
        def _():
            add_value_piece(z - 1 - t, half)

        @pl.when(from_above(t))
        def _():
            add_value_piece(z + 1 + t, half)

    wait_weight(1)
    send_chain(0, 1)
    for r in range(1, PLANE):
        s_copies[r].start()
    local[3].wait()
    for i in range(6, 11):
        local[i].wait()
    prepare(0)
    wait_token(1)
    prepare(1)
    wait_weight(2)
    send_chain(0, 2)
    wait_weight(3)
    send_chain(0, 3)
    recv_half(0, 0)
    send_chain(1, 0)
    wait_token(2, 0, 1)
    send_token(2, 6, 4, 0, 1)
    recv_half(0, 1)
    send_chain(1, 1)
    local[2].wait()
    wait_values()
    send_value_first(1)
    wait_token(2, 1, 1)
    send_token(2, 6, 4, 1, 1)
    wait_token(4, 3, 1)
    send_token(4, 6, 2, 3, 1)
    wait_token(4, 0, 3)
    send_token(4, 5, 1)
    prepare(4)
    wait_token(2, 2, 1)
    send_token(2, 6, 4, 2, 1)
    for r in (6, 7, 4, 5, 2, 3, 1):
        g_copies[r].start()
    wait_token(5)
    prepare(5)
    recv_half(1, 0)
    send_chain(2, 0)
    wait_token(2, 3, 1)
    send_token(2, 3, 1)
    prepare(2)
    wait_token(3)
    prepare(3)
    recv_half(1, 1)
    send_chain(2, 1)
    for k in range(2, chain):
        send_value_first(k)
    add_near(0)
    wait_token(6)
    send_token(6, 7, 1)
    prepare(6)
    wait_token(7)
    prepare(7)

    @pl.when(middle)
    def _():
        for half in range(2):
            recv_value(0, half)
            send_value(1, half)

    add_near(1)
    for t in range(2, chain - 1):
        for half in range(2):
            recv_half(t, half)
            if t + 1 < chain - 1:
                send_chain(t + 1, half)
            for part in range(2):
                add_step(t, half, part)

    tiles = PLANE * tok // seq
    local[4].wait()
    local[5].wait()
    g_others = G.at[pl.ds(0, (PLANE - 1) * tok)]
    g_all_copies = remote(g_others, g_others, g_sem.at[0], g_sem.at[1], peer(1))
    g_all_copies.wait_recv()
    s_others = SG.at[pl.ds(0, PLANE - 1)]
    s_all_copies = remote(s_others, s_others, s_sem.at[0], s_sem.at[1], peer(1))
    s_all_copies.wait_recv()

    pos_i = lax.broadcasted_iota(jnp.int32, (seq, seq), 0)
    pos_j = lax.broadcasted_iota(jnp.int32, (seq, seq), 1)
    band = (pos_j <= pos_i) & (pos_j > pos_i - 2 * tok)

    @pl.loop(0, tiles, unroll=2)
    def _(i):
        at = pl.ds(pl.multiple_of(i * seq, seq), seq)
        q_all = acc[at, 0:qcols].astype(BF16)
        k = acc[at, qcols:].astype(BF16)
        K[at, :] = k
        g_all = G[at, :]
        traces = [SG[2 * i].astype(F32), SG[2 * i + 1].astype(F32)]
        along = jnp.concatenate(traces, axis=1)
        turned = [jnp.broadcast_to(own, (tok, tok)).T for own in traces]
        across = jnp.concatenate([jnp.concatenate([own, own], axis=1) for own in turned], axis=0)
        mask = band & (across == along)
        dv = jnp.zeros((seq, kcols), F32)
        for n in range(heads):
            q = q_all[:, n * kcols:(n + 1) * kcols]
            g = g_all[:, n * kcols:(n + 1) * kcols]
            t = jnp.tanh(dot(q, k, ((1,), (1,))) * (QSCALE / CAP))
            expo = jnp.where(mask, jnp.exp(CAP * t), 0.0)
            weights = expo * (1.0 / jnp.sum(expo, axis=-1, keepdims=True))
            weights16 = weights.astype(BF16)
            P[i * heads + n] = weights16
            C[i * heads + n] = weights * (1.0 - t * t)
            dv = dv + dot(weights16, g, ((0,), (0,)))
        DV[at, :] = dv.astype(BF16)

    @pl.when(middle)
    def _():
        for t in range(1, chain - 1):
            for half in range(2):
                recv_value(t, half)
                if t + 1 < chain - 1:
                    send_value(t + 1, half)

    half_tokens = PLANE * tok // 2

    def token_half(half):
        return pl.ds(half * half_tokens, half_tokens)

    def send_pull(half, up, change, gathered, send, recv):
        own = gathered.at[half, h]
        own[...] = dot(up, change[token_half(half), :], ((1,), (1,))).astype(BF16)
        for r in (7, 6, 5, 4, 3, 2, 1):
            remote(own, own, send.at[half], recv.at[half], peer(r)).start()

    def pulls(half, gathered, send, recv):
        at = gathered.at[half, pl.ds(0, PLANE - 1)]
        return remote(at, at, send.at[half], recv.at[half], peer(1))

    def down_gradient(columns, width, gathered, send, recv):
        total = jnp.zeros((ranks, width), F32)
        for half in range(2):
            pulls(half, gathered, send, recv).wait_recv()
            pull = gathered[half, 0].astype(F32)
            for r in range(1, PLANE):
                pull = pull + gathered[half, r].astype(F32)
            total = total + dot(pull.astype(BF16), M[token_half(half), columns])
        return total.astype(BF16)

    def share(sums, sem):
        own = sums.at[z]
        for d in range(1, chain):
            remote(own, own, sem.at[0], sem.at[1], above((z + d) % chain)).start()

    def shares(sums, sem):
        at = sums.at[pl.ds(0, chain - 1)]
        return remote(at, at, sem.at[0], sem.at[1], peer(1))

    def shared(sums):
        total = sums[0].astype(F32)
        for d in range(1, chain):
            total = total + sums[d].astype(F32)
        return (total * coefficient).astype(BF16)

    def spread(total, mine, out, sem):
        mine[...] = total
        for r in (7, 6, 5, 4, 3, 2, 1):
            remote(mine, out.at[h], sem.at[2], sem.at[3], peer(r)).start()
        out[h] = total

    def spreads(out, sem):
        at = out.at[pl.ds(0, PLANE - 1)]
        return remote(at, at, sem.at[2], sem.at[3], peer(1))

    for half in range(2):
        send_pull(half, value_up(), DV, PV, v1_send, v1_recv)
    low_gradient = dot(LL[...], DV[...], ((0,), (0,)))
    RSV.at[z][:, piece:piece + kcols] = low_gradient[ranks:, :].astype(BF16)
    add_value_piece(z, None)
    for t in range(chain - 2):
        @pl.when(outer)
        def _():
            for half in range(2):
                recv_value(t, half)

        add_value(t, None)
    own_columns = pl.ds(pl.multiple_of(h * piece, piece), piece)
    RSV.at[z][:, 0:piece] = down_gradient(own_columns, piece, PV, v1_send, v1_recv)
    for half in range(2):
        @pl.when(outer)
        def _():
            recv_value(chain - 2, half)

        add_value(chain - 2, half)

    for half in range(2):
        for i in range(half * tiles // 2, (half + 1) * tiles // 2):
            at = pl.ds(i * seq, seq)
            v = accv[at, :].astype(BF16)
            k = K[at, :]
            for n in range(heads):
                g = G[at, n * kcols:(n + 1) * kcols]
                dweight = dot(g, v, ((1,), (1,)))
                delta = jnp.sum(P[i * heads + n].astype(F32) * dweight, axis=-1, keepdims=True)
                dscore = (C[i * heads + n] * (dweight - delta)).astype(BF16)
                DQ[at, n * kcols:(n + 1) * kcols] = (dot(dscore, k) * QSCALE).astype(BF16)
        send_pull(half, query_up(), DQ, PQ, q1_send, q1_recv)

    low_gradient = dot(LL[...], DQ[...], ((0,), (0,)))
    RSV.at[z][:, piece + kcols:] = low_gradient[0:ranks, :].astype(BF16)
    share(RSV, v_sem)
    width = feats // 2
    core_columns = pl.ds(pl.multiple_of(c * width, width), width)
    RSA[z] = down_gradient(core_columns, width, PQ, q1_send, q1_recv)

    @pl.when(outer)
    def _():
        share(RSA, a_sem)

    shares(RSV, v_sem).wait_recv()

    @pl.when(middle)
    def _():
        share(RSA, a_sem)

    spread(shared(RSV), TV, OUTV, v_sem)
    shares(RSA, a_sem).wait_recv()
    TA[...] = shared(RSA)
    core_copy = remote(TA, OUTA.at[c], a_sem.at[2], a_sem.at[3], peer(1))
    core_copy.start()
    OUTA[c] = TA[...]
    spreads(OUTV, v_sem).wait_recv()
    at = OUTA.at[1 - c]
    remote(at, at, a_sem.at[2], a_sem.at[3], peer(1)).wait_recv()

    at = WA.at[pl.ds(0, 3 * rows)]
    remote(at, at, w_send.at[0], w_recv.at[1], peer(1)).wait_send()
    at = WV.at[pl.ds(0, 3 * rows)]
    remote(at, at, w_send.at[1], w_recv.at[0], peer(1)).wait_send()
    at = N.at[pl.ds(0, (PLANE - 1) * tok)]
    remote(at, at, t_send.at[0], t_recv.at[0], peer(1)).wait_send()
    g_all_copies.wait_send()
    s_all_copies.wait_send()
    for t in range(chain - 1):
        @pl.when(has_up(t))
        def _():
            at = WA.at[plane_rows(z - t)]
            remote(at, at, up_send.at[t], up_recv.at[t, 0], above(z + 1)).wait_send()
            at = WV.at[plane_rows(z - t)]
            remote(at, at, vup_send.at[t], vup_recv.at[t, 0], above(z + 1)).wait_send()

        @pl.when(has_down(t))
        def _():
            at = WA.at[plane_rows(z + t)]
            remote(at, at, down_send.at[t], down_recv.at[t, 0], above(z - 1)).wait_send()
            at = WV.at[plane_rows(z + t)]
            remote(at, at, vdown_send.at[t], vdown_recv.at[t, 0], above(z - 1)).wait_send()
    for half in range(2):
        pulls(half, PV, v1_send, v1_recv).wait_send()
        pulls(half, PQ, q1_send, q1_recv).wait_send()
    for sums, sem in ((RSV, v_sem), (RSA, a_sem)):
        shares(sums, sem).wait_send()
    spreads(OUTV, v_sem).wait_send()
    core_copy.wait_send()


def unpack_kernel(outa, outv, out_aq, out_bq, out_av, out_bv):
    feats = out_aq.shape[1]
    piece = feats // PLANE
    qcols = out_bq.shape[1] // PLANE
    kcols = out_bv.shape[1] // PLANE
    for core in range(2):
        out_aq[:, core * feats // 2:(core + 1) * feats // 2] = outa[core].astype(F32)
    for h in range(PLANE):
        value = outv[h].astype(F32)
        out_bq[:, h * qcols:(h + 1) * qcols] = value[:, piece + kcols:]
        out_av[:, h * piece:(h + 1) * piece] = value[:, 0:piece]
        out_bv[:, h * kcols:(h + 1) * kcols] = value[:, piece:piece + kcols]


def on_plane(
    tokens,
    trace_index,
    input_norm_scale,
    query_weight,
    key_weight,
    value_weight,
    query_down_weight,
    query_up_weight,
    value_down_weight,
    value_up_weight,
    output_gradient,
):
    tok = tokens.shape[1]
    feats = tokens.shape[2]
    fsdp = lax.axis_size("fsdp")
    chain = fsdp // 4
    ranks = query_down_weight.shape[1]
    qcols = query_weight.shape[1] // PLANE
    kcols = key_weight.shape[1] // PLANE
    piece = feats // PLANE
    many = PLANE * tok
    token_total = lax.axis_size("ctx") * fsdp * tok
    coefficient = ADAPTER_NAME / math.sqrt(token_total)
    hbm = pl.BlockSpec(memory_space=pltpu.HBM)
    vmem = pl.BlockSpec(memory_space=pltpu.VMEM)
    dma = pltpu.SemaphoreType.DMA
    steps = chain - 1
    tiles = many // (2 * tok)
    heads = qcols // kcols
    outa, outv = pl.pallas_call(
        functools.partial(plane_kernel, chain, coefficient),
        out_shape=(
            pltpu.VMEM((2, ranks, feats // 2), BF16),
            pltpu.VMEM((PLANE, ranks, piece + kcols + qcols), BF16),
        ),
        in_specs=[hbm] * 11,
        out_specs=(vmem, vmem),
        scratch_shapes=[
            pltpu.VMEM((many, feats), BF16),
            pltpu.VMEM((many, feats), BF16),
            pltpu.VMEM((feats, qcols + kcols), BF16),
            pltpu.VMEM((feats, kcols), BF16),
            pltpu.VMEM((many, qcols), BF16),
            pltpu.VMEM((PLANE, 1, tok), jnp.int32),
            pltpu.VMEM((many, qcols + kcols), F32),
            pltpu.VMEM((many, kcols), F32),
            pltpu.VMEM((tiles * heads, 2 * tok, 2 * tok), BF16),
            pltpu.VMEM((tiles * heads, 2 * tok, 2 * tok), F32),
            pltpu.VMEM((many, kcols), BF16),
            pltpu.VMEM((many, qcols), BF16),
            pltpu.VMEM((many, kcols), BF16),
            pltpu.VMEM((many, 2 * ranks), BF16),
            pltpu.VMEM((feats,), BF16),
            pltpu.VMEM((2 * ranks, feats), BF16),
            pltpu.VMEM((ranks, query_weight.shape[1]), BF16),
            pltpu.VMEM((ranks, value_weight.shape[1]), BF16),
            pltpu.VMEM((2, PLANE, ranks, many // 2), BF16),
            pltpu.VMEM((2, PLANE, ranks, many // 2), BF16),
            pltpu.VMEM((chain, ranks, feats // 2), BF16),
            pltpu.VMEM((chain, ranks, piece + kcols + qcols), BF16),
            pltpu.VMEM((ranks, feats // 2), BF16),
            pltpu.VMEM((ranks, piece + kcols + qcols), BF16),
            dma((11,)),
            dma((2,)), dma((4,)), dma((1,)), dma((11,)), dma((2,)), dma((2,)),
            dma((steps,)), dma((steps, 2)), dma((steps,)), dma((steps, 2)),
            dma((steps,)), dma((steps, 2)), dma((steps,)), dma((steps, 2)),
            dma((2,)), dma((2,)), dma((2,)), dma((2,)), dma((4,)), dma((4,)),
        ],
        compiler_params=pltpu.CompilerParams(
            collective_id=0, has_side_effects=True, vmem_limit_bytes=56 * 1024 * 1024
        ),
    )(
        tokens.reshape(tok, feats), trace_index, input_norm_scale,
        query_weight, key_weight, value_weight,
        query_down_weight.T, query_up_weight, value_down_weight.T, value_up_weight,
        output_gradient.reshape(tok, output_gradient.shape[2]),
    )
    aq, bq, av, bv = pl.pallas_call(
        unpack_kernel,
        out_shape=(
            jax.ShapeDtypeStruct((ranks, feats), F32),
            jax.ShapeDtypeStruct((ranks, query_weight.shape[1]), F32),
            jax.ShapeDtypeStruct((ranks, feats), F32),
            jax.ShapeDtypeStruct((ranks, value_weight.shape[1]), F32),
        ),
        in_specs=[vmem, vmem],
        out_specs=(vmem, vmem, vmem, vmem),
        compiler_params=pltpu.CompilerParams(vmem_limit_bytes=16 * 1024 * 1024),
    )(outa, outv)
    return (aq.T, bq, av.T, bv)


def solution(mesh):
    shape = mesh.shape
    planes = shape["groups"] == 1 and shape["ctx"] == 2 and shape["fsdp"] % 4 == 0 and shape["fsdp"] > 8
    return jax.shard_map(
        on_plane if planes else on_device,
        mesh=mesh,
        in_specs=(
            P(("groups", "fsdp"), "ctx", None),
            P(("groups", "fsdp"), "ctx"),
            P(),
            P("fsdp", None),
            P("fsdp", None),
            P("fsdp", None),
            P(),
            P(),
            P(),
            P(),
            P(("groups", "fsdp"), "ctx", None),
        ),
        out_specs=(P("groups", None), P("groups", None), P("groups", None), P("groups", None)),
        check_vma=False,
    )
```

```python
import functools
import math

import jax
import jax.numpy as jnp
from jax import lax
from jax.experimental import pallas as pl
from jax.experimental.pallas import tpu as pltpu
from jax.sharding import PartitionSpec as P

HEAD_SIZE = 128


CAP = 50.0
QSCALE = 1.0 / 12.0
ADAPTER_NAME = 0.5
EPS = 1e-06


def shifted(value, axis, by):
    devices = lax.axis_size(axis)
    pairs = [(i, i + by) for i in range(devices) if 0 <= i + by < devices]
    return lax.ppermute(value, axis, pairs)


def normed_rows(values, gain):
    flt = values.astype(jnp.float32)
    meansq = jnp.mean(flt * flt, axis=-1, keepdims=True)
    return (flt * lax.rsqrt(meansq + EPS) * gain.astype(jnp.float32)).astype(jnp.bfloat16)


def add_rows(left, piece):
    return jnp.dot(left, piece, preferred_element_type=jnp.float32)


def attend_head(operands, mask):
    q_head, k_head, v_head, g_head = operands
    s = jnp.einsum("igd,jd->gij", q_head, k_head, preferred_element_type=jnp.float32) * QSCALE
    t = jnp.tanh(s / CAP)
    capped = CAP * t
    expo = jnp.where(mask[None], jnp.exp(capped), jnp.float32(0.0))
    weights = expo / jnp.sum(expo, axis=-1, keepdims=True)
    weights16 = weights.astype(jnp.bfloat16)
    attended = jnp.einsum("gij,jd->igd", weights16, v_head, preferred_element_type=jnp.float32)
    dweight = jnp.einsum("igd,jd->gij", g_head, v_head, preferred_element_type=jnp.float32)
    delta = jnp.sum(g_head.astype(jnp.float32) * attended, axis=-1).T
    dscore = (weights * (dweight - delta[..., None]) * (1.0 - t * t) * QSCALE).astype(jnp.bfloat16)
    query_gradient = jnp.einsum(
        "gij,jd->igd", dscore, k_head, preferred_element_type=jnp.float32
    ).astype(jnp.bfloat16)
    value_gradient = jnp.einsum(
        "gij,igd->jd", weights16, g_head, preferred_element_type=jnp.float32
    )
    return (query_gradient, value_gradient)


def partial_attend(mask):

    def run_head(operands):
        return attend_head(operands, mask)

    return run_head


def on_device(
    tokens,
    trace_index,
    input_norm_scale,
    query_weight,
    key_weight,
    value_weight,
    query_down_weight,
    query_up_weight,
    value_down_weight,
    value_up_weight,
    output_gradient,
):
    window_width = tokens.shape[1]
    feats = tokens.shape[2]
    heads_kv = key_weight.shape[1] // HEAD_SIZE
    heads_q = query_weight.shape[1] // HEAD_SIZE
    head_group = heads_q // heads_kv
    normalized_input = normed_rows(tokens.reshape(window_width, feats), input_norm_scale)
    seg_own = trace_index.reshape(window_width).astype(jnp.bfloat16)
    seg_parts = []

    def add_keyval(piece):
        return add_rows(normalized_input, piece)

    query_frozen = add_rows(
        normalized_input, lax.all_gather(query_weight, "fsdp", axis=0, tiled=True)
    )
    k_base = add_keyval(lax.all_gather(key_weight, "fsdp", axis=0, tiled=True))
    value_frozen = add_keyval(lax.all_gather(value_weight, "fsdp", axis=0, tiled=True))
    query_reduced = jnp.dot(
        normalized_input, query_down_weight, preferred_element_type=jnp.float32
    ).astype(jnp.bfloat16)
    reduced_rows = jnp.dot(
        normalized_input, value_down_weight, preferred_element_type=jnp.float32
    ).astype(jnp.bfloat16)
    query_matrix = (
        query_frozen
        + ADAPTER_NAME * jnp.dot(query_reduced, query_up_weight, preferred_element_type=jnp.float32)
    ).astype(jnp.bfloat16)
    key_rows = k_base.astype(jnp.bfloat16)
    value_rows = (
        value_frozen
        + ADAPTER_NAME * jnp.dot(reduced_rows, value_up_weight, preferred_element_type=jnp.float32)
    ).astype(jnp.bfloat16)
    key_parts = []
    value_parts = []
    for distance in (2, 1):
        key_prev, value_prev, seg_prev = shifted((key_rows, value_rows, seg_own), "ctx", distance)
        key_parts.append(key_prev)
        value_parts.append(value_prev)
        seg_parts.append(seg_prev)
    keys_all = jnp.concatenate(key_parts + [key_rows], 0)
    values_all = jnp.concatenate(value_parts + [value_rows], 0)
    seg_keys = jnp.concatenate(seg_parts + [seg_own], 0)
    pos_q = jnp.arange(window_width, dtype=jnp.int32)[:, None]
    pos_k = jnp.arange(3 * window_width, dtype=jnp.int32)[None, :]
    position = lax.axis_index("ctx")
    mask = (
        (pos_k > pos_q)
        & (pos_k <= pos_q + 2 * window_width)
        & (seg_keys[None, :] == seg_own[:, None])
    )
    mask = mask & (
        (pos_k >= 2 * window_width) | (pos_k >= window_width) & (position >= 1) | (position >= 2)
    )
    q_heads = jnp.moveaxis(
        query_matrix.reshape(window_width, heads_kv, head_group, HEAD_SIZE), 1, 0
    )
    g_heads = jnp.moveaxis(
        output_gradient.reshape(window_width, heads_kv, head_group, HEAD_SIZE), 1, 0
    )
    k_heads = jnp.moveaxis(keys_all.reshape(3 * window_width, heads_kv, HEAD_SIZE), 1, 0)
    v_heads = jnp.moveaxis(values_all.reshape(3 * window_width, heads_kv, HEAD_SIZE), 1, 0)
    dquery_heads, dvalue_heads = lax.map(partial_attend(mask), (q_heads, k_heads, v_heads, g_heads))
    query_gradient = jnp.moveaxis(dquery_heads, 0, 1).reshape(window_width, heads_q * HEAD_SIZE)
    dvalue_triple = jnp.moveaxis(dvalue_heads, 0, 1).reshape(3 * window_width, heads_kv * HEAD_SIZE)
    value_gradient = dvalue_triple[2 * window_width :]
    for distance in (1, 2):
        begin = (2 - distance) * window_width
        value_gradient = value_gradient + shifted(
            dvalue_triple[begin : begin + window_width], "ctx", -distance
        )
    query_backward = jnp.dot(
        query_gradient, query_up_weight.T, preferred_element_type=jnp.float32
    ).astype(jnp.bfloat16)
    value_backward = jnp.dot(
        value_gradient, value_up_weight.astype(jnp.float32).T, precision=lax.Precision.HIGHEST
    )
    part_aq = jnp.dot(normalized_input.T, query_backward, preferred_element_type=jnp.float32)
    part_bq = jnp.dot(query_reduced.T, query_gradient, preferred_element_type=jnp.float32)
    part_av = jnp.dot(
        normalized_input.astype(jnp.float32).T, value_backward, precision=lax.Precision.HIGHEST
    )
    part_bv = jnp.dot(
        reduced_rows.astype(jnp.float32).T, value_gradient, precision=lax.Precision.HIGHEST
    )
    sum_aq, sum_bq, sum_av, sum_bv = lax.psum((part_aq, part_bq, part_av, part_bv), ("ctx", "fsdp"))
    token_total = lax.axis_size("ctx") * lax.axis_size("fsdp") * window_width
    coefficient = ADAPTER_NAME / math.sqrt(token_total)
    return (sum_aq * coefficient, sum_bq * coefficient, sum_av * coefficient, sum_bv * coefficient)


F32 = jnp.float32
BF16 = jnp.bfloat16
PLANE = 8


def dot(a, b, dims=((1,), (0,))):
    return lax.dot_general(a, b, (dims, ((), ())), preferred_element_type=F32)


def plane_kernel(
    chain, coefficient,
    raw, seg, gain_in, wq, wk, wv, qd, qu_in, vd, vu_in, grad,
    OUTA, OUTV,
    N, M, WA, WV, G, SG, acc, accv, P, C, K, DQ, DV, LL,
    gain, down, qu, vu,
    PQ, PV, RSA, RSV, TA, TV,
    local_sem, w_send, w_recv, t_send, t_recv, g_sem, s_sem,
    up_send, up_recv, down_send, down_recv, vup_send, vup_recv, vdown_send, vdown_recv,
    q1_send, q1_recv, v1_send, v1_recv, a_sem, v_sem,
):
    x = lax.axis_index("ctx")
    f = lax.axis_index("fsdp")
    z = f // 4
    y = (f // 2) % 2
    c = f % 2
    tok, feats = raw.shape
    rows = wq.shape[0]
    qcols = wq.shape[1] // PLANE
    kcols = wk.shape[1] // PLANE
    acols = qcols + kcols
    piece = feats // PLANE
    seq = 2 * tok
    sub = tok // 4
    heads = qcols // kcols
    ranks = qd.shape[0]
    middle = (z > 0) & (z < chain - 1)
    outer = (z == 0) | (z == chain - 1)

    def coords(r):
        px = 1 - x if r & 4 else x
        py = 1 - y if r & 2 else y
        pc = 1 - c if r & 1 else c
        return px, py, pc

    def head_of(r):
        px, py, pc = coords(r)
        return (px * 2 + py) * 2 + pc

    def peer(r):
        px, py, pc = coords(r)
        return {"ctx": px, "fsdp": (z * 2 + py) * 2 + pc}

    def above(pz):
        return {"ctx": x, "fsdp": (pz * 2 + y) * 2 + c}

    def tok_slot(r):
        px, py, pc = coords(r)
        return (py * 2 + pc) * 2 + px

    def tok_piece(r, low, count):
        begin = tok_slot(r) * tok + low * sub
        return pl.ds(pl.multiple_of(begin, sub), count * sub)

    def tok_rows(r):
        return pl.ds(pl.multiple_of(tok_slot(r) * tok, tok), tok)

    def remote(src, dst, send, recv, device):
        return pltpu.make_async_remote_copy(
            src_ref=src, dst_ref=dst, send_sem=send, recv_sem=recv,
            device_id=device, device_id_type=pl.DeviceIdType.MESH,
        )

    barrier = pltpu.get_barrier_semaphore()
    for r in range(1, PLANE):
        pl.semaphore_signal(barrier, inc=1, device_id=peer(r), device_id_type=pl.DeviceIdType.MESH)
    for d in range(1, chain):
        pl.semaphore_signal(
            barrier, inc=1, device_id=above((z + d) % chain), device_id_type=pl.DeviceIdType.MESH
        )

    def w_rows(r):
        px, py, pc = coords(r)
        return pl.ds(pl.multiple_of(((z * 2 + py) * 2 + pc) * rows, rows), rows)

    def w_parts(r):
        h = head_of(r)
        own = w_rows(0)
        return (
            (wq.at[:, pl.ds(pl.multiple_of(h * qcols, qcols), qcols)], WA.at[own, pl.ds(0, qcols)]),
            (wk.at[:, pl.ds(pl.multiple_of(h * kcols, kcols), kcols)], WA.at[own, pl.ds(qcols, kcols)]),
            (wv.at[:, pl.ds(pl.multiple_of(h * kcols, kcols), kcols)], WV.at[own]),
        )

    def g_cols(r):
        h = head_of(r)
        return grad.at[:, pl.ds(pl.multiple_of(h * qcols, qcols), qcols)]

    local = [pltpu.make_async_copy(a, b, local_sem.at[i]) for i, (a, b) in enumerate(w_parts(0))]
    local.append(pltpu.make_async_copy(raw, N.at[tok_rows(0)], local_sem.at[3]))
    local.append(pltpu.make_async_copy(g_cols(0), G.at[tok_rows(0)], local_sem.at[4]))
    local.append(pltpu.make_async_copy(seg, SG.at[tok_slot(0)], local_sem.at[5]))
    local.append(pltpu.make_async_copy(qd, down.at[pl.ds(0, ranks)], local_sem.at[6]))
    local.append(pltpu.make_async_copy(vd, down.at[pl.ds(ranks, ranks)], local_sem.at[7]))
    local.append(pltpu.make_async_copy(qu_in, qu, local_sem.at[8]))
    local.append(pltpu.make_async_copy(vu_in, vu, local_sem.at[9]))
    local.append(pltpu.make_async_copy(gain_in, gain, local_sem.at[10]))
    for copy in local:
        copy.start()
    for i in range(2):
        local[i].wait()
    pl.semaphore_wait(barrier, PLANE - 1 + chain - 1)

    def half_rows(plane, half):
        py = y if half == 0 else 1 - y
        return pl.ds(pl.multiple_of((plane * 4 + py * 2) * rows, 2 * rows), 2 * rows)

    def quarter_rows(plane, quarter):
        px, py, pc = coords(quarter)
        return pl.ds(pl.multiple_of((plane * 4 + py * 2 + pc) * rows, rows), rows)

    def has_up(t):
        return (z < chain - 1) & (z - t >= 0)

    def has_down(t):
        return (z > 0) & (z + t <= chain - 1)

    def from_below(t):
        return z - 1 - t >= 0

    def from_above(t):
        return z + 1 + t <= chain - 1

    def pieces_of(t):
        return range(4) if t == 0 else range(2)

    def piece_rows(plane, t, i):
        return quarter_rows(plane, i) if t == 0 else half_rows(plane, i)

    def half_of(t, i):
        return i // 2 if t == 0 else i

    def plane_rows(plane):
        return pl.ds(pl.multiple_of(plane * 4 * rows, 4 * rows), 4 * rows)

    def up_copy(t, i):
        at = WA.at[piece_rows(z - t, t, i)]
        return remote(at, at, up_send.at[t], up_recv.at[t, half_of(t, i)], above(z + 1))

    def down_copy(t, i):
        at = WA.at[piece_rows(z + t, t, i)]
        return remote(at, at, down_send.at[t], down_recv.at[t, half_of(t, i)], above(z - 1))

    def up_arrival(t, half):
        at = WA.at[half_rows(z - 1 - t, half)]
        return remote(at, at, up_send.at[t], up_recv.at[t, half], above(z - 1))

    def down_arrival(t, half):
        at = WA.at[half_rows(z + 1 + t, half)]
        return remote(at, at, down_send.at[t], down_recv.at[t, half], above(z + 1))

    def vup_copy(t, half):
        at = WV.at[half_rows(z - t, half)]
        return remote(at, at, vup_send.at[t], vup_recv.at[t, half], above(z + 1))

    def vdown_copy(t, half):
        at = WV.at[half_rows(z + t, half)]
        return remote(at, at, vdown_send.at[t], vdown_recv.at[t, half], above(z - 1))

    def vup_arrival(t, half):
        at = WV.at[half_rows(z - 1 - t, half)]
        return remote(at, at, vup_send.at[t], vup_recv.at[t, half], above(z - 1))

    def vdown_arrival(t, half):
        at = WV.at[half_rows(z + 1 + t, half)]
        return remote(at, at, vdown_send.at[t], vdown_recv.at[t, half], above(z + 1))

    def send_chain(t, i):
        @pl.when(has_up(t))
        def _():
            up_copy(t, i).start()

        @pl.when(has_down(t))
        def _():
            down_copy(t, i).start()

    def recv_half(t, half):
        @pl.when(from_below(t))
        def _():
            up_arrival(t, half).wait_recv()

        @pl.when(from_above(t))
        def _():
            down_arrival(t, half).wait_recv()

    def send_value_first(k):
        @pl.when(has_up(k - 1) & jnp.logical_not(has_up(k)))
        def _():
            for half in range(2):
                vup_copy(0, half).start()

        @pl.when(has_down(k - 1) & jnp.logical_not(has_down(k)))
        def _():
            for half in range(2):
                vdown_copy(0, half).start()

    def send_value(t, half):
        @pl.when(has_up(t))
        def _():
            vup_copy(t, half).start()

        @pl.when(has_down(t))
        def _():
            vdown_copy(t, half).start()

    def recv_value(t, half):
        @pl.when(from_below(t))
        def _():
            vup_arrival(t, half).wait_recv()

        @pl.when(from_above(t))
        def _():
            vdown_arrival(t, half).wait_recv()

    w_copies = {}
    for r in (1, 2, 3):
        w_copies[r] = [
            remote(a, b, w_send.at[i // 2], w_recv.at[r if i < 2 else 0], peer(r))
            for i, (a, b) in enumerate(w_parts(r))
        ]
    send_chain(0, 0)
    for r in (1, 2, 3):
        for i in range(2):
            w_copies[r][i].start()
    for r in (1, 2, 3):
        w_copies[r][2].start()

    t_slot = {(1, 0): 0, (4, 3): 1, (4, 0): 2, (5, 0): 3, (3, 0): 4, (7, 0): 5}
    for low in range(4):
        t_slot[2, low] = 6 + low
        t_slot[6, low] = 10

    def send_token(r_mine, r_there, hop, low=0, count=4):
        at = N.at[tok_piece(r_mine, low, count)]
        source = raw.at[pl.ds(low * sub, count * sub)] if r_mine == 0 else at
        remote(source, at, t_send.at[0], t_recv.at[t_slot[r_there, low]], peer(hop)).start()

    def wait_token(r, low=0, count=4):
        at = N.at[tok_piece(r, low, count)]
        remote(at, at, t_send.at[0], t_recv.at[t_slot[r, low]], peer(1)).wait_recv()

    send_token(0, 1, 1)
    send_token(0, 4, 4, 3, 1)
    send_token(0, 4, 4, 0, 3)
    for low in range(4):
        send_token(0, 2, 2, low, 1)
    g_copies = {}
    s_copies = {}
    for r in range(1, PLANE):
        g_copies[r] = remote(g_cols(r), G.at[tok_rows(0)], g_sem.at[0], g_sem.at[1], peer(r))
        s_copies[r] = remote(seg, SG.at[tok_slot(0)], s_sem.at[0], s_sem.at[1], peer(r))

    def wait_weight(r):
        ref = WA.at[w_rows(r)]
        remote(ref, ref, w_send.at[0], w_recv.at[r], peer(r)).wait_recv()

    def wait_values():
        ref = WV.at[pl.ds(0, 3 * rows)]
        remote(ref, ref, w_send.at[1], w_recv.at[0], peer(1)).wait_recv()

    part_rows = 4 * tok

    def part_at(part, i, height):
        py = y if part == 0 else 1 - y
        return pl.ds(pl.multiple_of(py * part_rows + i * height, height), height)

    h = head_of(0)

    def query_up():
        return qu[:, pl.ds(pl.multiple_of(h * qcols, qcols), qcols)]

    def value_up():
        return vu[:, pl.ds(pl.multiple_of(h * kcols, kcols), kcols)]

    def prepare(r):
        height = tok // 2

        @pl.loop(0, 2)
        def _(i):
            begin = tok_slot(r) * tok + i * height
            at = pl.ds(pl.multiple_of(begin, height), height)
            flt = N[at, :].astype(F32)
            meansq = jnp.sum(flt * flt, axis=-1, keepdims=True) / feats
            M[at, :] = (flt * lax.rsqrt(meansq + EPS) * gain[...].astype(F32).reshape(1, feats)).astype(BF16)

        at = tok_rows(r)
        block = M[at, :]
        low = dot(block, down[...], ((1,), (1,))).astype(BF16)
        LL[at, :] = low
        filler = jnp.zeros((ranks, qcols), BF16)
        acc[at, 0:qcols] = ADAPTER_NAME * dot(low, jnp.concatenate([query_up(), filler], axis=0))
        acc[at, qcols:] = jnp.zeros((tok, kcols), F32)
        accv[at, :] = ADAPTER_NAME * dot(low, jnp.concatenate([filler[:, 0:kcols], value_up()], axis=0))

    def add_piece(plane, half, part):
        chosen = half_rows(plane, half)

        @pl.loop(0, part_rows // seq)
        def _(i):
            at = part_at(part, i, seq)
            acc[at, :] = acc[at, :] + dot(M[at, chosen], WA[chosen, :])

    def add_near(part):
        low = jnp.maximum(z - 2, 0)
        high = jnp.minimum(z + 2, chain - 1)
        for count in range(3, min(chain, 5) + 1):
            @pl.when(high - low == count - 1)
            def _():
                chosen = pl.ds(pl.multiple_of(low * 4 * rows, 4 * rows), count * 4 * rows)

                @pl.loop(0, part_rows // seq)
                def _(i):
                    at = part_at(part, i, seq)
                    acc[at, :] = acc[at, :] + dot(M[at, chosen], WA[chosen, :])

    def add_step(t, half, part):
        @pl.when(from_below(t))
        def _():
            add_piece(z - 1 - t, half, part)

        @pl.when(from_above(t))
        def _():
            add_piece(z + 1 + t, half, part)

    def add_value_piece(plane, half):
        chosen = plane_rows(plane) if half is None else half_rows(plane, half)

        @pl.loop(0, 2 * part_rows // seq)
        def _(i):
            at = pl.ds(pl.multiple_of(i * seq, seq), seq)
            accv[at, :] = accv[at, :] + dot(M[at, chosen], WV[chosen, :])

    def add_value(t, half):
        @pl.when(from_below(t))
        def _():
            add_value_piece(z - 1 - t, half)

        @pl.when(from_above(t))
        def _():
            add_value_piece(z + 1 + t, half)

    wait_weight(1)
    send_chain(0, 1)
    for r in range(1, PLANE):
        s_copies[r].start()
    local[3].wait()
    for i in range(6, 11):
        local[i].wait()
    prepare(0)
    wait_token(1)
    prepare(1)
    wait_weight(2)
    send_chain(0, 2)
    wait_weight(3)
    send_chain(0, 3)
    recv_half(0, 0)
    send_chain(1, 0)
    wait_token(2, 0, 1)
    send_token(2, 6, 4, 0, 1)
    recv_half(0, 1)
    send_chain(1, 1)
    local[2].wait()
    wait_values()
    send_value_first(1)
    wait_token(2, 1, 1)
    send_token(2, 6, 4, 1, 1)
    wait_token(4, 3, 1)
    send_token(4, 6, 2, 3, 1)
    wait_token(4, 0, 3)
    send_token(4, 5, 1)
    prepare(4)
    wait_token(2, 2, 1)
    send_token(2, 6, 4, 2, 1)
    for r in (6, 7, 4, 5, 2, 3, 1):
        g_copies[r].start()
    wait_token(5)
    prepare(5)
    recv_half(1, 0)
    send_chain(2, 0)
    wait_token(2, 3, 1)
    send_token(2, 3, 1)
    prepare(2)
    wait_token(3)
    prepare(3)
    recv_half(1, 1)
    send_chain(2, 1)
    for k in range(2, chain):
        send_value_first(k)
    add_near(0)
    wait_token(6)
    send_token(6, 7, 1)
    prepare(6)
    wait_token(7)
    prepare(7)

    @pl.when(middle)
    def _():
        for half in range(2):
            recv_value(0, half)
            send_value(1, half)

    add_near(1)
    add_value_piece(z, None)
    for t in range(2, chain - 1):
        for half in range(2):
            recv_half(t, half)
            if t + 1 < chain - 1:
                send_chain(t + 1, half)
            for part in range(2):
                add_step(t, half, part)

    tiles = PLANE * tok // seq
    local[4].wait()
    local[5].wait()
    g_others = G.at[pl.ds(0, (PLANE - 1) * tok)]
    g_all_copies = remote(g_others, g_others, g_sem.at[0], g_sem.at[1], peer(1))
    g_all_copies.wait_recv()
    s_others = SG.at[pl.ds(0, PLANE - 1)]
    s_all_copies = remote(s_others, s_others, s_sem.at[0], s_sem.at[1], peer(1))
    s_all_copies.wait_recv()

    pos_i = lax.broadcasted_iota(jnp.int32, (seq, seq), 0)
    pos_j = lax.broadcasted_iota(jnp.int32, (seq, seq), 1)
    band = (pos_j <= pos_i) & (pos_j > pos_i - 2 * tok)

    @pl.loop(0, tiles, unroll=2)
    def _(i):
        at = pl.ds(pl.multiple_of(i * seq, seq), seq)
        q_all = acc[at, 0:qcols].astype(BF16)
        k = acc[at, qcols:].astype(BF16)
        K[at, :] = k
        g_all = G[at, :]
        traces = [SG[2 * i].astype(F32), SG[2 * i + 1].astype(F32)]
        along = jnp.concatenate(traces, axis=1)
        turned = [jnp.broadcast_to(own, (tok, tok)).T for own in traces]
        across = jnp.concatenate([jnp.concatenate([own, own], axis=1) for own in turned], axis=0)
        mask = band & (across == along)
        dv = jnp.zeros((seq, kcols), F32)
        for n in range(heads):
            q = q_all[:, n * kcols:(n + 1) * kcols]
            g = g_all[:, n * kcols:(n + 1) * kcols]
            t = jnp.tanh(dot(q, k, ((1,), (1,))) * (QSCALE / CAP))
            expo = jnp.where(mask, jnp.exp(CAP * t), 0.0)
            weights = expo * (1.0 / jnp.sum(expo, axis=-1, keepdims=True))
            weights16 = weights.astype(BF16)
            P[i * heads + n] = weights16
            C[i * heads + n] = weights * (1.0 - t * t)
            dv = dv + dot(weights16, g, ((0,), (0,)))
        DV[at, :] = dv.astype(BF16)

    @pl.when(middle)
    def _():
        for t in range(1, chain - 1):
            for half in range(2):
                recv_value(t, half)
                if t + 1 < chain - 1:
                    send_value(t + 1, half)

    half_tokens = PLANE * tok // 2

    def token_half(half):
        return pl.ds(half * half_tokens, half_tokens)

    def send_pull(half, up, change, gathered, send, recv):
        own = gathered.at[half, h]
        own[...] = dot(up, change[token_half(half), :], ((1,), (1,))).astype(BF16)
        for r in (7, 6, 5, 4, 3, 2, 1):
            remote(own, own, send.at[half], recv.at[half], peer(r)).start()

    def pulls(half, gathered, send, recv):
        at = gathered.at[half, pl.ds(0, PLANE - 1)]
        return remote(at, at, send.at[half], recv.at[half], peer(1))

    def down_gradient(columns, width, gathered, send, recv):
        total = jnp.zeros((ranks, width), F32)
        for half in range(2):
            pulls(half, gathered, send, recv).wait_recv()
            pull = gathered[half, 0].astype(F32)
            for r in range(1, PLANE):
                pull = pull + gathered[half, r].astype(F32)
            total = total + dot(pull.astype(BF16), M[token_half(half), columns])
        return total.astype(BF16)

    def share(sums, sem):
        own = sums.at[z]
        for d in range(1, chain):
            remote(own, own, sem.at[0], sem.at[1], above((z + d) % chain)).start()

    def shares(sums, sem):
        at = sums.at[pl.ds(0, chain - 1)]
        return remote(at, at, sem.at[0], sem.at[1], peer(1))

    def shared(sums):
        total = sums[0].astype(F32)
        for d in range(1, chain):
            total = total + sums[d].astype(F32)
        return (total * coefficient).astype(BF16)

    def spread(total, mine, out, sem):
        mine[...] = total
        for r in (7, 6, 5, 4, 3, 2, 1):
            remote(mine, out.at[h], sem.at[2], sem.at[3], peer(r)).start()
        out[h] = total

    def spreads(out, sem):
        at = out.at[pl.ds(0, PLANE - 1)]
        return remote(at, at, sem.at[2], sem.at[3], peer(1))

    for half in range(2):
        send_pull(half, value_up(), DV, PV, v1_send, v1_recv)
    low_gradient = dot(LL[...], DV[...], ((0,), (0,)))
    RSV.at[z][:, piece:piece + kcols] = low_gradient[ranks:, :].astype(BF16)
    for t in range(chain - 2):
        @pl.when(outer)
        def _():
            for half in range(2):
                recv_value(t, half)

        add_value(t, None)
    own_columns = pl.ds(pl.multiple_of(h * piece, piece), piece)
    RSV.at[z][:, 0:piece] = down_gradient(own_columns, piece, PV, v1_send, v1_recv)
    for half in range(2):
        @pl.when(outer)
        def _():
            recv_value(chain - 2, half)

        add_value(chain - 2, half)

    for half in range(2):
        for i in range(half * tiles // 2, (half + 1) * tiles // 2):
            at = pl.ds(i * seq, seq)
            v = accv[at, :].astype(BF16)
            k = K[at, :]
            for n in range(heads):
                g = G[at, n * kcols:(n + 1) * kcols]
                dweight = dot(g, v, ((1,), (1,)))
                delta = jnp.sum(P[i * heads + n].astype(F32) * dweight, axis=-1, keepdims=True)
                dscore = (C[i * heads + n] * (dweight - delta)).astype(BF16)
                DQ[at, n * kcols:(n + 1) * kcols] = (dot(dscore, k) * QSCALE).astype(BF16)
        send_pull(half, query_up(), DQ, PQ, q1_send, q1_recv)

    low_gradient = dot(LL[...], DQ[...], ((0,), (0,)))
    RSV.at[z][:, piece + kcols:] = low_gradient[0:ranks, :].astype(BF16)
    share(RSV, v_sem)
    width = feats // 2
    core_columns = pl.ds(pl.multiple_of(c * width, width), width)
    RSA[z] = down_gradient(core_columns, width, PQ, q1_send, q1_recv)
    share(RSA, a_sem)
    shares(RSV, v_sem).wait_recv()
    spread(shared(RSV), TV, OUTV, v_sem)
    shares(RSA, a_sem).wait_recv()
    TA[...] = shared(RSA)
    core_copy = remote(TA, OUTA.at[c], a_sem.at[2], a_sem.at[3], peer(1))
    core_copy.start()
    OUTA[c] = TA[...]
    spreads(OUTV, v_sem).wait_recv()
    at = OUTA.at[1 - c]
    remote(at, at, a_sem.at[2], a_sem.at[3], peer(1)).wait_recv()

    at = WA.at[pl.ds(0, 3 * rows)]
    remote(at, at, w_send.at[0], w_recv.at[1], peer(1)).wait_send()
    at = WV.at[pl.ds(0, 3 * rows)]
    remote(at, at, w_send.at[1], w_recv.at[0], peer(1)).wait_send()
    at = N.at[pl.ds(0, (PLANE - 1) * tok)]
    remote(at, at, t_send.at[0], t_recv.at[0], peer(1)).wait_send()
    g_all_copies.wait_send()
    s_all_copies.wait_send()
    for t in range(chain - 1):
        @pl.when(has_up(t))
        def _():
            at = WA.at[plane_rows(z - t)]
            remote(at, at, up_send.at[t], up_recv.at[t, 0], above(z + 1)).wait_send()
            at = WV.at[plane_rows(z - t)]
            remote(at, at, vup_send.at[t], vup_recv.at[t, 0], above(z + 1)).wait_send()

        @pl.when(has_down(t))
        def _():
            at = WA.at[plane_rows(z + t)]
            remote(at, at, down_send.at[t], down_recv.at[t, 0], above(z - 1)).wait_send()
            at = WV.at[plane_rows(z + t)]
            remote(at, at, vdown_send.at[t], vdown_recv.at[t, 0], above(z - 1)).wait_send()
    for half in range(2):
        pulls(half, PV, v1_send, v1_recv).wait_send()
        pulls(half, PQ, q1_send, q1_recv).wait_send()
    for sums, sem in ((RSV, v_sem), (RSA, a_sem)):
        shares(sums, sem).wait_send()
    spreads(OUTV, v_sem).wait_send()
    core_copy.wait_send()


def unpack_kernel(outa, outv, out_aq, out_bq, out_av, out_bv):
    feats = out_aq.shape[1]
    piece = feats // PLANE
    qcols = out_bq.shape[1] // PLANE
    kcols = out_bv.shape[1] // PLANE
    for core in range(2):
        out_aq[:, core * feats // 2:(core + 1) * feats // 2] = outa[core].astype(F32)
    for h in range(PLANE):
        value = outv[h].astype(F32)
        out_bq[:, h * qcols:(h + 1) * qcols] = value[:, piece + kcols:]
        out_av[:, h * piece:(h + 1) * piece] = value[:, 0:piece]
        out_bv[:, h * kcols:(h + 1) * kcols] = value[:, piece:piece + kcols]


def on_plane(
    tokens,
    trace_index,
    input_norm_scale,
    query_weight,
    key_weight,
    value_weight,
    query_down_weight,
    query_up_weight,
    value_down_weight,
    value_up_weight,
    output_gradient,
):
    tok = tokens.shape[1]
    feats = tokens.shape[2]
    fsdp = lax.axis_size("fsdp")
    chain = fsdp // 4
    ranks = query_down_weight.shape[1]
    qcols = query_weight.shape[1] // PLANE
    kcols = key_weight.shape[1] // PLANE
    piece = feats // PLANE
    many = PLANE * tok
    token_total = lax.axis_size("ctx") * fsdp * tok
    coefficient = ADAPTER_NAME / math.sqrt(token_total)
    hbm = pl.BlockSpec(memory_space=pltpu.HBM)
    vmem = pl.BlockSpec(memory_space=pltpu.VMEM)
    dma = pltpu.SemaphoreType.DMA
    steps = chain - 1
    tiles = many // (2 * tok)
    heads = qcols // kcols
    outa, outv = pl.pallas_call(
        functools.partial(plane_kernel, chain, coefficient),
        out_shape=(
            pltpu.VMEM((2, ranks, feats // 2), BF16),
            pltpu.VMEM((PLANE, ranks, piece + kcols + qcols), BF16),
        ),
        in_specs=[hbm] * 11,
        out_specs=(vmem, vmem),
        scratch_shapes=[
            pltpu.VMEM((many, feats), BF16),
            pltpu.VMEM((many, feats), BF16),
            pltpu.VMEM((feats, qcols + kcols), BF16),
            pltpu.VMEM((feats, kcols), BF16),
            pltpu.VMEM((many, qcols), BF16),
            pltpu.VMEM((PLANE, 1, tok), jnp.int32),
            pltpu.VMEM((many, qcols + kcols), F32),
            pltpu.VMEM((many, kcols), F32),
            pltpu.VMEM((tiles * heads, 2 * tok, 2 * tok), BF16),
            pltpu.VMEM((tiles * heads, 2 * tok, 2 * tok), F32),
            pltpu.VMEM((many, kcols), BF16),
            pltpu.VMEM((many, qcols), BF16),
            pltpu.VMEM((many, kcols), BF16),
            pltpu.VMEM((many, 2 * ranks), BF16),
            pltpu.VMEM((feats,), BF16),
            pltpu.VMEM((2 * ranks, feats), BF16),
            pltpu.VMEM((ranks, query_weight.shape[1]), BF16),
            pltpu.VMEM((ranks, value_weight.shape[1]), BF16),
            pltpu.VMEM((2, PLANE, ranks, many // 2), BF16),
            pltpu.VMEM((2, PLANE, ranks, many // 2), BF16),
            pltpu.VMEM((chain, ranks, feats // 2), BF16),
            pltpu.VMEM((chain, ranks, piece + kcols + qcols), BF16),
            pltpu.VMEM((ranks, feats // 2), BF16),
            pltpu.VMEM((ranks, piece + kcols + qcols), BF16),
            dma((11,)),
            dma((2,)), dma((4,)), dma((1,)), dma((11,)), dma((2,)), dma((2,)),
            dma((steps,)), dma((steps, 2)), dma((steps,)), dma((steps, 2)),
            dma((steps,)), dma((steps, 2)), dma((steps,)), dma((steps, 2)),
            dma((2,)), dma((2,)), dma((2,)), dma((2,)), dma((4,)), dma((4,)),
        ],
        compiler_params=pltpu.CompilerParams(
            collective_id=0, has_side_effects=True, vmem_limit_bytes=56 * 1024 * 1024
        ),
    )(
        tokens.reshape(tok, feats), trace_index, input_norm_scale,
        query_weight, key_weight, value_weight,
        query_down_weight.T, query_up_weight, value_down_weight.T, value_up_weight,
        output_gradient.reshape(tok, output_gradient.shape[2]),
    )
    aq, bq, av, bv = pl.pallas_call(
        unpack_kernel,
        out_shape=(
            jax.ShapeDtypeStruct((ranks, feats), F32),
            jax.ShapeDtypeStruct((ranks, query_weight.shape[1]), F32),
            jax.ShapeDtypeStruct((ranks, feats), F32),
            jax.ShapeDtypeStruct((ranks, value_weight.shape[1]), F32),
        ),
        in_specs=[vmem, vmem],
        out_specs=(vmem, vmem, vmem, vmem),
        compiler_params=pltpu.CompilerParams(vmem_limit_bytes=16 * 1024 * 1024),
    )(outa, outv)
    return (aq.T, bq, av.T, bv)


def solution(mesh):
    shape = mesh.shape
    planes = shape["groups"] == 1 and shape["ctx"] == 2 and shape["fsdp"] % 4 == 0 and shape["fsdp"] > 8
    return jax.shard_map(
        on_plane if planes else on_device,
        mesh=mesh,
        in_specs=(
            P(("groups", "fsdp"), "ctx", None),
            P(("groups", "fsdp"), "ctx"),
            P(),
            P("fsdp", None),
            P("fsdp", None),
            P("fsdp", None),
            P(),
            P(),
            P(),
            P(),
            P(("groups", "fsdp"), "ctx", None),
        ),
        out_specs=(P("groups", None), P("groups", None), P("groups", None), P("groups", None)),
        check_vma=False,
    )
```

```python
import functools
import math

import jax
import jax.numpy as jnp
from jax import lax
from jax.experimental import pallas as pl
from jax.experimental.pallas import tpu as pltpu
from jax.sharding import PartitionSpec as P

HEAD_SIZE = 128


CAP = 50.0
QSCALE = 1.0 / 12.0
ADAPTER_NAME = 0.5
EPS = 1e-06


def shifted(value, axis, by):
    devices = lax.axis_size(axis)
    pairs = [(i, i + by) for i in range(devices) if 0 <= i + by < devices]
    return lax.ppermute(value, axis, pairs)


def normed_rows(values, gain):
    flt = values.astype(jnp.float32)
    meansq = jnp.mean(flt * flt, axis=-1, keepdims=True)
    return (flt * lax.rsqrt(meansq + EPS) * gain.astype(jnp.float32)).astype(jnp.bfloat16)


def add_rows(left, piece):
    return jnp.dot(left, piece, preferred_element_type=jnp.float32)


def attend_head(operands, mask):
    q_head, k_head, v_head, g_head = operands
    s = jnp.einsum("igd,jd->gij", q_head, k_head, preferred_element_type=jnp.float32) * QSCALE
    t = jnp.tanh(s / CAP)
    capped = CAP * t
    expo = jnp.where(mask[None], jnp.exp(capped), jnp.float32(0.0))
    weights = expo / jnp.sum(expo, axis=-1, keepdims=True)
    weights16 = weights.astype(jnp.bfloat16)
    attended = jnp.einsum("gij,jd->igd", weights16, v_head, preferred_element_type=jnp.float32)
    dweight = jnp.einsum("igd,jd->gij", g_head, v_head, preferred_element_type=jnp.float32)
    delta = jnp.sum(g_head.astype(jnp.float32) * attended, axis=-1).T
    dscore = (weights * (dweight - delta[..., None]) * (1.0 - t * t) * QSCALE).astype(jnp.bfloat16)
    query_gradient = jnp.einsum(
        "gij,jd->igd", dscore, k_head, preferred_element_type=jnp.float32
    ).astype(jnp.bfloat16)
    value_gradient = jnp.einsum(
        "gij,igd->jd", weights16, g_head, preferred_element_type=jnp.float32
    )
    return (query_gradient, value_gradient)


def partial_attend(mask):

    def run_head(operands):
        return attend_head(operands, mask)

    return run_head


def on_device(
    tokens,
    trace_index,
    input_norm_scale,
    query_weight,
    key_weight,
    value_weight,
    query_down_weight,
    query_up_weight,
    value_down_weight,
    value_up_weight,
    output_gradient,
):
    window_width = tokens.shape[1]
    feats = tokens.shape[2]
    heads_kv = key_weight.shape[1] // HEAD_SIZE
    heads_q = query_weight.shape[1] // HEAD_SIZE
    head_group = heads_q // heads_kv
    normalized_input = normed_rows(tokens.reshape(window_width, feats), input_norm_scale)
    seg_own = trace_index.reshape(window_width).astype(jnp.bfloat16)
    seg_parts = []

    def add_keyval(piece):
        return add_rows(normalized_input, piece)

    query_frozen = add_rows(
        normalized_input, lax.all_gather(query_weight, "fsdp", axis=0, tiled=True)
    )
    k_base = add_keyval(lax.all_gather(key_weight, "fsdp", axis=0, tiled=True))
    value_frozen = add_keyval(lax.all_gather(value_weight, "fsdp", axis=0, tiled=True))
    query_reduced = jnp.dot(
        normalized_input, query_down_weight, preferred_element_type=jnp.float32
    ).astype(jnp.bfloat16)
    reduced_rows = jnp.dot(
        normalized_input, value_down_weight, preferred_element_type=jnp.float32
    ).astype(jnp.bfloat16)
    query_matrix = (
        query_frozen
        + ADAPTER_NAME * jnp.dot(query_reduced, query_up_weight, preferred_element_type=jnp.float32)
    ).astype(jnp.bfloat16)
    key_rows = k_base.astype(jnp.bfloat16)
    value_rows = (
        value_frozen
        + ADAPTER_NAME * jnp.dot(reduced_rows, value_up_weight, preferred_element_type=jnp.float32)
    ).astype(jnp.bfloat16)
    key_parts = []
    value_parts = []
    for distance in (2, 1):
        key_prev, value_prev, seg_prev = shifted((key_rows, value_rows, seg_own), "ctx", distance)
        key_parts.append(key_prev)
        value_parts.append(value_prev)
        seg_parts.append(seg_prev)
    keys_all = jnp.concatenate(key_parts + [key_rows], 0)
    values_all = jnp.concatenate(value_parts + [value_rows], 0)
    seg_keys = jnp.concatenate(seg_parts + [seg_own], 0)
    pos_q = jnp.arange(window_width, dtype=jnp.int32)[:, None]
    pos_k = jnp.arange(3 * window_width, dtype=jnp.int32)[None, :]
    position = lax.axis_index("ctx")
    mask = (
        (pos_k > pos_q)
        & (pos_k <= pos_q + 2 * window_width)
        & (seg_keys[None, :] == seg_own[:, None])
    )
    mask = mask & (
        (pos_k >= 2 * window_width) | (pos_k >= window_width) & (position >= 1) | (position >= 2)
    )
    q_heads = jnp.moveaxis(
        query_matrix.reshape(window_width, heads_kv, head_group, HEAD_SIZE), 1, 0
    )
    g_heads = jnp.moveaxis(
        output_gradient.reshape(window_width, heads_kv, head_group, HEAD_SIZE), 1, 0
    )
    k_heads = jnp.moveaxis(keys_all.reshape(3 * window_width, heads_kv, HEAD_SIZE), 1, 0)
    v_heads = jnp.moveaxis(values_all.reshape(3 * window_width, heads_kv, HEAD_SIZE), 1, 0)
    dquery_heads, dvalue_heads = lax.map(partial_attend(mask), (q_heads, k_heads, v_heads, g_heads))
    query_gradient = jnp.moveaxis(dquery_heads, 0, 1).reshape(window_width, heads_q * HEAD_SIZE)
    dvalue_triple = jnp.moveaxis(dvalue_heads, 0, 1).reshape(3 * window_width, heads_kv * HEAD_SIZE)
    value_gradient = dvalue_triple[2 * window_width :]
    for distance in (1, 2):
        begin = (2 - distance) * window_width
        value_gradient = value_gradient + shifted(
            dvalue_triple[begin : begin + window_width], "ctx", -distance
        )
    query_backward = jnp.dot(
        query_gradient, query_up_weight.T, preferred_element_type=jnp.float32
    ).astype(jnp.bfloat16)
    value_backward = jnp.dot(
        value_gradient, value_up_weight.astype(jnp.float32).T, precision=lax.Precision.HIGHEST
    )
    part_aq = jnp.dot(normalized_input.T, query_backward, preferred_element_type=jnp.float32)
    part_bq = jnp.dot(query_reduced.T, query_gradient, preferred_element_type=jnp.float32)
    part_av = jnp.dot(
        normalized_input.astype(jnp.float32).T, value_backward, precision=lax.Precision.HIGHEST
    )
    part_bv = jnp.dot(
        reduced_rows.astype(jnp.float32).T, value_gradient, precision=lax.Precision.HIGHEST
    )
    sum_aq, sum_bq, sum_av, sum_bv = lax.psum((part_aq, part_bq, part_av, part_bv), ("ctx", "fsdp"))
    token_total = lax.axis_size("ctx") * lax.axis_size("fsdp") * window_width
    coefficient = ADAPTER_NAME / math.sqrt(token_total)
    return (sum_aq * coefficient, sum_bq * coefficient, sum_av * coefficient, sum_bv * coefficient)


F32 = jnp.float32
BF16 = jnp.bfloat16
PLANE = 8


def dot(a, b, dims=((1,), (0,))):
    return lax.dot_general(a, b, (dims, ((), ())), preferred_element_type=F32)


def plane_kernel(
    chain, coefficient,
    raw, seg, gain_in, wq, wk, wv, qd, qu_in, vd, vu_in, grad,
    OUTA, OUTV,
    N, M, WA, WV, G, SG, acc, accv, P, C, K, DQ, DV, LL,
    gain, down, qu, vu,
    PQ, PV, RSA, RSV, TA, TV,
    local_sem, w_send, w_recv, t_send, t_recv, g_sem, s_sem,
    up_send, up_recv, down_send, down_recv, vup_send, vup_recv, vdown_send, vdown_recv,
    q1_send, q1_recv, v1_send, v1_recv, a_sem, v_sem,
):
    x = lax.axis_index("ctx")
    f = lax.axis_index("fsdp")
    z = f // 4
    y = (f // 2) % 2
    c = f % 2
    tok, feats = raw.shape
    rows = wq.shape[0]
    qcols = wq.shape[1] // PLANE
    kcols = wk.shape[1] // PLANE
    acols = qcols + kcols
    piece = feats // PLANE
    seq = 2 * tok
    sub = tok // 4
    heads = qcols // kcols
    ranks = qd.shape[0]
    middle = (z > 0) & (z < chain - 1)
    outer = (z == 0) | (z == chain - 1)

    def coords(r):
        px = 1 - x if r & 4 else x
        py = 1 - y if r & 2 else y
        pc = 1 - c if r & 1 else c
        return px, py, pc

    def head_of(r):
        px, py, pc = coords(r)
        return (px * 2 + py) * 2 + pc

    def peer(r):
        px, py, pc = coords(r)
        return {"ctx": px, "fsdp": (z * 2 + py) * 2 + pc}

    def above(pz):
        return {"ctx": x, "fsdp": (pz * 2 + y) * 2 + c}

    def tok_slot(r):
        px, py, pc = coords(r)
        return (py * 2 + pc) * 2 + px

    def tok_piece(r, low, count):
        begin = tok_slot(r) * tok + low * sub
        return pl.ds(pl.multiple_of(begin, sub), count * sub)

    def tok_rows(r):
        return pl.ds(pl.multiple_of(tok_slot(r) * tok, tok), tok)

    def remote(src, dst, send, recv, device):
        return pltpu.make_async_remote_copy(
            src_ref=src, dst_ref=dst, send_sem=send, recv_sem=recv,
            device_id=device, device_id_type=pl.DeviceIdType.MESH,
        )

    barrier = pltpu.get_barrier_semaphore()
    for r in range(1, PLANE):
        pl.semaphore_signal(barrier, inc=1, device_id=peer(r), device_id_type=pl.DeviceIdType.MESH)
    for d in range(1, chain):
        pl.semaphore_signal(
            barrier, inc=1, device_id=above((z + d) % chain), device_id_type=pl.DeviceIdType.MESH
        )

    def w_rows(r):
        px, py, pc = coords(r)
        return pl.ds(pl.multiple_of(((z * 2 + py) * 2 + pc) * rows, rows), rows)

    def w_parts(r):
        h = head_of(r)
        own = w_rows(0)
        return (
            (wq.at[:, pl.ds(pl.multiple_of(h * qcols, qcols), qcols)], WA.at[own, pl.ds(0, qcols)]),
            (wk.at[:, pl.ds(pl.multiple_of(h * kcols, kcols), kcols)], WA.at[own, pl.ds(qcols, kcols)]),
            (wv.at[:, pl.ds(pl.multiple_of(h * kcols, kcols), kcols)], WV.at[own]),
        )

    def g_cols(r):
        h = head_of(r)
        return grad.at[:, pl.ds(pl.multiple_of(h * qcols, qcols), qcols)]

    local = [pltpu.make_async_copy(a, b, local_sem.at[i]) for i, (a, b) in enumerate(w_parts(0))]
    local.append(pltpu.make_async_copy(raw, N.at[tok_rows(0)], local_sem.at[3]))
    local.append(pltpu.make_async_copy(g_cols(0), G.at[tok_rows(0)], local_sem.at[4]))
    local.append(pltpu.make_async_copy(seg, SG.at[tok_slot(0)], local_sem.at[5]))
    local.append(pltpu.make_async_copy(qd, down.at[pl.ds(0, ranks)], local_sem.at[6]))
    local.append(pltpu.make_async_copy(vd, down.at[pl.ds(ranks, ranks)], local_sem.at[7]))
    local.append(pltpu.make_async_copy(qu_in, qu, local_sem.at[8]))
    local.append(pltpu.make_async_copy(vu_in, vu, local_sem.at[9]))
    local.append(pltpu.make_async_copy(gain_in, gain, local_sem.at[10]))
    for copy in local:
        copy.start()
    for i in range(2):
        local[i].wait()
    pl.semaphore_wait(barrier, PLANE - 1 + chain - 1)

    def half_rows(plane, half):
        py = y if half == 0 else 1 - y
        return pl.ds(pl.multiple_of((plane * 4 + py * 2) * rows, 2 * rows), 2 * rows)

    def quarter_rows(plane, quarter):
        px, py, pc = coords(quarter)
        return pl.ds(pl.multiple_of((plane * 4 + py * 2 + pc) * rows, rows), rows)

    def has_up(t):
        return (z < chain - 1) & (z - t >= 0)

    def has_down(t):
        return (z > 0) & (z + t <= chain - 1)

    def from_below(t):
        return z - 1 - t >= 0

    def from_above(t):
        return z + 1 + t <= chain - 1

    def pieces_of(t):
        return range(4) if t == 0 else range(2)

    def piece_rows(plane, t, i):
        return quarter_rows(plane, i) if t == 0 else half_rows(plane, i)

    def half_of(t, i):
        return i // 2 if t == 0 else i

    def plane_rows(plane):
        return pl.ds(pl.multiple_of(plane * 4 * rows, 4 * rows), 4 * rows)

    def up_copy(t, i):
        at = WA.at[piece_rows(z - t, t, i)]
        return remote(at, at, up_send.at[t], up_recv.at[t, half_of(t, i)], above(z + 1))

    def down_copy(t, i):
        at = WA.at[piece_rows(z + t, t, i)]
        return remote(at, at, down_send.at[t], down_recv.at[t, half_of(t, i)], above(z - 1))

    def up_arrival(t, half):
        at = WA.at[half_rows(z - 1 - t, half)]
        return remote(at, at, up_send.at[t], up_recv.at[t, half], above(z - 1))

    def down_arrival(t, half):
        at = WA.at[half_rows(z + 1 + t, half)]
        return remote(at, at, down_send.at[t], down_recv.at[t, half], above(z + 1))

    def vup_copy(t, half):
        at = WV.at[half_rows(z - t, half)]
        return remote(at, at, vup_send.at[t], vup_recv.at[t, half], above(z + 1))

    def vdown_copy(t, half):
        at = WV.at[half_rows(z + t, half)]
        return remote(at, at, vdown_send.at[t], vdown_recv.at[t, half], above(z - 1))

    def vup_arrival(t, half):
        at = WV.at[half_rows(z - 1 - t, half)]
        return remote(at, at, vup_send.at[t], vup_recv.at[t, half], above(z - 1))

    def vdown_arrival(t, half):
        at = WV.at[half_rows(z + 1 + t, half)]
        return remote(at, at, vdown_send.at[t], vdown_recv.at[t, half], above(z + 1))

    def send_chain(t, i):
        @pl.when(has_up(t))
        def _():
            up_copy(t, i).start()

        @pl.when(has_down(t))
        def _():
            down_copy(t, i).start()

    def recv_half(t, half):
        @pl.when(from_below(t))
        def _():
            up_arrival(t, half).wait_recv()

        @pl.when(from_above(t))
        def _():
            down_arrival(t, half).wait_recv()

    def send_value_first(k):
        @pl.when(has_up(k - 1) & jnp.logical_not(has_up(k)))
        def _():
            for half in range(2):
                vup_copy(0, half).start()

        @pl.when(has_down(k - 1) & jnp.logical_not(has_down(k)))
        def _():
            for half in range(2):
                vdown_copy(0, half).start()

    def send_value(t, half):
        @pl.when(has_up(t))
        def _():
            vup_copy(t, half).start()

        @pl.when(has_down(t))
        def _():
            vdown_copy(t, half).start()

    def recv_value(t, half):
        @pl.when(from_below(t))
        def _():
            vup_arrival(t, half).wait_recv()

        @pl.when(from_above(t))
        def _():
            vdown_arrival(t, half).wait_recv()

    w_copies = {}
    for r in (1, 2, 3):
        w_copies[r] = [
            remote(a, b, w_send.at[i // 2], w_recv.at[r if i < 2 else 0], peer(r))
            for i, (a, b) in enumerate(w_parts(r))
        ]
    send_chain(0, 0)
    for r in (1, 2, 3):
        for i in range(2):
            w_copies[r][i].start()
    for r in (1, 2, 3):
        w_copies[r][2].start()

    t_slot = {(1, 0): 0, (4, 3): 1, (4, 0): 2, (5, 0): 3, (3, 0): 4, (7, 0): 5}
    for low in range(4):
        t_slot[2, low] = 6 + low
        t_slot[6, low] = 10

    def send_token(r_mine, r_there, hop, low=0, count=4):
        at = N.at[tok_piece(r_mine, low, count)]
        source = raw.at[pl.ds(low * sub, count * sub)] if r_mine == 0 else at
        remote(source, at, t_send.at[0], t_recv.at[t_slot[r_there, low]], peer(hop)).start()

    def wait_token(r, low=0, count=4):
        at = N.at[tok_piece(r, low, count)]
        remote(at, at, t_send.at[0], t_recv.at[t_slot[r, low]], peer(1)).wait_recv()

    send_token(0, 1, 1)
    send_token(0, 4, 4, 3, 1)
    send_token(0, 4, 4, 0, 3)
    for low in range(4):
        send_token(0, 2, 2, low, 1)
    g_copies = {}
    s_copies = {}
    for r in range(1, PLANE):
        g_copies[r] = remote(g_cols(r), G.at[tok_rows(0)], g_sem.at[0], g_sem.at[1], peer(r))
        s_copies[r] = remote(seg, SG.at[tok_slot(0)], s_sem.at[0], s_sem.at[1], peer(r))

    def wait_weight(r):
        ref = WA.at[w_rows(r)]
        remote(ref, ref, w_send.at[0], w_recv.at[r], peer(r)).wait_recv()

    def wait_values():
        ref = WV.at[pl.ds(0, 3 * rows)]
        remote(ref, ref, w_send.at[1], w_recv.at[0], peer(1)).wait_recv()

    part_rows = 4 * tok

    def part_at(part, i, height):
        py = y if part == 0 else 1 - y
        return pl.ds(pl.multiple_of(py * part_rows + i * height, height), height)

    h = head_of(0)

    def query_up():
        return qu[:, pl.ds(pl.multiple_of(h * qcols, qcols), qcols)]

    def value_up():
        return vu[:, pl.ds(pl.multiple_of(h * kcols, kcols), kcols)]

    def prepare(r):
        height = tok // 2

        @pl.loop(0, 2)
        def _(i):
            begin = tok_slot(r) * tok + i * height
            at = pl.ds(pl.multiple_of(begin, height), height)
            flt = N[at, :].astype(F32)
            meansq = jnp.sum(flt * flt, axis=-1, keepdims=True) / feats
            M[at, :] = (flt * lax.rsqrt(meansq + EPS) * gain[...].astype(F32).reshape(1, feats)).astype(BF16)

        at = tok_rows(r)
        block = M[at, :]
        low = dot(block, down[...], ((1,), (1,))).astype(BF16)
        LL[at, :] = low
        filler = jnp.zeros((ranks, qcols), BF16)
        acc[at, 0:qcols] = ADAPTER_NAME * dot(low, jnp.concatenate([query_up(), filler], axis=0))
        acc[at, qcols:] = jnp.zeros((tok, kcols), F32)
        accv[at, :] = ADAPTER_NAME * dot(low, jnp.concatenate([filler[:, 0:kcols], value_up()], axis=0))

    def add_piece(plane, half, part):
        chosen = half_rows(plane, half)

        @pl.loop(0, part_rows // seq)
        def _(i):
            at = part_at(part, i, seq)
            acc[at, :] = acc[at, :] + dot(M[at, chosen], WA[chosen, :])

    def add_near(part):
        low = jnp.maximum(z - 2, 0)
        high = jnp.minimum(z + 2, chain - 1)
        for count in range(3, min(chain, 5) + 1):
            @pl.when(high - low == count - 1)
            def _():
                chosen = pl.ds(pl.multiple_of(low * 4 * rows, 4 * rows), count * 4 * rows)

                @pl.loop(0, part_rows // seq)
                def _(i):
                    at = part_at(part, i, seq)
                    acc[at, :] = acc[at, :] + dot(M[at, chosen], WA[chosen, :])

    def add_step(t, half, part):
        @pl.when(from_below(t))
        def _():
            add_piece(z - 1 - t, half, part)

        @pl.when(from_above(t))
        def _():
            add_piece(z + 1 + t, half, part)

    def add_value_piece(plane, half):
        chosen = plane_rows(plane) if half is None else half_rows(plane, half)

        @pl.loop(0, 2 * part_rows // seq)
        def _(i):
            at = pl.ds(pl.multiple_of(i * seq, seq), seq)
            accv[at, :] = accv[at, :] + dot(M[at, chosen], WV[chosen, :])

    def add_value(t, half):
        @pl.when(from_below(t))
        def _():
            add_value_piece(z - 1 - t, half)

        @pl.when(from_above(t))
        def _():
            add_value_piece(z + 1 + t, half)

    wait_weight(1)
    send_chain(0, 1)
    for r in range(1, PLANE):
        s_copies[r].start()
    local[3].wait()
    for i in range(6, 11):
        local[i].wait()
    prepare(0)
    wait_token(1)
    prepare(1)
    wait_weight(2)
    send_chain(0, 2)
    wait_weight(3)
    send_chain(0, 3)
    recv_half(0, 0)
    send_chain(1, 0)
    wait_token(2, 0, 1)
    send_token(2, 6, 4, 0, 1)
    recv_half(0, 1)
    send_chain(1, 1)
    local[2].wait()
    wait_values()
    send_value_first(1)
    wait_token(2, 1, 1)
    send_token(2, 6, 4, 1, 1)
    wait_token(4, 3, 1)
    send_token(4, 6, 2, 3, 1)
    wait_token(4, 0, 3)
    send_token(4, 5, 1)
    prepare(4)
    wait_token(2, 2, 1)
    send_token(2, 6, 4, 2, 1)
    for r in (6, 7, 4, 5, 2, 3, 1):
        g_copies[r].start()
    wait_token(5)
    prepare(5)
    recv_half(1, 0)
    send_chain(2, 0)
    wait_token(2, 3, 1)
    send_token(2, 3, 1)
    prepare(2)
    wait_token(3)
    prepare(3)
    recv_half(1, 1)
    send_chain(2, 1)
    for k in range(2, chain):
        send_value_first(k)
    add_near(0)
    wait_token(6)
    send_token(6, 7, 1)
    prepare(6)
    wait_token(7)
    prepare(7)

    @pl.when(middle)
    def _():
        for half in range(2):
            recv_value(0, half)
            send_value(1, half)

    add_near(1)
    add_value_piece(z, None)
    for t in range(2, chain - 1):
        for half in range(2):
            recv_half(t, half)
            if t + 1 < chain - 1:
                send_chain(t + 1, half)
            for part in range(2):
                add_step(t, half, part)

    tiles = PLANE * tok // seq
    local[4].wait()
    local[5].wait()
    g_others = G.at[pl.ds(0, (PLANE - 1) * tok)]
    g_all_copies = remote(g_others, g_others, g_sem.at[0], g_sem.at[1], peer(1))
    g_all_copies.wait_recv()
    s_others = SG.at[pl.ds(0, PLANE - 1)]
    s_all_copies = remote(s_others, s_others, s_sem.at[0], s_sem.at[1], peer(1))
    s_all_copies.wait_recv()

    pos_i = lax.broadcasted_iota(jnp.int32, (seq, seq), 0)
    pos_j = lax.broadcasted_iota(jnp.int32, (seq, seq), 1)
    band = (pos_j <= pos_i) & (pos_j > pos_i - 2 * tok)

    @pl.loop(0, tiles, unroll=2)
    def _(i):
        at = pl.ds(pl.multiple_of(i * seq, seq), seq)
        q_all = acc[at, 0:qcols].astype(BF16)
        k = acc[at, qcols:].astype(BF16)
        K[at, :] = k
        g_all = G[at, :]
        traces = [SG[2 * i].astype(F32), SG[2 * i + 1].astype(F32)]
        along = jnp.concatenate(traces, axis=1)
        turned = [jnp.broadcast_to(own, (tok, tok)).T for own in traces]
        across = jnp.concatenate([jnp.concatenate([own, own], axis=1) for own in turned], axis=0)
        mask = band & (across == along)
        dv = jnp.zeros((seq, kcols), F32)
        for n in range(heads):
            q = q_all[:, n * kcols:(n + 1) * kcols]
            g = g_all[:, n * kcols:(n + 1) * kcols]
            t = jnp.tanh(dot(q, k, ((1,), (1,))) * (QSCALE / CAP))
            expo = jnp.where(mask, jnp.exp(CAP * t), 0.0)
            weights = expo * (1.0 / jnp.sum(expo, axis=-1, keepdims=True))
            weights16 = weights.astype(BF16)
            P[i * heads + n] = weights16
            C[i * heads + n] = weights * (1.0 - t * t)
            dv = dv + dot(weights16, g, ((0,), (0,)))
        DV[at, :] = dv.astype(BF16)

    @pl.when(middle)
    def _():
        for t in range(1, chain - 1):
            for half in range(2):
                recv_value(t, half)
                if t + 1 < chain - 1:
                    send_value(t + 1, half)

    half_tokens = PLANE * tok // 2

    def token_half(half):
        return pl.ds(half * half_tokens, half_tokens)

    def send_pull(half, up, change, gathered, send, recv):
        own = gathered.at[half, h]
        own[...] = dot(up, change[token_half(half), :], ((1,), (1,))).astype(BF16)
        for r in (7, 6, 5, 4, 3, 2, 1):
            remote(own, own, send.at[half], recv.at[half], peer(r)).start()

    def pulls(half, gathered, send, recv):
        at = gathered.at[half, pl.ds(0, PLANE - 1)]
        return remote(at, at, send.at[half], recv.at[half], peer(1))

    def down_gradient(columns, width, gathered, send, recv):
        total = jnp.zeros((ranks, width), F32)
        for half in range(2):
            pulls(half, gathered, send, recv).wait_recv()
            pull = gathered[half, 0].astype(F32)
            for r in range(1, PLANE):
                pull = pull + gathered[half, r].astype(F32)
            total = total + dot(pull.astype(BF16), M[token_half(half), columns])
        return total.astype(BF16)

    def share(sums, sem):
        own = sums.at[z]
        turn = jnp.where(2 * z < chain, chain - 1, 1)
        for d in range(1, chain):
            remote(own, own, sem.at[0], sem.at[1], above((z + turn * d) % chain)).start()

    def shares(sums, sem):
        at = sums.at[pl.ds(0, chain - 1)]
        return remote(at, at, sem.at[0], sem.at[1], peer(1))

    def shared(sums):
        total = sums[0].astype(F32)
        for d in range(1, chain):
            total = total + sums[d].astype(F32)
        return (total * coefficient).astype(BF16)

    def spread(total, mine, out, sem):
        mine[...] = total
        for r in (7, 6, 5, 4, 3, 2, 1):
            remote(mine, out.at[h], sem.at[2], sem.at[3], peer(r)).start()
        out[h] = total

    def spreads(out, sem):
        at = out.at[pl.ds(0, PLANE - 1)]
        return remote(at, at, sem.at[2], sem.at[3], peer(1))

    for half in range(2):
        send_pull(half, value_up(), DV, PV, v1_send, v1_recv)
    low_gradient = dot(LL[...], DV[...], ((0,), (0,)))
    RSV.at[z][:, piece:piece + kcols] = low_gradient[ranks:, :].astype(BF16)
    for t in range(chain - 2):
        @pl.when(outer)
        def _():
            for half in range(2):
                recv_value(t, half)

        add_value(t, None)
    own_columns = pl.ds(pl.multiple_of(h * piece, piece), piece)
    RSV.at[z][:, 0:piece] = down_gradient(own_columns, piece, PV, v1_send, v1_recv)
    for half in range(2):
        @pl.when(outer)
        def _():
            recv_value(chain - 2, half)

        add_value(chain - 2, half)

    for half in range(2):
        for i in range(half * tiles // 2, (half + 1) * tiles // 2):
            at = pl.ds(i * seq, seq)
            v = accv[at, :].astype(BF16)
            k = K[at, :]
            for n in range(heads):
                g = G[at, n * kcols:(n + 1) * kcols]
                dweight = dot(g, v, ((1,), (1,)))
                delta = jnp.sum(P[i * heads + n].astype(F32) * dweight, axis=-1, keepdims=True)
                dscore = (C[i * heads + n] * (dweight - delta)).astype(BF16)
                DQ[at, n * kcols:(n + 1) * kcols] = (dot(dscore, k) * QSCALE).astype(BF16)
        send_pull(half, query_up(), DQ, PQ, q1_send, q1_recv)

    low_gradient = dot(LL[...], DQ[...], ((0,), (0,)))
    RSV.at[z][:, piece + kcols:] = low_gradient[0:ranks, :].astype(BF16)
    share(RSV, v_sem)
    width = feats // 2
    core_columns = pl.ds(pl.multiple_of(c * width, width), width)
    RSA[z] = down_gradient(core_columns, width, PQ, q1_send, q1_recv)
    share(RSA, a_sem)
    shares(RSV, v_sem).wait_recv()
    spread(shared(RSV), TV, OUTV, v_sem)
    shares(RSA, a_sem).wait_recv()
    TA[...] = shared(RSA)
    core_copy = remote(TA, OUTA.at[c], a_sem.at[2], a_sem.at[3], peer(1))
    core_copy.start()
    OUTA[c] = TA[...]
    spreads(OUTV, v_sem).wait_recv()
    at = OUTA.at[1 - c]
    remote(at, at, a_sem.at[2], a_sem.at[3], peer(1)).wait_recv()

    at = WA.at[pl.ds(0, 3 * rows)]
    remote(at, at, w_send.at[0], w_recv.at[1], peer(1)).wait_send()
    at = WV.at[pl.ds(0, 3 * rows)]
    remote(at, at, w_send.at[1], w_recv.at[0], peer(1)).wait_send()
    at = N.at[pl.ds(0, (PLANE - 1) * tok)]
    remote(at, at, t_send.at[0], t_recv.at[0], peer(1)).wait_send()
    g_all_copies.wait_send()
    s_all_copies.wait_send()
    for t in range(chain - 1):
        @pl.when(has_up(t))
        def _():
            at = WA.at[plane_rows(z - t)]
            remote(at, at, up_send.at[t], up_recv.at[t, 0], above(z + 1)).wait_send()
            at = WV.at[plane_rows(z - t)]
            remote(at, at, vup_send.at[t], vup_recv.at[t, 0], above(z + 1)).wait_send()

        @pl.when(has_down(t))
        def _():
            at = WA.at[plane_rows(z + t)]
            remote(at, at, down_send.at[t], down_recv.at[t, 0], above(z - 1)).wait_send()
            at = WV.at[plane_rows(z + t)]
            remote(at, at, vdown_send.at[t], vdown_recv.at[t, 0], above(z - 1)).wait_send()
    for half in range(2):
        pulls(half, PV, v1_send, v1_recv).wait_send()
        pulls(half, PQ, q1_send, q1_recv).wait_send()
    for sums, sem in ((RSV, v_sem), (RSA, a_sem)):
        shares(sums, sem).wait_send()
    spreads(OUTV, v_sem).wait_send()
    core_copy.wait_send()


def unpack_kernel(outa, outv, out_aq, out_bq, out_av, out_bv):
    feats = out_aq.shape[1]
    piece = feats // PLANE
    qcols = out_bq.shape[1] // PLANE
    kcols = out_bv.shape[1] // PLANE
    for core in range(2):
        out_aq[:, core * feats // 2:(core + 1) * feats // 2] = outa[core].astype(F32)
    for h in range(PLANE):
        value = outv[h].astype(F32)
        out_bq[:, h * qcols:(h + 1) * qcols] = value[:, piece + kcols:]
        out_av[:, h * piece:(h + 1) * piece] = value[:, 0:piece]
        out_bv[:, h * kcols:(h + 1) * kcols] = value[:, piece:piece + kcols]


def on_plane(
    tokens,
    trace_index,
    input_norm_scale,
    query_weight,
    key_weight,
    value_weight,
    query_down_weight,
    query_up_weight,
    value_down_weight,
    value_up_weight,
    output_gradient,
):
    tok = tokens.shape[1]
    feats = tokens.shape[2]
    fsdp = lax.axis_size("fsdp")
    chain = fsdp // 4
    ranks = query_down_weight.shape[1]
    qcols = query_weight.shape[1] // PLANE
    kcols = key_weight.shape[1] // PLANE
    piece = feats // PLANE
    many = PLANE * tok
    token_total = lax.axis_size("ctx") * fsdp * tok
    coefficient = ADAPTER_NAME / math.sqrt(token_total)
    hbm = pl.BlockSpec(memory_space=pltpu.HBM)
    vmem = pl.BlockSpec(memory_space=pltpu.VMEM)
    dma = pltpu.SemaphoreType.DMA
    steps = chain - 1
    tiles = many // (2 * tok)
    heads = qcols // kcols
    outa, outv = pl.pallas_call(
        functools.partial(plane_kernel, chain, coefficient),
        out_shape=(
            pltpu.VMEM((2, ranks, feats // 2), BF16),
            pltpu.VMEM((PLANE, ranks, piece + kcols + qcols), BF16),
        ),
        in_specs=[hbm] * 11,
        out_specs=(vmem, vmem),
        scratch_shapes=[
            pltpu.VMEM((many, feats), BF16),
            pltpu.VMEM((many, feats), BF16),
            pltpu.VMEM((feats, qcols + kcols), BF16),
            pltpu.VMEM((feats, kcols), BF16),
            pltpu.VMEM((many, qcols), BF16),
            pltpu.VMEM((PLANE, 1, tok), jnp.int32),
            pltpu.VMEM((many, qcols + kcols), F32),
            pltpu.VMEM((many, kcols), F32),
            pltpu.VMEM((tiles * heads, 2 * tok, 2 * tok), BF16),
            pltpu.VMEM((tiles * heads, 2 * tok, 2 * tok), F32),
            pltpu.VMEM((many, kcols), BF16),
            pltpu.VMEM((many, qcols), BF16),
            pltpu.VMEM((many, kcols), BF16),
            pltpu.VMEM((many, 2 * ranks), BF16),
            pltpu.VMEM((feats,), BF16),
            pltpu.VMEM((2 * ranks, feats), BF16),
            pltpu.VMEM((ranks, query_weight.shape[1]), BF16),
            pltpu.VMEM((ranks, value_weight.shape[1]), BF16),
            pltpu.VMEM((2, PLANE, ranks, many // 2), BF16),
            pltpu.VMEM((2, PLANE, ranks, many // 2), BF16),
            pltpu.VMEM((chain, ranks, feats // 2), BF16),
            pltpu.VMEM((chain, ranks, piece + kcols + qcols), BF16),
            pltpu.VMEM((ranks, feats // 2), BF16),
            pltpu.VMEM((ranks, piece + kcols + qcols), BF16),
            dma((11,)),
            dma((2,)), dma((4,)), dma((1,)), dma((11,)), dma((2,)), dma((2,)),
            dma((steps,)), dma((steps, 2)), dma((steps,)), dma((steps, 2)),
            dma((steps,)), dma((steps, 2)), dma((steps,)), dma((steps, 2)),
            dma((2,)), dma((2,)), dma((2,)), dma((2,)), dma((4,)), dma((4,)),
        ],
        compiler_params=pltpu.CompilerParams(
            collective_id=0, has_side_effects=True, vmem_limit_bytes=56 * 1024 * 1024
        ),
    )(
        tokens.reshape(tok, feats), trace_index, input_norm_scale,
        query_weight, key_weight, value_weight,
        query_down_weight.T, query_up_weight, value_down_weight.T, value_up_weight,
        output_gradient.reshape(tok, output_gradient.shape[2]),
    )
    aq, bq, av, bv = pl.pallas_call(
        unpack_kernel,
        out_shape=(
            jax.ShapeDtypeStruct((ranks, feats), F32),
            jax.ShapeDtypeStruct((ranks, query_weight.shape[1]), F32),
            jax.ShapeDtypeStruct((ranks, feats), F32),
            jax.ShapeDtypeStruct((ranks, value_weight.shape[1]), F32),
        ),
        in_specs=[vmem, vmem],
        out_specs=(vmem, vmem, vmem, vmem),
        compiler_params=pltpu.CompilerParams(vmem_limit_bytes=16 * 1024 * 1024),
    )(outa, outv)
    return (aq.T, bq, av.T, bv)


def solution(mesh):
    shape = mesh.shape
    planes = shape["groups"] == 1 and shape["ctx"] == 2 and shape["fsdp"] % 4 == 0 and shape["fsdp"] > 8
    return jax.shard_map(
        on_plane if planes else on_device,
        mesh=mesh,
        in_specs=(
            P(("groups", "fsdp"), "ctx", None),
            P(("groups", "fsdp"), "ctx"),
            P(),
            P("fsdp", None),
            P("fsdp", None),
            P("fsdp", None),
            P(),
            P(),
            P(),
            P(),
            P(("groups", "fsdp"), "ctx", None),
        ),
        out_specs=(P("groups", None), P("groups", None), P("groups", None), P("groups", None)),
        check_vma=False,
    )
```
